32 devices in a mesh: dp: 8 (over y, x, core), tensor: 4 (over z).
Axes of the slice: x: 2, y: 2, z: 4, core: 2. Of those that a mesh axis runs over, the one named last changes fastest.
Arguments:
- inputs: bfloat16 [8192, 2048], P(('dp', 'tensor')), may hold values from -6 to 6
- cotangent: bfloat16 [8192, 2048], P(('dp', 'tensor')), may hold values from -6 to 6
- attn_gain: bfloat16 [2048], P('dp'), may hold values from 0.5 to 1.5
- w_query: bfloat16 [2048, 2048], P('dp', 'tensor'), may hold values from -0.1875 to 0.1875
- w_key: bfloat16 [2048, 512], P('dp', 'tensor'), may hold values from -0.1875 to 0.1875
- w_value: bfloat16 [2048, 512], P('dp', 'tensor'), may hold values from -0.125 to 0.125
- w_out: bfloat16 [2048, 2048], P(('tensor', 'dp')), may hold values from -1 to 1
- mlp_gain: bfloat16 [2048], P('dp'), may hold values from 0.5 to 1.5
- w_gate: bfloat16 [2048, 8192], P('dp', 'tensor'), may hold values from -0.125 to 0.125
- w_up: bfloat16 [2048, 8192], P('dp', 'tensor'), may hold values from -0.125 to 0.125
- w_down: bfloat16 [8192, 2048], P(('tensor', 'dp')), may hold values from -0.125 to 0.125
- seq_lengths: int32 [12], replicated, may hold values from 256 to 1024, as said below
- group_perm: int32 [12], replicated, may hold values from 0 to 11, as said below
- group_starts: int32 [9], replicated, may hold values from 0 to 12, as said below
Outputs:
- outputs: bfloat16 [8192, 2048], P(('dp', 'tensor'))
- input_grad: bfloat16 [8192, 2048], P(('dp', 'tensor'))
- attn_gain_grad: float32 [2048], P('dp')
- w_query_grad: float32 [2048, 2048], P('dp', 'tensor')
- w_key_grad: float32 [2048, 512], P('dp', 'tensor')
- w_value_grad: float32 [2048, 512], P('dp', 'tensor')
- w_out_grad: float32 [2048, 2048], P(('tensor', 'dp'))
- mlp_gain_grad: float32 [2048], P('dp')
- w_gate_grad: float32 [2048, 8192], P('dp', 'tensor')
- w_up_grad: float32 [2048, 8192], P('dp', 'tensor')
- w_down_grad: float32 [8192, 2048], P(('tensor', 'dp'))
The draws below stay inside these ranges and needn't reach their ends.
Inputs may be any that keep to these rules, and one draw needn't show every extreme that they name: `seq_lengths`: every length is a multiple of 128; the sequences of one group take at most 1024 rows together, and some sequence fills a group alone. `group_perm`: each sequence number appears once. `group_starts`: starts at 0, ends at 12, and rises by one or two from group to group: a group holds 1 to 2 sequences.
All inputs are finite; a program needn't handle non-finite values.
Results may differ from the reference program's by a relative error of at most 0.025.
Values may be sent and summed in bfloat16 or wider, within the bound.
A program may use at most 256 MiB of HBM per device.

```python
import math
import jax
import jax.numpy as jnp
from jax import lax

D = 2048
HEADS = 32
KV_HEADS = 8
HEAD_SIZE = 64
HIDDEN_SIZE = 8192
TILE = 128
MOST_SEQS = 2
GROUP_ROWS = 1024
ROWS = 8192
SEQS = 12
N_DP = 8


def deal(key):
    pattern = jnp.tile(jnp.array([1, 1, 2, 2], dtype=jnp.int32), N_DP // 4)
    counts = jax.random.permutation(jax.random.fold_in(key, 11), pattern).astype(jnp.int32)
    starts = jnp.concatenate([jnp.zeros((1,), jnp.int32), jnp.cumsum(counts).astype(jnp.int32)])
    unit_count = GROUP_ROWS // TILE
    places = jnp.arange(SEQS, dtype=jnp.int32)
    owners = jnp.sum((starts[None, 1:] <= places[:, None]).astype(jnp.int32), axis=1)
    upper_units = unit_count // counts[owners]
    raw_draw = jax.random.randint(jax.random.fold_in(key, 12), (SEQS,), 0, 1 << 20).astype(jnp.int32)
    pieces = 2 + raw_draw % (upper_units - 1)
    first_single = jnp.argmax(counts == 1).astype(jnp.int32)
    forced = starts[first_single]
    pieces = jnp.where(places == forced, unit_count, pieces).astype(jnp.int32)
    dealing = jax.random.permutation(jax.random.fold_in(key, 13), SEQS).astype(jnp.int32)
    lengths = jnp.zeros((SEQS,), jnp.int32).at[dealing].set(pieces * TILE)
    return (lengths, dealing, starts)


def draw_seq_lengths(key, part):
    return deal(key)[0]


def draw_group_perm(key, part):
    return deal(key)[1]


def draw_group_starts(key, part):
    return deal(key)[2]


def strengthened(values, stream_key, source, target, parts, factor):
    owner, partner = [(jnp.arange(values.shape[position]) // (values.shape[position] // parts)).reshape([-1 if axis == position else 1 for axis in range(values.ndim)]) for position in (source, target)]
    chosen = jax.random.permutation(stream_key, parts)[partner]
    strong = (owner == chosen) | (owner == (partner + parts // 2) % parts)
    return jnp.where(strong, factor * values, values)


def shard_levels(stream_key, extent, cuts, least, largest):
    level = 1.0
    for position, parts in cuts:
        draws = jax.random.uniform(jax.random.fold_in(jax.random.fold_in(stream_key, 6), position), (parts,), jnp.float32, least / len(cuts), largest / len(cuts))
        level = level * jnp.repeat(jnp.exp(draws), extent[position] // parts).reshape((-1,) + (1,) * (len(extent) - 1 - position))
    return level


def centred(stream_key, dims, width, reach, cuts=(), kind=jnp.bfloat16):
    gain = shard_levels(stream_key, dims, cuts, -0.22, 0.18) if cuts else 1.0
    values = jax.random.normal(stream_key, dims, jnp.float32) * width * gain
    return jnp.minimum(jnp.maximum(values, -reach), reach).astype(kind)


def noise_with(rng, shape, spread, most, cuts, heavy, held_as=jnp.bfloat16):
    entries = spread * jax.random.normal(rng, shape, jnp.float32)
    if cuts:
        entries = entries * shard_levels(rng, shape, cuts, -0.22, 0.18)
    return jnp.clip(strengthened(entries, jax.random.fold_in(rng, 3), *heavy), -most, most).astype(held_as)


def setup_inputs(seed: int = 0) -> dict:
    key_list = jax.random.split(jax.random.key(seed), 15)
    return {
        "inputs": centred(key_list[0], (ROWS, D), 1.0, 6.0, ((0, 32),)),
        "cotangent": noise_with(key_list[1], (ROWS, D), 1.0, 6.0, ((0, 32),), (0, 1, 32, 2.75)),
        "attn_gain": jnp.clip(1.0 + 0.1 * jax.random.normal(key_list[2], (D,), jnp.float32), 0.5, 1.5).astype(jnp.bfloat16),
        "w_query": centred(key_list[3], (D, HEADS * HEAD_SIZE), (D // 2) ** -0.5, 0.1875, ((0, 8), (1, 4))),
        "w_key": centred(key_list[4], (D, KV_HEADS * HEAD_SIZE), (D // 2) ** -0.5, 0.1875, ((0, 8), (1, 4))),
        "w_value": centred(key_list[5], (D, KV_HEADS * HEAD_SIZE), D ** -0.5, 0.125, ((0, 8), (1, 4))),
        "w_out": centred(key_list[6], (HEADS * HEAD_SIZE, D), (HEADS * HEAD_SIZE // 64) ** -0.5, 1.0, ((0, 32),)),
        "mlp_gain": jnp.clip(1.0 + 0.1 * jax.random.normal(key_list[7], (D,), jnp.float32), 0.5, 1.5).astype(jnp.bfloat16),
        "w_gate": centred(key_list[8], (D, HIDDEN_SIZE), D ** -0.5, 0.125, ((0, 8), (1, 4))),
        "w_up": centred(key_list[9], (D, HIDDEN_SIZE), D ** -0.5, 0.125, ((0, 8), (1, 4))),
        "w_down": centred(key_list[10], (HIDDEN_SIZE, D), (HIDDEN_SIZE // 4) ** -0.5, 0.125, ((0, 32),)),
        "seq_lengths": draw_seq_lengths(jax.random.fold_in(key_list[14], 71), 0),
        "group_perm": draw_group_perm(jax.random.fold_in(key_list[14], 71), 0),
        "group_starts": draw_group_starts(jax.random.fold_in(key_list[14], 71), 0),
    }


norm_epsilon = 1e-05
rope_theta = 500000.0
rope_factor = 32.0
low_factor = 1.0
high_factor = 4.0
context_span = 8192.0
mask_fill = -1e+30

@jax.custom_vjp
def low(v):
    return lax.optimization_barrier(v.astype(jnp.bfloat16)).astype(jnp.float32)

@jax.custom_vjp
def low_back(v):
    return v

def low_keep(v):
    return (low(v), None)

def low_pass(kept, grad):
    return (grad,)

def back_keep(v):
    return (v, None)

def back_low(kept, grad):
    return (low(grad),)
low.defvjp(low_keep, low_pass)
low_back.defvjp(back_keep, back_low)

def rotary_freqs(head_size):
    exponents = jnp.arange(0, head_size, 2).astype(jnp.float32) / head_size
    inverse = 1.0 / jnp.power(jnp.float32(rope_theta), exponents)
    wavelength = 2.0 * math.pi / inverse
    smooth = (context_span / wavelength - low_factor) / (high_factor - low_factor)
    blended = (1.0 - smooth) * inverse / rope_factor + smooth * inverse
    scaled = jnp.where(wavelength > context_span / low_factor, inverse / rope_factor, blended)
    return jnp.where(wavelength < context_span / high_factor, inverse, scaled)

def rotary_tables(positions, head_size):
    angles = positions.astype(jnp.float32)[:, None] * rotary_freqs(head_size)[None, :]
    angles = jnp.concatenate([angles, angles], axis=1)
    return (jnp.cos(angles)[:, None, :], jnp.sin(angles)[:, None, :])

def rotary(vectors, cosine, sine_table):
    half_size = vectors.shape[-1] // 2
    turned = jnp.concatenate([-vectors[..., half_size:], vectors[..., :half_size]], axis=-1)
    return vectors * cosine + turned * sine_table

def group_layout(seq_lengths, group_perm, group_starts, group_id, row_total, slot_total):
    bounds = jnp.arange(group_starts.shape[0], dtype=jnp.int32)
    numbers = jnp.arange(group_perm.shape[0], dtype=jnp.int32)
    opening = jnp.sum(jnp.where(bounds == group_id, group_starts, 0)).astype(jnp.int32)
    closing = jnp.sum(jnp.where(bounds == group_id + 1, group_starts, 0)).astype(jnp.int32)
    row_ids = jnp.arange(row_total, dtype=jnp.int32)
    segment = jnp.zeros((row_total,), jnp.int32)
    offset = jnp.zeros((row_total,), jnp.int32)
    finish = jnp.zeros((), jnp.int32)
    for slot_id in range(slot_total):
        slot_place = opening + slot_id
        sequence = jnp.sum(jnp.where(numbers == slot_place, group_perm, 0)).astype(jnp.int32)
        length = jnp.sum(jnp.where(numbers == sequence, seq_lengths, 0)).astype(jnp.int32)
        length = jnp.where(slot_place < closing, length, 0).astype(jnp.int32)
        finish = finish + length
        passed = row_ids >= finish
        segment = segment + passed.astype(jnp.int32)
        offset = jnp.where(passed, finish, offset).astype(jnp.int32)
    return (segment, row_ids - offset)

def gain_norm(vectors, scales):
    return vectors * lax.rsqrt(lax.optimization_barrier(jnp.mean(vectors * vectors, axis=-1, keepdims=True)) + norm_epsilon) * scales

def product(left, right):
    return jnp.dot(left, right, precision=lax.Precision.HIGHEST, preferred_element_type=jnp.float32)

def group_forward(hidden, segment, positions, params):
    attn_gain, w_query, w_key, w_value, w_out, mlp_gain, w_gate, w_up, w_down = params
    row_count = hidden.shape[0]
    normed = low(gain_norm(hidden, attn_gain))
    cosine, sine_table = rotary_tables(positions, HEAD_SIZE)
    queries = low_back(product(normed, w_query)).reshape(row_count, HEADS, HEAD_SIZE)
    queries = low(rotary(queries, cosine, sine_table))
    queries = queries.reshape(row_count, KV_HEADS, HEADS // KV_HEADS, HEAD_SIZE)
    key_rows = low_back(product(normed, w_key)).reshape(row_count, KV_HEADS, HEAD_SIZE)
    key_rows = low(rotary(key_rows, cosine, sine_table))
    value_rows = low(low_back(product(normed, w_value))).reshape(row_count, KV_HEADS, HEAD_SIZE)
    scores = jnp.einsum('qcgd,kcd->cgqk', queries, key_rows, precision=lax.Precision.HIGHEST)
    scores = low_back(scores * HEAD_SIZE ** (-0.5))
    row_ids = jnp.arange(row_count, dtype=jnp.int32)
    allowed = (segment[:, None] == segment[None, :]) & (row_ids[None, :] <= row_ids[:, None])
    scores = jnp.where(allowed, scores, mask_fill)
    row_top = lax.optimization_barrier(jnp.max(scores, axis=-1, keepdims=True))
    weights = jnp.exp(scores - row_top)
    chances = weights / lax.optimization_barrier(jnp.sum(weights, axis=-1, keepdims=True))
    mixed_heads = jnp.einsum('cgqk,kcd->qcgd', low(chances), value_rows, precision=lax.Precision.HIGHEST)
    mixed_heads = low(low_back(mixed_heads.reshape(row_count, HEADS * HEAD_SIZE)))
    middle = hidden + low_back(product(mixed_heads, w_out))
    normed_two = low(gain_norm(middle, mlp_gain))
    gate_pre = low_back(product(normed_two, w_gate))
    up_pre = low_back(product(normed_two, w_up))
    active = low(jax.nn.silu(gate_pre) * up_pre)
    return middle + product(active, w_down)

def reference(inputs, cotangent, attn_gain, w_query, w_key, w_value, w_out, mlp_gain, w_gate, w_up, w_down, seq_lengths, group_perm, group_starts):
    params = tuple((weight.astype(jnp.float32) for weight in (attn_gain, w_query, w_key, w_value, w_out, mlp_gain, w_gate, w_up, w_down)))
    hidden = inputs.astype(jnp.float32).reshape(N_DP, GROUP_ROWS, D)
    groups = jnp.arange(N_DP, dtype=jnp.int32)
    checked = jax.checkpoint(group_forward)

    def forward(hidden_all, params_all):

        def one_group(carry, group_item):
            block_rows, group_id = group_item
            segment, positions = group_layout(seq_lengths, group_perm, group_starts, group_id, GROUP_ROWS, MOST_SEQS)
            return (carry, checked(block_rows, segment, positions, params_all))
        unused, result = lax.scan(one_group, 0, (hidden_all, groups))
        return result
    result, backward = jax.vjp(forward, hidden, params)
    input_grad, weight_grads = backward(cotangent.astype(jnp.float32).reshape(N_DP, GROUP_ROWS, D))
    return (result.reshape(ROWS, D).astype(jnp.bfloat16), input_grad.reshape(ROWS, D).astype(jnp.bfloat16), weight_grads[0], weight_grads[1], weight_grads[2], weight_grads[3], weight_grads[4], weight_grads[5], weight_grads[6], weight_grads[7], weight_grads[8])
```

```python
import functools
import math

import jax
import jax.numpy as jnp
from jax import lax
from jax.experimental import pallas as pl
from jax.experimental.pallas import tpu as pltpu
from jax.sharding import PartitionSpec as P

HEAD_SIZE = 64
MOST_SEQS = 2
SLAB = 128
SPAN = 256

norm_epsilon = 1e-05
rope_theta = 500000.0
rope_factor = 32.0
low_factor = 1.0
high_factor = 4.0
context_span = 8192.0
mask_fill = -1e30

F32 = jnp.float32
BF16 = jnp.bfloat16
VMEM_LIMIT = 60 * 1024 * 1024


def rotary_freqs(head_size):
    exponents = jnp.arange(0, head_size, 2).astype(jnp.float32) / head_size
    inverse = 1.0 / jnp.power(jnp.float32(rope_theta), exponents)
    wavelength = 2.0 * math.pi / inverse
    smooth = (context_span / wavelength - low_factor) / (high_factor - low_factor)
    blended = (1.0 - smooth) * inverse / rope_factor + smooth * inverse
    scaled = jnp.where(wavelength > context_span / low_factor, inverse / rope_factor, blended)
    return jnp.where(wavelength < context_span / high_factor, inverse, scaled)


def slab_tables(positions):
    freqs = rotary_freqs(HEAD_SIZE)
    freqs = jnp.concatenate([freqs] * 4)
    angles = positions.astype(jnp.float32)[:, None] * freqs[None, :]
    low_half = (jnp.arange(SLAB) % HEAD_SIZE) < HEAD_SIZE // 2
    sines = jnp.sin(angles)
    return jnp.cos(angles), jnp.where(low_half[None, :], -sines, sines)


def group_layout(seq_lengths, group_perm, group_starts, group_id, row_total, slot_total):
    bounds = jnp.arange(group_starts.shape[0], dtype=jnp.int32)
    numbers = jnp.arange(group_perm.shape[0], dtype=jnp.int32)
    opening = jnp.sum(jnp.where(bounds == group_id, group_starts, 0))
    closing = jnp.sum(jnp.where(bounds == group_id + 1, group_starts, 0))
    row_ids = jnp.arange(row_total, dtype=jnp.int32)
    offset = jnp.zeros((row_total,), jnp.int32)
    finish = jnp.zeros((), jnp.int32)
    for slot_id in range(slot_total):
        slot_place = opening + slot_id
        sequence = jnp.sum(jnp.where(numbers == slot_place, group_perm, 0))
        length = jnp.sum(jnp.where(numbers == sequence, seq_lengths, 0))
        length = jnp.where(slot_place < closing, length, 0)
        finish = finish + length
        offset = jnp.where(row_ids >= finish, finish, offset)
    return offset, row_ids - offset


def project(left, right):
    return jnp.dot(left, right, preferred_element_type=F32)


def project_back(left, right):
    return lax.dot_general(left, right, (((1,), (1,)), ((), ())), preferred_element_type=F32)


def row_contract(left, right):
    return lax.dot_general(left, right, (((0,), (0,)), ((), ())), preferred_element_type=F32)


def lanes(shape):
    return lax.broadcasted_iota(jnp.int32, shape, len(shape) - 1)


def turned(slab):
    half = HEAD_SIZE // 2
    ahead = pltpu.roll(slab, SLAB - half, 1)
    behind = pltpu.roll(slab, half, 1)
    return jnp.where(lanes(slab.shape) % HEAD_SIZE < half, ahead, behind)


def head_pair(slab):
    left = lanes(slab.shape) < HEAD_SIZE
    zero = jnp.zeros_like(slab)
    return jnp.concatenate([jnp.where(left, slab, zero), jnp.where(left, zero, slab)], axis=0)


def join_pair(stacked):
    half = stacked.shape[0] // 2
    left = lanes((half, SLAB)) < HEAD_SIZE
    return jnp.where(left, stacked[:half], stacked[half:])


def params(**kwargs):
    return pltpu.CompilerParams(vmem_limit_bytes=VMEM_LIMIT, **kwargs)


def vmem_specs(count):
    return [pl.BlockSpec(memory_space=pltpu.VMEM)] * count


def attend_kernel(
    x_ref, w_ref, gain_ref, cos_ref, sin_ref, start_ref,
    normed_ref, q_ref, k_ref, v_ref, mixed_ref, lse_ref, bias_ref, stat_ref,
):
    rows_all = x_ref.shape[0]
    q_width = q_ref.shape[1]
    kv_slabs = v_ref.shape[0] // 2
    slabs = q_width // SLAB
    scale = HEAD_SIZE ** (-0.5)

    @pl.loop(0, rows_all // SPAN)
    def _(step):
        rows = pl.ds(step * SPAN, SPAN)
        x = x_ref[rows, :].astype(F32)
        inverse = lax.rsqrt(jnp.mean(x * x, axis=-1, keepdims=True) + norm_epsilon)
        normed = (x * inverse * gain_ref[...]).astype(BF16)
        normed_ref[rows, :] = normed
        pre = project(normed, w_ref[:, : q_width + 2 * kv_slabs * SLAB])
        cosine, sine = cos_ref[rows, :], sin_ref[rows, :]
        for slab in range(slabs):
            part = pre[:, slab * SLAB : (slab + 1) * SLAB]
            part = (part * cosine + turned(part) * sine).astype(BF16)
            q_ref[rows, slab * SLAB : (slab + 1) * SLAB] = (part.astype(F32) * scale).astype(BF16)
        left = lanes((SPAN, SLAB)) < HEAD_SIZE
        for pair in range(kv_slabs):
            at = q_width + pair * SLAB
            key = pre[:, at : at + SLAB]
            key = key * cosine + turned(key) * sine
            at = at + kv_slabs * SLAB
            value = pre[:, at : at + SLAB]
            for ref, full in ((k_ref, key), (v_ref, value)):
                other = pltpu.roll(full, HEAD_SIZE, 1)
                ref[2 * pair, rows, :] = jnp.where(left, full, other).astype(BF16)
                ref[2 * pair + 1, rows, :] = jnp.where(left, other, full).astype(BF16)

    members = slabs // (2 * kv_slabs)
    for tile in range(rows_all // SPAN):
        first, span = tile * SPAN, (tile + 1) * SPAN
        columns = lanes((SPAN, span))
        row_ids = first + lax.broadcasted_iota(jnp.int32, (SPAN, span), 0)
        allowed = (columns >= start_ref[first : first + SPAN, :]) & (columns <= row_ids)
        bias_ref[:, :span] = jnp.where(allowed, 0.0, mask_fill)

        @pl.loop(0, slabs)
        def _(slab):
            at = pl.ds(pl.multiple_of(slab * SLAB, SLAB), SLAB)
            head = slab // members
            stacked = head_pair(q_ref[first : first + SPAN, at])
            scores = project_back(stacked, k_ref[head, :span, :])
            bias = bias_ref[:, :span]
            scores = scores + jnp.concatenate([bias, bias], axis=0)
            top = jnp.max(scores, axis=-1, keepdims=True)
            weights = jnp.exp(scores - top)
            total = jnp.sum(weights, axis=-1, keepdims=True)
            mixed = project(weights.astype(BF16), v_ref[head, :span, :]) / total
            mixed_ref[first : first + SPAN, at] = join_pair(mixed).astype(BF16)
            logs = top + jnp.log(total)
            old = stat_ref[first : first + SPAN, :]
            lane = lanes(old.shape)
            old = jnp.where(lane == 2 * slab, logs[:SPAN], old)
            stat_ref[first : first + SPAN, :] = jnp.where(lane == 2 * slab + 1, logs[SPAN:], old)

    lse_ref[...] = jnp.transpose(stat_ref[...])[: lse_ref.shape[0], :]


def attend(x_full, w_qkv, gain, cosine, sine, start, q_width, kv_width):
    rows = x_full.shape[0]
    heads = 2 * (kv_width // SLAB)
    flops = 2 * rows * x_full.shape[1] * (q_width + 2 * kv_width) + 8 * rows * rows * q_width
    return pl.pallas_call(
        attend_kernel,
        out_shape=(
            jax.ShapeDtypeStruct(x_full.shape, BF16),
            jax.ShapeDtypeStruct((rows, q_width), BF16),
            jax.ShapeDtypeStruct((heads, rows, SLAB), BF16),
            jax.ShapeDtypeStruct((heads, rows, SLAB), BF16),
            jax.ShapeDtypeStruct((rows, q_width), BF16),
            jax.ShapeDtypeStruct((q_width // HEAD_SIZE, rows), F32),
        ),
        in_specs=vmem_specs(6),
        out_specs=tuple(vmem_specs(6)),
        scratch_shapes=[pltpu.VMEM((SPAN, rows), F32), pltpu.VMEM((rows, SLAB), F32)],
        compiler_params=params(),
        cost_estimate=pl.CostEstimate(flops=flops, bytes_accessed=1 << 24, transcendentals=1 << 23),
        name="attend",
    )(x_full, w_qkv, gain, cosine, sine, start)


def attend_back_kernel(
    branch_ref, w_ref, q_ref, k_ref, v_ref, lse_ref, cos_ref, sin_ref, start_ref,
    dqkv_ref, dmix_ref, bias_ref, dq_ref, dk_ref, dv_ref,
):
    rows_all = branch_ref.shape[0]
    q_width = q_ref.shape[1]
    slabs = q_width // SLAB
    kv_heads = k_ref.shape[0]
    members = slabs // kv_heads
    scale = HEAD_SIZE ** (-0.5)

    @pl.loop(0, rows_all // SPAN)
    def _(step):
        rows = pl.ds(step * SPAN, SPAN)
        dmix_ref[rows, :] = project_back(branch_ref[rows, :], w_ref[...]).astype(BF16)

    dk_ref[...] = jnp.zeros_like(dk_ref)
    dv_ref[...] = jnp.zeros_like(dv_ref)
    for tile in range(rows_all // SPAN):
        first, span = tile * SPAN, (tile + 1) * SPAN
        key_ids = lax.broadcasted_iota(jnp.int32, (span, SPAN), 0)
        row_ids = first + lanes((span, SPAN))
        allowed = (key_ids >= start_ref[:, first : first + SPAN]) & (key_ids <= row_ids)
        bias_ref[:span, :] = jnp.where(allowed, 0.0, mask_fill)

        @pl.loop(0, slabs)
        def _(slab):
            at = pl.ds(pl.multiple_of(slab * SLAB, SLAB), SLAB)
            head = slab // members
            queries = head_pair(q_ref[first : first + SPAN, at])
            grads = head_pair(dmix_ref[first : first + SPAN, at])
            keys = k_ref[head, :span, :]
            scores = project_back(keys, queries)
            bias = bias_ref[:span, :]
            logs = jnp.concatenate(
                [
                    lse_ref[pl.ds(2 * slab, 1), first : first + SPAN],
                    lse_ref[pl.ds(2 * slab + 1, 1), first : first + SPAN],
                ],
                axis=1,
            )
            chances = jnp.exp(scores + jnp.concatenate([bias, bias], axis=1) - logs)
            chances_grad = project_back(v_ref[head, :span, :], grads)
            shared = jnp.sum(chances * chances_grad, axis=0, keepdims=True)
            score_grad = (chances * (chances_grad - shared)).astype(BF16)
            dv_ref[head, :span, :] += project(chances.astype(BF16), grads)
            dk_ref[head, :span, :] += project(score_grad, queries)
            dq_ref[first : first + SPAN, at] = join_pair(row_contract(score_grad, keys)) * scale

    left = lanes((SPAN, SLAB)) < HEAD_SIZE

    @pl.loop(0, rows_all // SPAN)
    def _(step):
        rows = pl.ds(step * SPAN, SPAN)
        cosine, sine = cos_ref[rows, :], sin_ref[rows, :]
        for slab in range(slabs):
            part = dq_ref[rows, slab * SLAB : (slab + 1) * SLAB]
            part = part * cosine - turned(part) * sine
            dqkv_ref[rows, slab * SLAB : (slab + 1) * SLAB] = part.astype(BF16)
        for pair in range(kv_heads // 2):
            joined = []
            for ref in (dk_ref, dv_ref):
                sums = []
                for head in (2 * pair, 2 * pair + 1):
                    full = ref[head, rows, :]
                    sums.append(full + pltpu.roll(full, HEAD_SIZE, 1))
                joined.append(jnp.where(left, sums[0], sums[1]))
            key, value = joined
            key = key * cosine - turned(key) * sine
            at = q_width + pair * SLAB
            dqkv_ref[rows, at : at + SLAB] = key.astype(BF16)
            at = at + (kv_heads // 2) * SLAB
            dqkv_ref[rows, at : at + SLAB] = value.astype(BF16)


def attend_back(branch_full, w_out, queries, keys, values, lse, cosine, sine, start):
    rows, q_width = queries.shape
    kv_heads = keys.shape[0]
    width = q_width + kv_heads * SLAB
    flops = 2 * rows * branch_full.shape[1] * q_width + 20 * rows * rows * q_width
    return pl.pallas_call(
        attend_back_kernel,
        out_shape=jax.ShapeDtypeStruct((rows, width), BF16),
        in_specs=vmem_specs(9),
        out_specs=vmem_specs(1)[0],
        scratch_shapes=[
            pltpu.VMEM((rows, q_width), BF16),
            pltpu.VMEM((rows, SPAN), F32),
            pltpu.VMEM((rows, q_width), F32),
            pltpu.VMEM((kv_heads, rows, SLAB), F32),
            pltpu.VMEM((kv_heads, rows, SLAB), F32),
        ],
        compiler_params=params(),
        cost_estimate=pl.CostEstimate(flops=flops, bytes_accessed=1 << 24, transcendentals=1 << 23),
        name="attend_back",
    )(branch_full, w_out, queries, keys, values, lse, cosine, sine, start)


class Line:
    def __init__(self, count):
        self.count = count
        self.place = lax.axis_index("tensor")
        self.has = (self.place < count - 1, self.place > 0)
        self.neighbour = (self.place + 1, self.place - 1)

    def barrier(self):
        semaphore = pltpu.get_barrier_semaphore()
        for way in (0, 1):
            @pl.when(self.has[way])
            def _(way=way):
                pl.semaphore_signal(semaphore, 1, device_id={"tensor": self.neighbour[way]})
        ends = (self.place == 0) | (self.place == self.count - 1)
        pl.semaphore_wait(semaphore, jnp.where(ends, 1, 2))

    def copy(self, source, target, send, receive, way):
        return pltpu.make_async_remote_copy(
            src_ref=source, dst_ref=target, send_sem=send, recv_sem=receive,
            device_id={"tensor": self.neighbour[way]},
        )


class Gather:
    def __init__(self, line, full, send, receive, chunk_rows, pieces):
        self.line, self.full, self.send, self.receive = line, full, send, receive
        self.chunk_rows, self.size = chunk_rows, chunk_rows // pieces

    def rows(self, chunk, piece):
        start = chunk * self.chunk_rows + piece * self.size
        return pl.ds(pl.multiple_of(start, self.size), self.size)

    def copy(self, chunk, piece, way, source=None):
        target = self.full.at[self.rows(chunk, piece)]
        return self.line.copy(
            target if source is None else source, target,
            self.send.at[way, chunk, piece], self.receive.at[way, chunk, piece], way,
        )

    def start(self, piece, source=None):
        for way in (0, 1):
            @pl.when(self.line.has[way])
            def _(way=way):
                self.copy(self.line.place, piece, way, source).start()

    def pass_on(self, piece, hops=None):
        line = self.line
        for hop in hops or range(1, line.count):
            for way, chunk in ((0, line.place - hop), (1, line.place + hop)):
                @pl.when((chunk >= 0) & (chunk < line.count))
                def _(way=way, chunk=chunk):
                    self.copy(chunk, piece, way).wait_recv()

                    @pl.when(line.has[way])
                    def _():
                        self.copy(chunk, piece, way).start()

    def finish(self, pieces, source=None):
        line = self.line
        for chunk in range(line.count):
            for piece in range(pieces):
                @pl.when(line.has[0] & (chunk <= line.place))
                def _():
                    self.copy(chunk, piece, 0, source).wait_send()

                @pl.when(line.has[1] & (chunk >= line.place))
                def _():
                    self.copy(chunk, piece, 1, source).wait_send()


class Scatter:
    def __init__(self, line, partial, landing, send, receive, chunk_rows, pieces):
        self.line, self.partial, self.landing = line, partial, landing
        self.send, self.receive = send, receive
        self.chunk_rows, self.size = chunk_rows, chunk_rows // pieces

    def rows(self, chunk, piece):
        start = chunk * self.chunk_rows + piece * self.size
        return pl.ds(pl.multiple_of(start, self.size), self.size)

    def copy(self, chunk, piece, way):
        rows = self.rows(chunk, piece)
        return self.line.copy(
            self.partial.at[rows], self.landing.at[way, rows],
            self.send.at[way, chunk, piece], self.receive.at[way, chunk, piece], way,
        )

    def step(self, piece):
        line = self.line
        for turn in range(line.count - 1):
            for way, chunk in ((0, line.count - 1 - turn), (1, turn)):
                beyond = chunk > line.place if way == 0 else chunk < line.place

                @pl.when(beyond)
                def _(way=way, chunk=chunk):
                    @pl.when(line.has[1 - way])
                    def _():
                        self.copy(chunk, piece, way).wait_recv()
                        rows = self.rows(chunk, piece)
                        total = self.partial[rows, :].astype(F32)
                        total = total + self.landing[way, rows, :].astype(F32)
                        self.partial[rows, :] = total.astype(BF16)

                    self.copy(chunk, piece, way).start()

    def arrived(self, piece):
        for way in (0, 1):
            @pl.when(self.line.has[1 - way])
            def _(way=way):
                self.copy(self.line.place, piece, way).wait_recv()

    def total(self, piece, part=None):
        rows = self.rows(self.line.place, piece) if part is None else part
        total = self.partial[rows, :].astype(F32)
        for way in (0, 1):
            got = self.landing[way, rows, :].astype(F32)
            total = total + jnp.where(self.line.has[1 - way], got, 0.0)
        return total

    def finish(self, pieces):
        line = self.line
        for chunk in range(line.count):
            for piece in range(pieces):
                @pl.when(chunk > line.place)
                def _():
                    self.copy(chunk, piece, 0).wait_send()

                @pl.when(chunk < line.place)
                def _():
                    self.copy(chunk, piece, 1).wait_send()


def copy_sems(count, pieces):
    return pltpu.SemaphoreType.DMA((2, count, pieces))


def gather_kernel(count, pieces, x_ref, full_ref, send, receive, local):
    line = Line(count)
    own = pl.ds(pl.multiple_of(line.place * x_ref.shape[0], x_ref.shape[0]), x_ref.shape[0])
    keep = pltpu.make_async_copy(x_ref, full_ref.at[own], local)
    keep.start()
    line.barrier()
    gather = Gather(line, full_ref, send, receive, x_ref.shape[0], pieces)
    for piece in range(pieces):
        gather.start(piece, x_ref.at[gather.rows(0, piece)])
    for hop in range(1, count):
        for piece in range(pieces):
            gather.pass_on(piece, (hop,))
    gather.finish(pieces)
    keep.wait()


def line_gather(x, count, collective_id, pieces=4):
    rows, width = x.shape
    return pl.pallas_call(
        functools.partial(gather_kernel, count, pieces),
        out_shape=jax.ShapeDtypeStruct((count * rows, width), x.dtype),
        in_specs=vmem_specs(1),
        out_specs=pl.BlockSpec(memory_space=pl.ANY),
        scratch_shapes=[
            copy_sems(count, pieces), copy_sems(count, pieces), pltpu.SemaphoreType.DMA
        ],
        compiler_params=params(collective_id=collective_id, has_side_effects=True),
        cost_estimate=pl.CostEstimate(
            flops=0, bytes_accessed=200 * rows * width, transcendentals=0
        ),
        name="line_gather",
    )(x)


def forward_turn_kernel(
    count, pieces, mixed_ref, w_ref, x_ref, gain_ref, middle_ref, full_ref,
    partial, landing, rs_send, rs_receive, ag_send, ag_receive,
):
    line = Line(count)
    chunk_rows = x_ref.shape[0]
    line.barrier()

    @pl.loop(0, partial.shape[0] // SPAN)
    def _(step):
        rows = pl.ds(step * SPAN, SPAN)
        partial[rows, :] = project(mixed_ref[rows, :], w_ref[...]).astype(BF16)

    scatter = Scatter(line, partial, landing, rs_send, rs_receive, chunk_rows, pieces)
    gather = Gather(line, full_ref, ag_send, ag_receive, chunk_rows, pieces)
    size = chunk_rows // pieces

    def settle(piece):
        scatter.arrived(piece)
        local = pl.ds(piece * size, size)
        middle = x_ref[local, :].astype(F32) + scatter.total(piece)
        middle_ref[local, :] = middle
        inverse = lax.rsqrt(jnp.mean(middle * middle, axis=-1, keepdims=True) + norm_epsilon)
        full_ref[gather.rows(line.place, piece), :] = (
            middle * inverse * gain_ref[...]
        ).astype(BF16)
        gather.start(piece)

    pipeline(pieces, scatter.step, settle, gather.pass_on)
    scatter.finish(pieces)
    gather.finish(pieces)


def pipeline(pieces, scatter_step, settle, pass_on):
    for turn in range(pieces + 2):
        if turn < pieces:
            scatter_step(turn)
        if 1 <= turn <= pieces:
            settle(turn - 1)
        if turn >= 2:
            pass_on(turn - 2)


def forward_turn(mixed, w_out, x, gain, count, collective_id, pieces=4):
    chunk_rows, width = x.shape
    rows = count * chunk_rows
    return pl.pallas_call(
        functools.partial(forward_turn_kernel, count, pieces),
        out_shape=(
            jax.ShapeDtypeStruct((chunk_rows, width), F32),
            jax.ShapeDtypeStruct((rows, width), BF16),
        ),
        in_specs=vmem_specs(4),
        out_specs=tuple(vmem_specs(2)),
        scratch_shapes=[
            pltpu.VMEM((rows, width), BF16),
            pltpu.VMEM((2, rows, width), BF16),
        ]
        + [copy_sems(count, pieces)] * 4,
        compiler_params=params(collective_id=collective_id, has_side_effects=True),
        cost_estimate=pl.CostEstimate(
            flops=2 * rows * width * mixed.shape[1],
            bytes_accessed=300 * chunk_rows * width, transcendentals=0,
        ),
        name="forward_turn",
    )(mixed, w_out, x, gain)


def backward_turn_kernel(
    count, pieces, given_ref, dy_ref, middle_ref, gain_ref,
    grad_ref, full_ref, gain_grad_ref,
    partial, landing, rs_send, rs_receive, ag_send, ag_receive, load,
):
    line = Line(count)
    chunk_rows = dy_ref.shape[0]
    fetch = pltpu.make_async_copy(given_ref, partial, load)
    fetch.start()
    line.barrier()
    fetch.wait()
    scatter = Scatter(line, partial, landing, rs_send, rs_receive, chunk_rows, pieces)
    gather = Gather(line, full_ref, ag_send, ag_receive, chunk_rows, pieces)
    size = chunk_rows // pieces
    gain_grad_ref[...] = jnp.zeros_like(gain_grad_ref)

    def settle(piece):
        scatter.arrived(piece)
        local = pl.ds(piece * size, size)
        total = scatter.total(piece)
        middle = middle_ref[local, :]
        grad, gain_grad = norm_back(total, middle, gain_ref[...])
        grad = grad + dy_ref[local, :].astype(F32)
        gain_grad_ref[...] += gain_grad
        grad_ref[local, :] = grad
        full_ref[gather.rows(line.place, piece), :] = grad.astype(BF16)
        gather.start(piece)

    pipeline(pieces, scatter.step, settle, gather.pass_on)
    scatter.finish(pieces)
    gather.finish(pieces)


def norm_back(grad, rows, gain):
    inverse = lax.rsqrt(jnp.mean(rows * rows, axis=-1, keepdims=True) + norm_epsilon)
    scaled = grad * gain
    common = jnp.mean(scaled * rows, axis=-1, keepdims=True) * (inverse * inverse * inverse)
    gain_grad = jnp.sum(grad * (rows * inverse), axis=0, keepdims=True)
    return inverse * scaled - rows * common, gain_grad


def backward_turn(given, dy, middle, gain, count, collective_id, pieces=4):
    chunk_rows, width = dy.shape
    rows = count * chunk_rows
    return pl.pallas_call(
        functools.partial(backward_turn_kernel, count, pieces),
        out_shape=(
            jax.ShapeDtypeStruct((chunk_rows, width), F32),
            jax.ShapeDtypeStruct((rows, width), BF16),
            jax.ShapeDtypeStruct((1, width), F32),
        ),
        in_specs=[pl.BlockSpec(memory_space=pl.ANY)] + vmem_specs(3),
        out_specs=tuple(vmem_specs(3)),
        scratch_shapes=[
            pltpu.VMEM((rows, width), BF16),
            pltpu.VMEM((2, rows, width), BF16),
        ]
        + [copy_sems(count, pieces)] * 4
        + [pltpu.SemaphoreType.DMA],
        compiler_params=params(collective_id=collective_id, has_side_effects=True),
        cost_estimate=pl.CostEstimate(
            flops=0, bytes_accessed=300 * chunk_rows * width, transcendentals=0
        ),
        name="backward_turn",
    )(given, dy, middle, gain)


def last_turn_kernel(
    count, pieces, dqkv_ref, w_ref, middle_grad_ref, x_ref, gain_ref,
    grad_ref, gain_grad_ref,
    partial, landing, rs_send, rs_receive,
):
    line = Line(count)
    chunk_rows = x_ref.shape[0]
    line.barrier()
    width = dqkv_ref.shape[1]

    @pl.loop(0, partial.shape[0] // SPAN)
    def _(step):
        rows = pl.ds(step * SPAN, SPAN)
        partial[rows, :] = project_back(dqkv_ref[rows, :], w_ref[:, :width]).astype(BF16)

    scatter = Scatter(line, partial, landing, rs_send, rs_receive, chunk_rows, pieces)
    size = chunk_rows // pieces
    gain_grad_ref[...] = jnp.zeros_like(gain_grad_ref)

    def settle(piece):
        scatter.arrived(piece)
        local = pl.ds(piece * size, size)
        total = scatter.total(piece)
        grad, gain_grad = norm_back(total, x_ref[local, :].astype(F32), gain_ref[...])
        gain_grad_ref[...] += gain_grad
        grad_ref[local, :] = (grad + middle_grad_ref[local, :]).astype(BF16)

    pipeline(pieces, scatter.step, settle, lambda piece: None)
    scatter.finish(pieces)


def last_turn(dqkv, w_qkv, middle_grad, x, gain, count, collective_id, pieces=4):
    chunk_rows, width = x.shape
    rows = count * chunk_rows
    return pl.pallas_call(
        functools.partial(last_turn_kernel, count, pieces),
        out_shape=(
            jax.ShapeDtypeStruct((chunk_rows, width), BF16),
            jax.ShapeDtypeStruct((1, width), F32),
        ),
        in_specs=vmem_specs(5),
        out_specs=tuple(vmem_specs(2)),
        scratch_shapes=[
            pltpu.VMEM((rows, width), BF16),
            pltpu.VMEM((2, rows, width), BF16),
        ]
        + [copy_sems(count, pieces)] * 2,
        compiler_params=params(collective_id=collective_id, has_side_effects=True),
        cost_estimate=pl.CostEstimate(
            flops=2 * rows * width * dqkv.shape[1],
            bytes_accessed=200 * chunk_rows * width, transcendentals=0,
        ),
        name="last_turn",
    )(dqkv, w_qkv, middle_grad, x, gain)


def scatter_sum(grad, axis):
    return lax.psum_scatter(grad.astype(BF16), axis, scatter_dimension=0, tiled=True)


def shards(
    inputs, cotangent, attn_gain, w_query, w_key, w_value, w_out, mlp_gain, w_gate, w_up, w_down,
    seq_lengths, group_perm, group_starts,
):
    count = lax.axis_size("tensor")
    group_rows = inputs.shape[0] * count
    q_width, kv_width = w_query.shape[1], w_key.shape[1]
    qkv_width = q_width + 2 * kv_width
    start, positions = group_layout(
        seq_lengths, group_perm, group_starts, lax.axis_index("dp"), group_rows, MOST_SEQS
    )
    cosine, sine = slab_tables(positions)

    gains = jnp.stack([attn_gain, mlp_gain], axis=1)
    gains = jnp.pad(gains, ((0, 0), (0, SLAB - 2)))
    packed = jnp.concatenate([w_query, w_key, w_value, gains], axis=1)
    qkv_full = lax.all_gather(packed, "dp", axis=0, tiled=True)
    out_full = lax.all_gather(w_out, "dp", axis=0, tiled=True)
    gate_full = lax.all_gather(w_gate, "dp", axis=0, tiled=True)
    up_full = lax.all_gather(w_up, "dp", axis=0, tiled=True)
    down_full = lax.all_gather(w_down, "dp", axis=0, tiled=True)
    grad_full = lax.all_gather(cotangent, "tensor", axis=0, tiled=True)
    gain_rows = jnp.transpose(qkv_full[:, qkv_width : qkv_width + 2].astype(F32))
    gain_one, gain_two = gain_rows[0:1], gain_rows[1:2]

    x_full = line_gather(inputs, count, 0)
    normed_full, queries, keys, values, mixed, lse = attend(
        x_full, qkv_full, gain_one, cosine, sine, start[:, None], q_width, kv_width
    )
    middle, normed_two_full = forward_turn(mixed, out_full, inputs, gain_two, count, 1)

    gate_pre = project(normed_two_full, gate_full)
    up_pre = project(normed_two_full, up_full)
    active_f, active_back = jax.vjp(
        lambda gate_in, up_in: jax.nn.silu(gate_in) * up_in, gate_pre, up_pre
    )
    active = active_f.astype(BF16)
    outputs = (
        middle
        + lax.psum_scatter(
            project(active, down_full).astype(BF16), "tensor", scatter_dimension=0, tiled=True
        ).astype(F32)
    ).astype(BF16)
    active_grad = project_back(grad_full, down_full)
    gate_grad_f, up_grad_f = active_back(active_grad)
    gate_grad = gate_grad_f.astype(BF16)
    up_grad = up_grad_f.astype(BF16)
    down_grad = scatter_sum(row_contract(active, grad_full), "dp")
    gate_weight_grad = scatter_sum(row_contract(normed_two_full, gate_grad), "dp")
    up_weight_grad = scatter_sum(row_contract(normed_two_full, up_grad), "dp")
    norm_two_grad = (project_back(gate_grad, gate_full) + project_back(up_grad, up_full)).astype(
        BF16
    )
    middle_grad, branch_full, gain_two_grad = backward_turn(
        norm_two_grad, cotangent, middle, gain_two, count, 2
    )
    dqkv = attend_back(
        branch_full, out_full, queries, keys, values, lse, cosine, sine, start[None, :]
    )
    out_grad = scatter_sum(row_contract(mixed, branch_full), "dp")
    qkv_grad = scatter_sum(row_contract(normed_full, dqkv), "dp").astype(F32)
    input_grad, gain_one_grad = last_turn(
        dqkv, qkv_full, middle_grad, inputs, gain_one, count, 3
    )
    gains_grad = lax.psum(
        lax.psum_scatter(
            jnp.concatenate([gain_one_grad, gain_two_grad], axis=0), "dp",
            scatter_dimension=1, tiled=True,
        ),
        "tensor",
    )
    return (
        outputs,
        input_grad,
        gains_grad[0],
        qkv_grad[:, :q_width],
        qkv_grad[:, q_width : q_width + kv_width],
        qkv_grad[:, q_width + kv_width :],
        out_grad.astype(F32),
        gains_grad[1],
        gate_weight_grad.astype(F32),
        up_weight_grad.astype(F32),
        down_grad.astype(F32),
    )


def solution(mesh):
    in_specs = (
        P(("dp", "tensor"), None),
        P(("dp", "tensor"), None),
        P("dp"),
        P("dp", "tensor"),
        P("dp", "tensor"),
        P("dp", "tensor"),
        P(("tensor", "dp"), None),
        P("dp"),
        P("dp", "tensor"),
        P("dp", "tensor"),
        P(("tensor", "dp"), None),
        P(),
        P(),
        P(),
    )
    out_specs = (
        P(("dp", "tensor"), None),
        P(("dp", "tensor"), None),
        P("dp"),
        P("dp", "tensor"),
        P("dp", "tensor"),
        P("dp", "tensor"),
        P(("tensor", "dp"), None),
        P("dp"),
        P("dp", "tensor"),
        P("dp", "tensor"),
        P(("tensor", "dp"), None),
    )
    return jax.shard_map(shards, mesh=mesh, in_specs=in_specs, out_specs=out_specs, check_vma=False)
```

```python
import functools
import math

import jax
import jax.numpy as jnp
from jax import lax
from jax.experimental import pallas as pl
from jax.experimental.pallas import tpu as pltpu
from jax.sharding import PartitionSpec as P

HEAD_SIZE = 64
MOST_SEQS = 2
SLAB = 128
SPAN = 256

norm_epsilon = 1e-05
rope_theta = 500000.0
rope_factor = 32.0
low_factor = 1.0
high_factor = 4.0
context_span = 8192.0
mask_fill = -1e30

F32 = jnp.float32
BF16 = jnp.bfloat16
VMEM_LIMIT = 60 * 1024 * 1024


def rotary_freqs(head_size):
    exponents = jnp.arange(0, head_size, 2).astype(jnp.float32) / head_size
    inverse = 1.0 / jnp.power(jnp.float32(rope_theta), exponents)
    wavelength = 2.0 * math.pi / inverse
    smooth = (context_span / wavelength - low_factor) / (high_factor - low_factor)
    blended = (1.0 - smooth) * inverse / rope_factor + smooth * inverse
    scaled = jnp.where(wavelength > context_span / low_factor, inverse / rope_factor, blended)
    return jnp.where(wavelength < context_span / high_factor, inverse, scaled)


def slab_tables(positions):
    freqs = rotary_freqs(HEAD_SIZE)
    freqs = jnp.concatenate([freqs] * 4)
    angles = positions.astype(jnp.float32)[:, None] * freqs[None, :]
    low_half = (jnp.arange(SLAB) % HEAD_SIZE) < HEAD_SIZE // 2
    sines = jnp.sin(angles)
    return jnp.cos(angles), jnp.where(low_half[None, :], -sines, sines)


def group_layout(seq_lengths, group_perm, group_starts, group_id, row_total, slot_total):
    bounds = jnp.arange(group_starts.shape[0], dtype=jnp.int32)
    numbers = jnp.arange(group_perm.shape[0], dtype=jnp.int32)
    opening = jnp.sum(jnp.where(bounds == group_id, group_starts, 0))
    closing = jnp.sum(jnp.where(bounds == group_id + 1, group_starts, 0))
    row_ids = jnp.arange(row_total, dtype=jnp.int32)
    offset = jnp.zeros((row_total,), jnp.int32)
    finish = jnp.zeros((), jnp.int32)
    for slot_id in range(slot_total):
        slot_place = opening + slot_id
        sequence = jnp.sum(jnp.where(numbers == slot_place, group_perm, 0))
        length = jnp.sum(jnp.where(numbers == sequence, seq_lengths, 0))
        length = jnp.where(slot_place < closing, length, 0)
        finish = finish + length
        offset = jnp.where(row_ids >= finish, finish, offset)
    return offset, row_ids - offset


def project(left, right):
    return jnp.dot(left, right, preferred_element_type=F32)


def project_back(left, right):
    return lax.dot_general(left, right, (((1,), (1,)), ((), ())), preferred_element_type=F32)


def row_contract(left, right):
    return lax.dot_general(left, right, (((0,), (0,)), ((), ())), preferred_element_type=F32)


def lanes(shape):
    return lax.broadcasted_iota(jnp.int32, shape, len(shape) - 1)


def turned(slab):
    half = HEAD_SIZE // 2
    ahead = pltpu.roll(slab, SLAB - half, 1)
    behind = pltpu.roll(slab, half, 1)
    return jnp.where(lanes(slab.shape) % HEAD_SIZE < half, ahead, behind)


def head_pair(slab):
    left = lanes(slab.shape) < HEAD_SIZE
    zero = jnp.zeros_like(slab)
    return jnp.concatenate([jnp.where(left, slab, zero), jnp.where(left, zero, slab)], axis=0)


def join_pair(stacked):
    half = stacked.shape[0] // 2
    left = lanes((half, SLAB)) < HEAD_SIZE
    return jnp.where(left, stacked[:half], stacked[half:])


def params(**kwargs):
    return pltpu.CompilerParams(vmem_limit_bytes=VMEM_LIMIT, **kwargs)


def vmem_specs(count):
    return [pl.BlockSpec(memory_space=pltpu.VMEM)] * count


def attend_kernel(
    x_ref, w_ref, gain_ref, cos_ref, sin_ref, start_ref,
    normed_ref, q_ref, k_ref, v_ref, mixed_ref, lse_ref, bias_ref, stat_ref,
):
    rows_all = x_ref.shape[0]
    q_width = q_ref.shape[1]
    kv_slabs = v_ref.shape[0] // 2
    slabs = q_width // SLAB
    scale = HEAD_SIZE ** (-0.5)

    @pl.loop(0, rows_all // SPAN)
    def _(step):
        rows = pl.ds(step * SPAN, SPAN)
        x = x_ref[rows, :].astype(F32)
        inverse = lax.rsqrt(jnp.mean(x * x, axis=-1, keepdims=True) + norm_epsilon)
        normed = (x * inverse * gain_ref[...]).astype(BF16)
        normed_ref[rows, :] = normed
        pre = project(normed, w_ref[:, : q_width + 2 * kv_slabs * SLAB])
        cosine, sine = cos_ref[rows, :], sin_ref[rows, :]
        for slab in range(slabs):
            part = pre[:, slab * SLAB : (slab + 1) * SLAB]
            part = (part * cosine + turned(part) * sine).astype(BF16)
            q_ref[rows, slab * SLAB : (slab + 1) * SLAB] = (part.astype(F32) * scale).astype(BF16)
        left = lanes((SPAN, SLAB)) < HEAD_SIZE
        for pair in range(kv_slabs):
            at = q_width + pair * SLAB
            key = pre[:, at : at + SLAB]
            key = key * cosine + turned(key) * sine
            at = at + kv_slabs * SLAB
            value = pre[:, at : at + SLAB]
            for ref, full in ((k_ref, key), (v_ref, value)):
                other = pltpu.roll(full, HEAD_SIZE, 1)
                ref[2 * pair, rows, :] = jnp.where(left, full, other).astype(BF16)
                ref[2 * pair + 1, rows, :] = jnp.where(left, other, full).astype(BF16)

    members = slabs // (2 * kv_slabs)
    for tile in range(rows_all // SPAN):
        first, span = tile * SPAN, (tile + 1) * SPAN
        columns = lanes((SPAN, span))
        row_ids = first + lax.broadcasted_iota(jnp.int32, (SPAN, span), 0)
        allowed = (columns >= start_ref[first : first + SPAN, :]) & (columns <= row_ids)
        bias_ref[:, :span] = jnp.where(allowed, 0.0, mask_fill)

        @pl.loop(0, slabs)
        def _(slab):
            at = pl.ds(pl.multiple_of(slab * SLAB, SLAB), SLAB)
            head = slab // members
            stacked = head_pair(q_ref[first : first + SPAN, at])
            scores = project_back(stacked, k_ref[head, :span, :])
            bias = bias_ref[:, :span]
            scores = scores + jnp.concatenate([bias, bias], axis=0)
            top = jnp.max(scores, axis=-1, keepdims=True)
            weights = jnp.exp(scores - top)
            total = jnp.sum(weights, axis=-1, keepdims=True)
            mixed = project(weights.astype(BF16), v_ref[head, :span, :]) / total
            mixed_ref[first : first + SPAN, at] = join_pair(mixed).astype(BF16)
            logs = top + jnp.log(total)
            old = stat_ref[first : first + SPAN, :]
            lane = lanes(old.shape)
            old = jnp.where(lane == 2 * slab, logs[:SPAN], old)
            stat_ref[first : first + SPAN, :] = jnp.where(lane == 2 * slab + 1, logs[SPAN:], old)

    lse_ref[...] = jnp.transpose(stat_ref[...])[: lse_ref.shape[0], :]


def attend(x_full, w_qkv, gain, cosine, sine, start, q_width, kv_width):
    rows = x_full.shape[0]
    heads = 2 * (kv_width // SLAB)
    flops = 2 * rows * x_full.shape[1] * (q_width + 2 * kv_width) + 8 * rows * rows * q_width
    return pl.pallas_call(
        attend_kernel,
        out_shape=(
            jax.ShapeDtypeStruct(x_full.shape, BF16),
            jax.ShapeDtypeStruct((rows, q_width), BF16),
            jax.ShapeDtypeStruct((heads, rows, SLAB), BF16),
            jax.ShapeDtypeStruct((heads, rows, SLAB), BF16),
            jax.ShapeDtypeStruct((rows, q_width), BF16),
            jax.ShapeDtypeStruct((q_width // HEAD_SIZE, rows), F32),
        ),
        in_specs=vmem_specs(6),
        out_specs=tuple(vmem_specs(6)),
        scratch_shapes=[pltpu.VMEM((SPAN, rows), F32), pltpu.VMEM((rows, SLAB), F32)],
        compiler_params=params(),
        cost_estimate=pl.CostEstimate(flops=flops, bytes_accessed=1 << 24, transcendentals=1 << 23),
        name="attend",
    )(x_full, w_qkv, gain, cosine, sine, start)


SUBS = 4
BLOCK = 1024


class Line:
    def __init__(self, count):
        self.count = count
        self.place = lax.axis_index("tensor")
        self.has = (self.place < count - 1, self.place > 0)
        self.neighbour = (self.place + 1, self.place - 1)
        other = count - 1 - self.place
        self.lag = jnp.where(self.place > other, self.place, other)

    def greet(self, semaphore):
        for way in (0, 1):
            @pl.when(self.has[way])
            def _(way=way):
                pl.semaphore_signal(semaphore, 1, device_id={"tensor": self.neighbour[way]})
        ends = (self.place == 0) | (self.place == self.count - 1)
        return jnp.where(ends, 1, 2)

    def barrier(self):
        semaphore = pltpu.get_barrier_semaphore()
        pl.semaphore_wait(semaphore, self.greet(semaphore))

    def copy(self, source, target, send, receive, way):
        return pltpu.make_async_remote_copy(
            src_ref=source, dst_ref=target, send_sem=send, recv_sem=receive,
            device_id={"tensor": self.neighbour[way]},
        )


class Gather:
    def __init__(self, line, full, send, receive, chunk_rows, pieces, lags=None):
        self.line, self.full, self.send, self.receive = line, full, send, receive
        self.chunk_rows, self.size, self.pieces = chunk_rows, chunk_rows // pieces, pieces
        self.lags = lags or [0] * line.count

    def rows(self, chunk, piece):
        start = chunk * self.chunk_rows + piece * self.size
        return pl.ds(pl.multiple_of(start, self.size), self.size)

    def copy(self, chunk, piece, way, source=None):
        target = self.full.at[self.rows(chunk, piece)]
        return self.line.copy(
            target if source is None else source, target,
            self.send.at[way, chunk, piece], self.receive.at[way, chunk, piece], way,
        )

    def start(self, piece, source=None):
        for way in (0, 1):
            @pl.when(self.line.has[way])
            def _(way=way):
                self.copy(self.line.place, piece, way, source).start()

    def turn(self, turn):
        line = self.line
        for chunk in range(line.count):
            for way in (0, 1):
                hop = line.place - chunk if way == 0 else chunk - line.place
                piece = turn - self.lags[chunk] - hop

                @pl.when((hop > 0) & (piece >= 0) & (piece < self.pieces))
                def _(way=way, chunk=chunk, piece=piece):
                    self.copy(chunk, piece, way).wait_recv()

                    @pl.when(line.has[way])
                    def _():
                        self.copy(chunk, piece, way).start()

    def finish(self, source=None):
        line = self.line

        @pl.loop(0, self.pieces)
        def _(piece):
            for chunk in range(line.count):
                @pl.when(line.has[0] & (chunk <= line.place))
                def _(chunk=chunk):
                    self.copy(chunk, piece, 0, source).wait_send()

                @pl.when(line.has[1] & (chunk >= line.place))
                def _(chunk=chunk):
                    self.copy(chunk, piece, 1, source).wait_send()


class Scatter:
    def __init__(self, line, partial, landing, send, receive, chunk_rows, pieces):
        self.line, self.partial, self.landing = line, partial, landing
        self.send, self.receive = send, receive
        self.chunk_rows, self.size, self.pieces = chunk_rows, chunk_rows // pieces, pieces

    def rows(self, chunk, piece):
        start = chunk * self.chunk_rows + piece * self.size
        return pl.ds(pl.multiple_of(start, self.size), self.size)

    def landed(self, chunk, piece, way, owner):
        if way == 1:
            chunk = jnp.where(chunk == owner, self.line.count, chunk)
        return self.rows(chunk, piece)

    def copy(self, chunk, piece, way, owner=None):
        owner = self.line.neighbour[way] if owner is None else owner
        return self.line.copy(
            self.partial.at[self.rows(chunk, piece)],
            self.landing.at[self.landed(chunk, piece, way, owner)],
            self.send.at[way, chunk, piece], self.receive.at[way, chunk, piece], way,
        )

    def wait(self, chunk, piece, way):
        self.copy(chunk, piece, way, self.line.place).wait_recv()

    def forward(self, piece, way):
        line = self.line
        for step in range(line.count - 1):
            chunk = line.count - 1 - step if way == 0 else step
            beyond = chunk > line.place if way == 0 else chunk < line.place

            @pl.when(beyond)
            def _(chunk=chunk):
                @pl.when(line.has[1 - way])
                def _():
                    self.wait(chunk, piece, way)
                    rows = self.rows(chunk, piece)
                    total = self.partial[rows, :].astype(F32)
                    total = total + self.landing[rows, :].astype(F32)
                    self.partial[rows, :] = total.astype(BF16)

                self.copy(chunk, piece, way).start()

    def turn(self, turn):
        line = self.line
        for way, lag in ((0, line.place), (1, line.count - 1 - line.place)):
            piece = turn - lag

            @pl.when((piece >= 0) & (piece < self.pieces))
            def _(way=way, piece=piece):
                self.forward(piece, way)

    def settle(self, turn, use):
        piece = turn - self.line.lag

        @pl.when((piece >= 0) & (piece < self.pieces))
        def _():
            for way in (0, 1):
                @pl.when(self.line.has[1 - way])
                def _(way=way):
                    self.wait(self.line.place, piece, way)
            use(piece)

    def total(self, piece):
        place = self.line.place
        total = self.partial[self.rows(place, piece), :].astype(F32)
        for way in (0, 1):
            got = self.landing[self.landed(place, piece, way, place), :].astype(F32)
            total = total + jnp.where(self.line.has[1 - way], got, 0.0)
        return total

    def finish(self):
        line = self.line

        @pl.loop(0, self.pieces)
        def _(piece):
            for chunk in range(line.count):
                @pl.when(chunk > line.place)
                def _(chunk=chunk):
                    self.copy(chunk, piece, 0).wait_send()

                @pl.when(chunk < line.place)
                def _(chunk=chunk):
                    self.copy(chunk, piece, 1).wait_send()


class Fold:
    def __init__(self, replicas, sums, traded, arrived, pair_sems, sends, receives):
        self.halves = replicas // 2
        self.sums, self.traded, self.arrived = sums, traded, arrived
        self.pair_sems, self.sends, self.receives = pair_sems, sends, receives
        replica = lax.axis_index("dp")
        self.side, self.mine = replica % 2, replica // 2
        self.partner = replica + 1 - 2 * self.side

    def greet(self, semaphore):
        pl.semaphore_signal(semaphore, 1, device_id={"dp": self.partner})
        for step in range(1, self.halves):
            peer = 2 * ((self.mine + step) % self.halves) + self.side
            pl.semaphore_signal(semaphore, 1, device_id={"dp": peer})
        return self.halves

    def pair(self):
        return pltpu.make_async_remote_copy(
            src_ref=self.sums.at[:, 1 - self.side], dst_ref=self.traded,
            send_sem=self.pair_sems.at[0], recv_sem=self.pair_sems.at[1],
            device_id={"dp": self.partner},
        )

    def peer(self, half, landing):
        return pltpu.make_async_remote_copy(
            src_ref=self.sums.at[half, self.side], dst_ref=self.arrived.at[landing],
            send_sem=self.sends.at[half], recv_sem=self.receives.at[landing],
            device_id={"dp": 2 * half + self.side},
        )

    def others(self):
        return [(self.mine + step) % self.halves for step in range(1, self.halves)]

    def spread(self):
        self.pair().wait_recv()

        @pl.loop(0, self.halves)
        def _(half):
            total = self.sums[half, self.side].astype(F32) + self.traded[half].astype(F32)
            self.sums[half, self.side] = total.astype(BF16)

        for half in self.others():
            self.peer(half, self.mine).start()

    def total(self):
        total = self.sums[self.mine, self.side].astype(F32)
        for half in self.others():
            self.peer(half, half).wait_recv()
            total = total + self.arrived[half].astype(F32)
        return total

    def finish(self):
        self.pair().wait_send()
        for half in self.others():
            self.peer(half, self.mine).wait_send()


def fold_scratch(replicas, rows, width):
    halves = replicas // 2
    return [
        pltpu.VMEM((halves, 2, rows, width), BF16),
        pltpu.VMEM((halves, rows, width), BF16),
        pltpu.VMEM((halves, rows, width), BF16),
        pltpu.SemaphoreType.DMA((2,)),
        pltpu.SemaphoreType.DMA((halves,)),
        pltpu.SemaphoreType.DMA((halves,)),
    ]


def attend_back_kernel(
    replicas, branch_ref, w_ref, mixed_ref, q_ref, k_ref, v_ref, lse_ref, cos_ref, sin_ref,
    start_ref, dqkv_ref, weight_grad_ref, dmix_ref, bias_ref, dq_ref, dk_ref, dv_ref,
    sums, traded, arrived, pair_sems, sends, receives,
):
    fold = Fold(replicas, sums, traded, arrived, pair_sems, sends, receives)
    semaphore = pltpu.get_barrier_semaphore()
    pl.semaphore_wait(semaphore, fold.greet(semaphore))
    weight_rows = sums.shape[2]
    for step in range(mixed_ref.shape[1] // SLAB):
        first = step * SLAB
        product = row_contract(mixed_ref[:, first : first + SLAB], branch_ref[...]).astype(BF16)
        for row in range(0, SLAB, weight_rows):
            owner = (first + row) // weight_rows
            sums[owner // 2, owner % 2] = product[row : row + weight_rows]
    fold.pair().start()

    rows_all = branch_ref.shape[0]
    q_width = q_ref.shape[1]
    slabs = q_width // SLAB
    kv_heads = k_ref.shape[0]
    members = slabs // kv_heads
    scale = HEAD_SIZE ** (-0.5)

    @pl.loop(0, rows_all // SPAN)
    def _(step):
        rows = pl.ds(step * SPAN, SPAN)
        dmix_ref[rows, :] = project_back(branch_ref[rows, :], w_ref[...]).astype(BF16)

    fold.spread()
    dk_ref[...] = jnp.zeros_like(dk_ref)
    dv_ref[...] = jnp.zeros_like(dv_ref)
    for tile in range(rows_all // SPAN):
        first, span = tile * SPAN, (tile + 1) * SPAN
        key_ids = lax.broadcasted_iota(jnp.int32, (span, SPAN), 0)
        row_ids = first + lanes((span, SPAN))
        allowed = (key_ids >= start_ref[:, first : first + SPAN]) & (key_ids <= row_ids)
        bias_ref[:span, :] = jnp.where(allowed, 0.0, mask_fill)

        @pl.loop(0, slabs)
        def _(slab):
            at = pl.ds(pl.multiple_of(slab * SLAB, SLAB), SLAB)
            head = slab // members
            queries = head_pair(q_ref[first : first + SPAN, at])
            grads = head_pair(dmix_ref[first : first + SPAN, at])
            keys = k_ref[head, :span, :]
            scores = project_back(keys, queries)
            bias = bias_ref[:span, :]
            logs = jnp.concatenate(
                [
                    lse_ref[pl.ds(2 * slab, 1), first : first + SPAN],
                    lse_ref[pl.ds(2 * slab + 1, 1), first : first + SPAN],
                ],
                axis=1,
            )
            chances = jnp.exp(scores + jnp.concatenate([bias, bias], axis=1) - logs)
            chances_grad = project_back(v_ref[head, :span, :], grads)
            shared = jnp.sum(chances * chances_grad, axis=0, keepdims=True)
            score_grad = (chances * (chances_grad - shared)).astype(BF16)
            dv_ref[head, :span, :] += project(chances.astype(BF16), grads)
            dk_ref[head, :span, :] += project(score_grad, queries)
            dq_ref[first : first + SPAN, at] = join_pair(row_contract(score_grad, keys)) * scale

    left = lanes((SPAN, SLAB)) < HEAD_SIZE

    @pl.loop(0, rows_all // SPAN)
    def _(step):
        rows = pl.ds(step * SPAN, SPAN)
        cosine, sine = cos_ref[rows, :], sin_ref[rows, :]
        for slab in range(slabs):
            part = dq_ref[rows, slab * SLAB : (slab + 1) * SLAB]
            part = part * cosine - turned(part) * sine
            dqkv_ref[rows, slab * SLAB : (slab + 1) * SLAB] = part.astype(BF16)
        for pair in range(kv_heads // 2):
            joined = []
            for ref in (dk_ref, dv_ref):
                sums = []
                for head in (2 * pair, 2 * pair + 1):
                    full = ref[head, rows, :]
                    sums.append(full + pltpu.roll(full, HEAD_SIZE, 1))
                joined.append(jnp.where(left, sums[0], sums[1]))
            key, value = joined
            key = key * cosine - turned(key) * sine
            at = q_width + pair * SLAB
            dqkv_ref[rows, at : at + SLAB] = key.astype(BF16)
            at = at + (kv_heads // 2) * SLAB
            dqkv_ref[rows, at : at + SLAB] = value.astype(BF16)

    weight_grad_ref[...] = fold.total()
    fold.finish()


def attend_back(
    branch_full, w_out, mixed, queries, keys, values, lse, cosine, sine, start,
    replicas, collective_id,
):
    rows, q_width = queries.shape
    kv_heads = keys.shape[0]
    width = q_width + kv_heads * SLAB
    flops = 2 * rows * branch_full.shape[1] * q_width + 20 * rows * rows * q_width
    return pl.pallas_call(
        functools.partial(attend_back_kernel, replicas),
        out_shape=(
            jax.ShapeDtypeStruct((rows, width), BF16),
            jax.ShapeDtypeStruct((q_width // replicas, branch_full.shape[1]), F32),
        ),
        in_specs=vmem_specs(10),
        out_specs=tuple(vmem_specs(2)),
        scratch_shapes=[
            pltpu.VMEM((rows, q_width), BF16),
            pltpu.VMEM((rows, SPAN), F32),
            pltpu.VMEM((rows, q_width), F32),
            pltpu.VMEM((kv_heads, rows, SLAB), F32),
            pltpu.VMEM((kv_heads, rows, SLAB), F32),
        ]
        + fold_scratch(replicas, q_width // replicas, branch_full.shape[1]),
        compiler_params=params(collective_id=collective_id, has_side_effects=True),
        cost_estimate=pl.CostEstimate(flops=flops, bytes_accessed=1 << 24, transcendentals=1 << 23),
        name="attend_back",
    )(branch_full, w_out, mixed, queries, keys, values, lse, cosine, sine, start)


def landing_rows(count, chunk_rows):
    return (count + 1) * chunk_rows


def copy_sems(count, pieces):
    return pltpu.SemaphoreType.DMA((2, count, pieces))


def settle_lags(count):
    return [max(place, count - 1 - place) for place in range(count)]


def gather_kernel(count, pieces, x_ref, full_ref, send, receive, local):
    line = Line(count)
    chunk_rows = x_ref.shape[0]
    own = pl.ds(pl.multiple_of(line.place * chunk_rows, chunk_rows), chunk_rows)
    keep = pltpu.make_async_copy(x_ref, full_ref.at[own], local)
    keep.start()
    line.barrier()
    gather = Gather(line, full_ref, send, receive, chunk_rows, pieces)
    for piece in range(pieces):
        gather.start(piece, x_ref.at[gather.rows(0, piece)])

    @pl.loop(1, pieces + count - 1)
    def _(turn):
        gather.turn(turn)

    gather.finish(x_ref.at[gather.rows(0, 0)])
    keep.wait()


def line_gather(x, count, collective_id, pieces=8):
    rows, width = x.shape
    return pl.pallas_call(
        functools.partial(gather_kernel, count, pieces),
        out_shape=jax.ShapeDtypeStruct((count * rows, width), x.dtype),
        in_specs=vmem_specs(1),
        out_specs=pl.BlockSpec(memory_space=pl.ANY),
        scratch_shapes=[
            copy_sems(count, pieces), copy_sems(count, pieces), pltpu.SemaphoreType.DMA
        ],
        compiler_params=params(collective_id=collective_id, has_side_effects=True),
        cost_estimate=pl.CostEstimate(
            flops=0, bytes_accessed=200 * rows * width, transcendentals=0
        ),
        name="line_gather",
    )(x)


def forward_turn_kernel(
    count, pieces, mixed_ref, w_ref, x_ref, gain_ref, middle_ref, full_ref,
    partial, landing, rs_send, rs_receive, ag_send, ag_receive,
):
    line = Line(count)
    chunk_rows = x_ref.shape[0]
    line.barrier()

    @pl.loop(0, partial.shape[0] // SPAN)
    def _(step):
        rows = pl.ds(pl.multiple_of(step * SPAN, SPAN), SPAN)
        partial[rows, :] = project(mixed_ref[rows, :], w_ref[...]).astype(BF16)

    scatter = Scatter(line, partial, landing, rs_send, rs_receive, chunk_rows, pieces)
    gather = Gather(
        line, full_ref, ag_send, ag_receive, chunk_rows, pieces, settle_lags(count)
    )
    size = chunk_rows // pieces

    def settle(piece):
        local = pl.ds(pl.multiple_of(piece * size, size), size)
        middle = x_ref[local, :].astype(F32) + scatter.total(piece)
        middle_ref[local, :] = middle
        inverse = lax.rsqrt(jnp.mean(middle * middle, axis=-1, keepdims=True) + norm_epsilon)
        normed = (middle * inverse * gain_ref[...]).astype(BF16)
        full_ref[gather.rows(line.place, piece), :] = normed
        gather.start(piece)

    @pl.loop(0, pieces + 2 * (count - 1))
    def _(turn):
        scatter.turn(turn)
        gather.turn(turn)
        scatter.settle(turn, settle)

    scatter.finish()
    gather.finish()


def forward_turn(mixed, w_out, x, gain, count, collective_id, pieces=8):
    chunk_rows, width = x.shape
    rows = count * chunk_rows
    return pl.pallas_call(
        functools.partial(forward_turn_kernel, count, pieces),
        out_shape=(
            jax.ShapeDtypeStruct((chunk_rows, width), F32),
            jax.ShapeDtypeStruct((rows, width), BF16),
        ),
        in_specs=vmem_specs(4),
        out_specs=tuple(vmem_specs(2)),
        scratch_shapes=[
            pltpu.VMEM((rows, width), BF16),
            pltpu.VMEM((landing_rows(count, chunk_rows), width), BF16),
        ]
        + [copy_sems(count, pieces)] * 4,
        compiler_params=params(collective_id=collective_id, has_side_effects=True),
        cost_estimate=pl.CostEstimate(
            flops=2 * rows * width * mixed.shape[1],
            bytes_accessed=300 * chunk_rows * width, transcendentals=0,
        ),
        name="forward_turn",
    )(mixed, w_out, x, gain)


def hidden_kernel(
    count, pieces, normed_ref, own_ref, middle_ref, gate_ref, up_ref, down_ref,
    full_ref, active_ref, gate_grad_ref, up_grad_ref, back_ref, out_ref,
    gate, up, down, normed, dy, active, slope, value, up_grad, back,
    partial, landing, rs_send, rs_receive, ag_send, ag_receive, loads, stores,
):
    line = Line(count)
    chunk_rows = own_ref.shape[0]
    hidden = gate_ref.shape[1]
    width = gate_ref.shape[0]
    sub = chunk_rows // SUBS
    fetches = [
        pltpu.make_async_copy(source, target, loads.at[at])
        for at, (source, target) in enumerate(
            ((normed_ref, normed), (gate_ref, gate), (up_ref, up), (down_ref, down))
        )
    ]
    for fetch in fetches:
        fetch.start()
    line.barrier()
    gather = Gather(line, dy, ag_send, ag_receive, chunk_rows, SUBS)
    scatter = Scatter(line, partial, landing, rs_send, rs_receive, chunk_rows, pieces)
    for piece in range(SUBS):
        gather.start(piece, own_ref.at[gather.rows(0, piece)])
    own = pl.ds(pl.multiple_of(line.place * chunk_rows, chunk_rows), chunk_rows)
    place_own = pltpu.make_async_copy(own_ref, dy.at[own], loads.at[4])
    place_own.start()
    gate_grad = active
    outs = ((active, active_ref), (gate_grad, gate_grad_ref), (up_grad, up_grad_ref),
            (back, back_ref))

    def store(which, step):
        source, target = outs[which]
        rows = pl.ds(pl.multiple_of(step * sub, sub), sub)
        return pltpu.make_async_copy(source, target.at[:, rows], stores.at[which])

    def rows_of(chunk, step):
        return pl.ds(pl.multiple_of(chunk * chunk_rows + step * sub, sub), sub)

    def picked(ref, step, at=slice(None)):
        return jnp.concatenate([ref[rows_of(chunk, step), at] for chunk in range(count)], axis=0)

    def put(ref, at, rows):
        for chunk in range(count):
            ref[chunk, :, at] = rows[chunk * sub : (chunk + 1) * sub]

    def whole(ref):
        return jnp.concatenate([ref[chunk] for chunk in range(count)], axis=0)

    def settle(piece):
        size = chunk_rows // pieces
        local = pl.ds(pl.multiple_of(piece * size, size), size)
        out_ref[local, :] = (middle_ref[local, :] + scatter.total(piece)).astype(BF16)

    def exchange(turn):
        scatter.turn(turn)
        gather.turn(turn)
        scatter.settle(turn, settle)

    for at in range(3):
        fetches[at].wait()

    @pl.loop(0, SUBS)
    def _(step):
        @pl.when(step > 0)
        def _():
            store(0, step - 1).wait()

        @pl.loop(0, hidden // BLOCK)
        def _(block):
            at = pl.ds(pl.multiple_of(block * BLOCK, BLOCK), BLOCK)
            source = picked(normed, step)
            gate_pre = project(source, gate[:, at])
            up_pre = project(source, up[:, at])
            chance = 1.0 / (1.0 + jnp.exp(-gate_pre))
            silu = gate_pre * chance
            put(active, at, (silu * up_pre).astype(BF16))
            put(value.at[step], at, silu.astype(BF16))
            raised = up_pre * chance * (1.0 + gate_pre * (1.0 - chance))
            put(slope.at[step], at, raised.astype(BF16))

        store(0, step).start()

        @pl.when(step == 0)
        def _():
            fetches[3].wait()

        @pl.loop(0, width // BLOCK)
        def _(block):
            at = pl.ds(pl.multiple_of(block * BLOCK, BLOCK), BLOCK)
            product = project(whole(active), down[:, at]).astype(BF16)
            for chunk in range(count):
                partial[rows_of(chunk, step), at] = product[chunk * sub : (chunk + 1) * sub]

        exchange(step)

    @pl.loop(0, SUBS)
    def _(step):
        @pl.when(step == 0)
        def _():
            store(0, SUBS - 1).wait()
            place_own.wait()

        @pl.when(step > 0)
        def _():
            for which in (1, 2, 3):
                store(which, step - 1).wait()

        @pl.loop(0, hidden // BLOCK)
        def _(block):
            at = pl.ds(pl.multiple_of(block * BLOCK, BLOCK), BLOCK)
            active_grad = project_back(picked(dy, step), down[at, :])
            for chunk in range(count):
                grad = active_grad[chunk * sub : (chunk + 1) * sub]
                here = (grad * slope[step, chunk, :, at].astype(F32)).astype(BF16)
                gate_grad[chunk, :, at] = here
                here = (grad * value[step, chunk, :, at].astype(F32)).astype(BF16)
                up_grad[chunk, :, at] = here

        for which in (1, 2):
            store(which, step).start()
        exchange(SUBS + 2 * step)

        @pl.loop(0, width // BLOCK)
        def _(block):
            at = pl.ds(pl.multiple_of(block * BLOCK, BLOCK), BLOCK)
            total = project_back(whole(gate_grad), gate[at, :])
            total = total + project_back(whole(up_grad), up[at, :])
            put(back, at, total.astype(BF16))

        store(3, step).start()
        exchange(SUBS + 2 * step + 1)

    keep = pltpu.make_async_copy(dy, full_ref, loads.at[0])
    keep.start()

    @pl.loop(3 * SUBS, pieces + count - 1)
    def _(turn):
        exchange(turn)

    for which in (1, 2, 3):
        store(which, SUBS - 1).wait()
    keep.wait()
    scatter.finish()
    gather.finish(own_ref.at[gather.rows(0, 0)])


def hidden_layer(normed, own, middle, w_gate, w_up, w_down, count, collective_id, pieces=8):
    chunk_rows, width = own.shape
    hidden = w_gate.shape[1]
    rows = count * chunk_rows
    sub = chunk_rows // SUBS
    tall = jax.ShapeDtypeStruct((count, chunk_rows, hidden), BF16)
    hbm = pl.BlockSpec(memory_space=pl.ANY)
    outs = pl.pallas_call(
        functools.partial(hidden_kernel, count, pieces),
        out_shape=(
            jax.ShapeDtypeStruct((rows, width), BF16), tall, tall, tall,
            jax.ShapeDtypeStruct((count, chunk_rows, width), BF16),
            jax.ShapeDtypeStruct((chunk_rows, width), BF16),
        ),
        in_specs=[hbm, hbm] + vmem_specs(1) + [hbm, hbm, hbm],
        out_specs=(hbm, hbm, hbm, hbm, hbm, vmem_specs(1)[0]),
        scratch_shapes=[
            pltpu.VMEM((width, hidden), BF16),
            pltpu.VMEM((width, hidden), BF16),
            pltpu.VMEM((hidden, width), BF16),
            pltpu.VMEM((rows, width), BF16),
            pltpu.VMEM((rows, width), BF16),
            pltpu.VMEM((count, sub, hidden), BF16),
            pltpu.VMEM((SUBS, count, sub, hidden), BF16),
            pltpu.VMEM((SUBS, count, sub, hidden), BF16),
            pltpu.VMEM((count, sub, hidden), BF16),
            pltpu.VMEM((count, sub, width), BF16),
            pltpu.VMEM((rows, width), BF16),
            pltpu.VMEM((landing_rows(count, chunk_rows), width), BF16),
            copy_sems(count, pieces), copy_sems(count, pieces),
            copy_sems(count, SUBS), copy_sems(count, SUBS),
            pltpu.SemaphoreType.DMA((5,)), pltpu.SemaphoreType.DMA((4,)),
        ],
        compiler_params=params(collective_id=collective_id, has_side_effects=True),
        cost_estimate=pl.CostEstimate(
            flops=12 * rows * width * hidden, bytes_accessed=1 << 26, transcendentals=rows * hidden
        ),
        name="hidden_layer",
    )(normed, own, middle, w_gate, w_up, w_down)
    return [outs[0]] + [out.reshape(rows, out.shape[-1]) for out in outs[1:5]] + [outs[5]]


def backward_turn_kernel(
    count, pieces, given_ref, dy_ref, middle_ref, gain_ref,
    normed_full_ref, gate_grad_ref, up_grad_ref, active_ref, dy_full_ref,
    grad_ref, full_ref, gain_grad_ref, sums_ref, traded_ref,
    partial, landing, tiles, traded,
    rs_send, rs_receive, ag_send, ag_receive, load, trade_send, trade_receive, fetches, stores,
):
    line = Line(count)
    chunk_rows = dy_ref.shape[0]
    fetch = pltpu.make_async_copy(given_ref, partial, load)
    fetch.start()
    replica = lax.axis_index("dp")
    side = replica % 2
    partner = replica + 1 - 2 * side
    semaphore = pltpu.get_barrier_semaphore()
    pl.semaphore_signal(semaphore, 1, device_id={"dp": partner})
    pl.semaphore_wait(semaphore, line.greet(semaphore) + 1)
    fetch.wait()
    scatter = Scatter(line, partial, landing, rs_send, rs_receive, chunk_rows, pieces)
    gather = Gather(
        line, full_ref, ag_send, ag_receive, chunk_rows, pieces, settle_lags(count)
    )
    size = chunk_rows // pieces
    gain_grad_ref[...] = jnp.zeros_like(gain_grad_ref)

    def settle(piece):
        local = pl.ds(pl.multiple_of(piece * size, size), size)
        grad, gain_grad = norm_back(scatter.total(piece), middle_ref[local, :], gain_ref[...])
        grad = grad + dy_ref[local, :].astype(F32)
        gain_grad_ref[...] += gain_grad
        grad_ref[local, :] = grad
        full_ref[gather.rows(line.place, piece), :] = grad.astype(BF16)
        gather.start(piece)

    block = traded.shape[0]
    width = traded.shape[1]
    products = (
        (normed_full_ref, gate_grad_ref), (normed_full_ref, up_grad_ref), (active_ref, dy_full_ref),
    )
    halves = sums_ref.shape[0] // block
    pairs = halves * len(products)
    theirs = pl.ds(pl.multiple_of((1 - side) * block, block), block)
    ours = pl.ds(pl.multiple_of(side * block, block), block)

    def trade(pair):
        return pltpu.make_async_remote_copy(
            src_ref=tiles.at[pair % 2, theirs], dst_ref=traded_ref.at[pair],
            send_sem=trade_send.at[pair], recv_sem=trade_receive.at[pair],
            device_id={"dp": partner},
        )

    def bring(pair):
        return pltpu.make_async_copy(traded_ref.at[pair], traded, fetches)

    def put(pair):
        rows = pl.ds(pl.multiple_of((pair % halves) * block, block), block)
        columns = pl.ds(pl.multiple_of((pair // halves) * width, width), width)
        return pltpu.make_async_copy(
            tiles.at[pair % 2, ours], sums_ref.at[rows, columns], stores.at[pair % 2]
        )

    def beside(pair):
        @pl.when((pair >= 2) & (pair < pairs))
        def _():
            trade(pair - 2).wait_send()
            put(pair - 2).wait()

        @pl.when((pair >= 1) & (pair <= pairs))
        def _():
            trade(pair - 1).wait_recv()
            bring(pair - 1).start()

        at = pl.ds(pl.multiple_of((pair % halves) * 2 * block, 2 * block), 2 * block)
        for which, (left, right) in enumerate(products):
            @pl.when(pair // halves == which)
            def _(left=left, right=right):
                tiles[pair % 2] = row_contract(left[:, at], right[...]).astype(BF16)

        @pl.when(pair < pairs)
        def _():
            trade(pair).start()

        @pl.when((pair >= 1) & (pair <= pairs))
        def _():
            bring(pair - 1).wait()
            slot = (pair - 1) % 2
            kept = tiles[slot, ours].astype(F32) + traded[...].astype(F32)
            tiles[slot, ours] = kept.astype(BF16)
            put(pair - 1).start()

    turns = pieces + 2 * (count - 1)

    @pl.loop(0, max(turns, pairs + 1))
    def _(turn):
        scatter.turn(turn)
        gather.turn(turn)
        scatter.settle(turn, settle)
        beside(turn)

    for pair in range(pairs - 2, pairs):
        trade(pair).wait_send()
        put(pair).wait()
    scatter.finish()
    gather.finish()


def norm_back(grad, rows, gain):
    inverse = lax.rsqrt(jnp.mean(rows * rows, axis=-1, keepdims=True) + norm_epsilon)
    scaled = grad * gain
    common = jnp.mean(scaled * rows, axis=-1, keepdims=True) * (inverse * inverse * inverse)
    gain_grad = jnp.sum(grad * (rows * inverse), axis=0, keepdims=True)
    return inverse * scaled - rows * common, gain_grad


def backward_turn(
    given, dy, middle, gain, normed_full, gate_grad, up_grad, active, dy_full,
    count, replicas, collective_id, pieces=8,
):
    chunk_rows, width = dy.shape
    rows = count * chunk_rows
    block = width // replicas
    kept_rows = width // 2
    pairs = 3 * kept_rows // block
    hbm = pl.BlockSpec(memory_space=pl.ANY)
    return pl.pallas_call(
        functools.partial(backward_turn_kernel, count, pieces),
        out_shape=(
            jax.ShapeDtypeStruct((chunk_rows, width), F32),
            jax.ShapeDtypeStruct((rows, width), BF16),
            jax.ShapeDtypeStruct((1, width), F32),
            jax.ShapeDtypeStruct((kept_rows, 3 * width), BF16),
            jax.ShapeDtypeStruct((pairs, block, width), BF16),
        ),
        in_specs=[hbm] + vmem_specs(8),
        out_specs=tuple(vmem_specs(3)) + (hbm, hbm),
        scratch_shapes=[
            pltpu.VMEM((rows, width), BF16),
            pltpu.VMEM((landing_rows(count, chunk_rows), width), BF16),
            pltpu.VMEM((2, 2 * block, width), BF16),
            pltpu.VMEM((block, width), BF16),
        ]
        + [copy_sems(count, pieces)] * 4
        + [
            pltpu.SemaphoreType.DMA,
            pltpu.SemaphoreType.DMA((pairs,)),
            pltpu.SemaphoreType.DMA((pairs,)),
            pltpu.SemaphoreType.DMA,
            pltpu.SemaphoreType.DMA((2,)),
        ],
        compiler_params=params(collective_id=collective_id, has_side_effects=True),
        cost_estimate=pl.CostEstimate(
            flops=6 * rows * width * width, bytes_accessed=1 << 26, transcendentals=0
        ),
        name="backward_turn",
    )(given, dy, middle, gain, normed_full, gate_grad, up_grad, active, dy_full)


def last_turn_kernel(
    count, pieces, replicas, dqkv_ref, w_ref, normed_ref, middle_grad_ref, x_ref, gain_ref, gain_two_ref,
    grad_ref, weight_grad_ref, gains_ref,
    partial, landing, sums, traded, arrived, pair_sems, sends, receives,
    gain_own, gain_row, gain_land, gain_line,
    rs_send, rs_receive, dp_send, dp_receive, line_send, line_receive,
):
    line = Line(count)
    chunk_rows = x_ref.shape[0]
    width = dqkv_ref.shape[1]
    replica = lax.axis_index("dp")
    semaphore = pltpu.get_barrier_semaphore()
    for step in range(1, replicas):
        pl.semaphore_signal(semaphore, 1, device_id={"dp": (replica + step) % replicas})
    for step in range(1, count):
        pl.semaphore_signal(semaphore, 1, device_id={"tensor": (line.place + step) % count})
    pl.semaphore_wait(semaphore, replicas - 1 + count - 1)
    fold = Fold(replicas, sums, traded, arrived, pair_sems, sends, receives)

    @pl.loop(0, partial.shape[0] // SPAN)
    def _(step):
        rows = pl.ds(pl.multiple_of(step * SPAN, SPAN), SPAN)
        partial[rows, :] = project_back(dqkv_ref[rows, :], w_ref[:, :width]).astype(BF16)

    scatter = Scatter(line, partial, landing, rs_send, rs_receive, chunk_rows, pieces)
    size = chunk_rows // pieces
    gain_own[...] = jnp.zeros_like(gain_own)

    def settle(piece):
        local = pl.ds(pl.multiple_of(piece * size, size), size)
        total = scatter.total(piece)
        grad, gain_grad = norm_back(total, x_ref[local, :].astype(F32), gain_ref[...])
        gain_own[...] += gain_grad
        grad_ref[local, :] = (grad + middle_grad_ref[local, :]).astype(BF16)

    block = sums.shape[2]

    @pl.loop(0, pieces + count - 1)
    def _(turn):
        scatter.turn(turn)
        scatter.settle(turn, settle)

        @pl.when(turn == 0)
        def _():
            @pl.loop(0, replicas // 2)
            def _(half):
                at = pl.ds(pl.multiple_of(half * 2 * block, 2 * block), 2 * block)
                product = row_contract(normed_ref[:, at], dqkv_ref[...]).astype(BF16)
                for side in range(2):
                    sums[half, side] = product[side * block : (side + 1) * block]

            fold.pair().start()

        @pl.when(turn == 2)
        def _():
            fold.spread()

    gain_row[0:1, :] = gain_own[...]
    gain_row[1:2, :] = gain_two_ref[...]

    def share(peer, landing):
        return pltpu.make_async_remote_copy(
            src_ref=gain_row, dst_ref=gain_land.at[landing],
            send_sem=dp_send.at[peer], recv_sem=dp_receive.at[landing], device_id={"dp": peer},
        )

    def pass_line(peer, landing):
        return pltpu.make_async_remote_copy(
            src_ref=gains_ref, dst_ref=gain_line.at[landing],
            send_sem=line_send.at[peer], recv_sem=line_receive.at[landing],
            device_id={"tensor": peer},
        )

    peers = [(replica + step) % replicas for step in range(1, replicas)]
    places = [(line.place + step) % count for step in range(1, count)]
    for peer in peers:
        share(peer, replica).start()
    weight_grad_ref[...] = fold.total()
    total = gain_row[...]
    for peer in peers:
        share(peer, peer).wait_recv()
        total = total + gain_land[peer]
    gains_ref[...] = total
    for peer in places:
        pass_line(peer, line.place).start()
    scatter.finish()
    fold.finish()
    for peer in peers:
        share(peer, replica).wait_send()
    for peer in places:
        pass_line(peer, peer).wait_recv()
        total = total + gain_line[peer]
    for peer in places:
        pass_line(peer, line.place).wait_send()
    gains_ref[...] = total


def last_turn(
    dqkv, w_qkv, normed, middle_grad, x, gain, gain_two_grad, count, replicas, collective_id,
    pieces=8,
):
    chunk_rows, width = x.shape
    rows = count * chunk_rows
    block = width // replicas
    return pl.pallas_call(
        functools.partial(last_turn_kernel, count, pieces, replicas),
        out_shape=(
            jax.ShapeDtypeStruct((chunk_rows, width), BF16),
            jax.ShapeDtypeStruct((block, dqkv.shape[1]), F32),
            jax.ShapeDtypeStruct((2, width), F32),
        ),
        in_specs=vmem_specs(7),
        out_specs=tuple(vmem_specs(3)),
        scratch_shapes=[
            pltpu.VMEM((rows, width), BF16),
            pltpu.VMEM((landing_rows(count, chunk_rows), width), BF16),
        ]
        + fold_scratch(replicas, block, dqkv.shape[1])
        + [
            pltpu.VMEM((1, width), F32),
            pltpu.VMEM((2, width), F32),
            pltpu.VMEM((replicas, 2, width), F32),
            pltpu.VMEM((count, 2, width), F32),
        ]
        + [copy_sems(count, pieces)] * 2
        + [pltpu.SemaphoreType.DMA((replicas,))] * 2
        + [pltpu.SemaphoreType.DMA((count,))] * 2,
        compiler_params=params(collective_id=collective_id, has_side_effects=True),
        cost_estimate=pl.CostEstimate(
            flops=4 * rows * width * dqkv.shape[1],
            bytes_accessed=200 * chunk_rows * width, transcendentals=0,
        ),
        name="last_turn",
    )(dqkv, w_qkv, normed, middle_grad, x, gain, gain_two_grad)


def shards(
    inputs, cotangent, attn_gain, w_query, w_key, w_value, w_out, mlp_gain, w_gate, w_up, w_down,
    seq_lengths, group_perm, group_starts,
):
    count = lax.axis_size("tensor")
    group_rows = inputs.shape[0] * count
    q_width, kv_width = w_query.shape[1], w_key.shape[1]
    qkv_width = q_width + 2 * kv_width
    start, positions = group_layout(
        seq_lengths, group_perm, group_starts, lax.axis_index("dp"), group_rows, MOST_SEQS
    )
    cosine, sine = slab_tables(positions)

    gains = jnp.stack([attn_gain, mlp_gain], axis=1)
    gains = jnp.pad(gains, ((0, 0), (0, SLAB - 2)))
    packed = jnp.concatenate([w_query, w_key, w_value, gains], axis=1)
    qkv_full = lax.all_gather(packed, "dp", axis=0, tiled=True)
    out_full = lax.all_gather(w_out, "dp", axis=0, tiled=True)
    gate_full = lax.all_gather(w_gate, "dp", axis=0, tiled=True)
    up_full = lax.all_gather(w_up, "dp", axis=0, tiled=True)
    down_full = lax.all_gather(w_down, "dp", axis=0, tiled=True)
    gain_rows = jnp.transpose(qkv_full[:, qkv_width : qkv_width + 2].astype(F32))
    gain_one, gain_two = gain_rows[0:1], gain_rows[1:2]

    x_full = line_gather(inputs, count, 0)
    normed_full, queries, keys, values, mixed, lse = attend(
        x_full, qkv_full, gain_one, cosine, sine, start[:, None], q_width, kv_width
    )
    replicas = lax.axis_size("dp")
    middle, normed_two_full = forward_turn(mixed, out_full, inputs, gain_two, count, 1)
    grad_full, active, gate_grad, up_grad, norm_two_grad, outputs = hidden_layer(
        normed_two_full, cotangent, middle, gate_full, up_full, down_full, count, 4
    )
    middle_grad, branch_full, gain_two_grad, sums, _ = backward_turn(
        norm_two_grad, cotangent, middle, gain_two, normed_two_full, gate_grad, up_grad, active,
        grad_full, count, replicas, 2,
    )
    sides = [list(range(side, replicas, 2)) for side in range(2)]
    hidden_grads = lax.psum_scatter(
        sums, "dp", scatter_dimension=0, axis_index_groups=sides, tiled=True
    ).astype(F32)
    gate_weight_grad, up_weight_grad, down_grad = jnp.split(hidden_grads, 3, axis=1)
    dqkv, out_grad = attend_back(
        branch_full, out_full, mixed, queries, keys, values, lse, cosine, sine, start[None, :],
        replicas, 5,
    )
    input_grad, qkv_grad, gains_grad = last_turn(
        dqkv, qkv_full, normed_full, middle_grad, inputs, gain_one, gain_two_grad,
        count, replicas, 3,
    )
    own = attn_gain.shape[0]
    gains_grad = lax.dynamic_slice_in_dim(gains_grad, lax.axis_index("dp") * own, own, axis=1)
    return (
        outputs,
        input_grad,
        gains_grad[0],
        qkv_grad[:, :q_width],
        qkv_grad[:, q_width : q_width + kv_width],
        qkv_grad[:, q_width + kv_width :],
        out_grad,
        gains_grad[1],
        gate_weight_grad,
        up_weight_grad,
        down_grad,
    )


def solution(mesh):
    in_specs = (
        P(("dp", "tensor"), None),
        P(("dp", "tensor"), None),
        P("dp"),
        P("dp", "tensor"),
        P("dp", "tensor"),
        P("dp", "tensor"),
        P(("tensor", "dp"), None),
        P("dp"),
        P("dp", "tensor"),
        P("dp", "tensor"),
        P(("tensor", "dp"), None),
        P(),
        P(),
        P(),
    )
    out_specs = (
        P(("dp", "tensor"), None),
        P(("dp", "tensor"), None),
        P("dp"),
        P("dp", "tensor"),
        P("dp", "tensor"),
        P("dp", "tensor"),
        P(("tensor", "dp"), None),
        P("dp"),
        P("dp", "tensor"),
        P("dp", "tensor"),
        P(("tensor", "dp"), None),
    )
    return jax.shard_map(shards, mesh=mesh, in_specs=in_specs, out_specs=out_specs, check_vma=False)
```

```python
import functools
import math

import jax
import jax.numpy as jnp
from jax import lax
from jax.experimental import pallas as pl
from jax.experimental.pallas import tpu as pltpu
from jax.sharding import PartitionSpec as P

HEAD_SIZE = 64
MOST_SEQS = 2
SLAB = 128
SPAN = 256
GAIN_ROWS = 16

norm_epsilon = 1e-05
rope_theta = 500000.0
rope_factor = 32.0
low_factor = 1.0
high_factor = 4.0
context_span = 8192.0
mask_fill = -1e30

F32 = jnp.float32
BF16 = jnp.bfloat16
VMEM_LIMIT = 60 * 1024 * 1024


def rotary_freqs():
    half = HEAD_SIZE // 2
    index = jnp.tile(jnp.arange(half, dtype=jnp.float32), SLAB // half)
    inverse = 1.0 / jnp.power(jnp.float32(rope_theta), 2.0 * index / HEAD_SIZE)
    wavelength = 2.0 * math.pi / inverse
    smooth = (context_span / wavelength - low_factor) / (high_factor - low_factor)
    blended = (1.0 - smooth) * inverse / rope_factor + smooth * inverse
    scaled = jnp.where(wavelength > context_span / low_factor, inverse / rope_factor, blended)
    return jnp.where(wavelength < context_span / high_factor, inverse, scaled)


def segment_starts(lengths_ref, perm_ref, starts_ref, rows):
    group = lax.axis_index("dp")
    opening, closing = starts_ref[group], starts_ref[group + 1]
    finish = jnp.int32(0)
    start = jnp.zeros_like(rows)
    for slot in range(MOST_SEQS):
        place = opening + slot
        sequence = perm_ref[jnp.minimum(place, perm_ref.shape[0] - 1)]
        finish = finish + jnp.where(place < closing, lengths_ref[sequence], 0)
        start = jnp.where(rows >= finish, finish, start)
    return start


def project(left, right):
    return jnp.dot(left, right, preferred_element_type=F32)


def project_back(left, right):
    return lax.dot_general(left, right, (((1,), (1,)), ((), ())), preferred_element_type=F32)


def row_contract(left, right):
    return lax.dot_general(left, right, (((0,), (0,)), ((), ())), preferred_element_type=F32)


def lanes(shape):
    return lax.broadcasted_iota(jnp.int32, shape, len(shape) - 1)


def turned(slab):
    half = HEAD_SIZE // 2
    ahead = pltpu.roll(slab, SLAB - half, 1)
    behind = pltpu.roll(slab, half, 1)
    return jnp.where(lanes(slab.shape) % HEAD_SIZE < half, ahead, behind)


def head_pair(slab):
    left = lanes(slab.shape) < HEAD_SIZE
    zero = jnp.zeros_like(slab)
    return jnp.concatenate([jnp.where(left, slab, zero), jnp.where(left, zero, slab)], axis=0)


def join_pair(stacked):
    half = stacked.shape[0] // 2
    left = lanes((half, SLAB)) < HEAD_SIZE
    return jnp.where(left, stacked[:half], stacked[half:])


def params(**kwargs):
    return pltpu.CompilerParams(vmem_limit_bytes=VMEM_LIMIT, **kwargs)


def vmem_specs(count):
    return [pl.BlockSpec(memory_space=pltpu.VMEM)] * count


def weight_fetches(packed, target, sems):
    rows = target.shape[0] // packed.shape[0]
    return [
        pltpu.make_async_copy(
            packed.at[block, :rows], target.at[block * rows : (block + 1) * rows], sems.at[block]
        )
        for block in range(packed.shape[0])
    ]


def attend_kernel(
    x_ref, packed_ref, gain_ref, cos_ref, sin_ref, start_ref,
    normed_ref, q_ref, k_ref, v_ref, mixed_ref, lse_ref, bias_ref, stat_ref, w_ref, sems,
):
    fetches = weight_fetches(packed_ref, w_ref, sems)
    for fetch in fetches:
        fetch.start()
    for fetch in fetches:
        fetch.wait()
    rows_all = x_ref.shape[0]
    q_width = q_ref.shape[1]
    kv_slabs = v_ref.shape[0] // 2
    slabs = q_width // SLAB
    scale = HEAD_SIZE ** (-0.5)

    @pl.loop(0, rows_all // SPAN)
    def _(step):
        rows = pl.ds(step * SPAN, SPAN)
        x = x_ref[rows, :].astype(F32)
        inverse = lax.rsqrt(jnp.mean(x * x, axis=-1, keepdims=True) + norm_epsilon)
        normed = (x * inverse * gain_ref[...]).astype(BF16)
        normed_ref[rows, :] = normed
        pre = project(normed, w_ref[...])
        cosine, sine = cos_ref[rows, :], sin_ref[rows, :]
        for slab in range(slabs):
            part = pre[:, slab * SLAB : (slab + 1) * SLAB]
            part = (part * cosine + turned(part) * sine).astype(BF16)
            q_ref[rows, slab * SLAB : (slab + 1) * SLAB] = (part.astype(F32) * scale).astype(BF16)
        left = lanes((SPAN, SLAB)) < HEAD_SIZE
        for pair in range(kv_slabs):
            at = q_width + pair * SLAB
            key = pre[:, at : at + SLAB]
            key = key * cosine + turned(key) * sine
            at = at + kv_slabs * SLAB
            value = pre[:, at : at + SLAB]
            for ref, full in ((k_ref, key), (v_ref, value)):
                other = pltpu.roll(full, HEAD_SIZE, 1)
                ref[2 * pair, rows, :] = jnp.where(left, full, other).astype(BF16)
                ref[2 * pair + 1, rows, :] = jnp.where(left, other, full).astype(BF16)

    members = slabs // (2 * kv_slabs)
    for tile in range(rows_all // SPAN):
        first, span = tile * SPAN, (tile + 1) * SPAN
        columns = lanes((SPAN, span))
        row_ids = first + lax.broadcasted_iota(jnp.int32, (SPAN, span), 0)
        allowed = (columns >= start_ref[first : first + SPAN, :]) & (columns <= row_ids)
        bias_ref[:, :span] = jnp.where(allowed, 0.0, mask_fill)

        @pl.loop(0, slabs)
        def _(slab):
            at = pl.ds(pl.multiple_of(slab * SLAB, SLAB), SLAB)
            head = slab // members
            stacked = head_pair(q_ref[first : first + SPAN, at])
            scores = project_back(stacked, k_ref[head, :span, :])
            bias = bias_ref[:, :span]
            scores = scores + jnp.concatenate([bias, bias], axis=0)
            top = jnp.max(scores, axis=-1, keepdims=True)
            weights = jnp.exp(scores - top)
            total = jnp.sum(weights, axis=-1, keepdims=True)
            mixed = project(weights.astype(BF16), v_ref[head, :span, :]) / total
            mixed_ref[first : first + SPAN, at] = join_pair(mixed).astype(BF16)
            logs = top + jnp.log(total)
            old = stat_ref[first : first + SPAN, :]
            lane = lanes(old.shape)
            old = jnp.where(lane == 2 * slab, logs[:SPAN], old)
            stat_ref[first : first + SPAN, :] = jnp.where(lane == 2 * slab + 1, logs[SPAN:], old)

    lse_ref[...] = jnp.transpose(stat_ref[...])[: lse_ref.shape[0], :]


def attend(x_full, w_qkv, gain, cosine, sine, start, q_width, kv_width):
    rows = x_full.shape[0]
    heads = 2 * (kv_width // SLAB)
    flops = 2 * rows * x_full.shape[1] * (q_width + 2 * kv_width) + 8 * rows * rows * q_width
    return pl.pallas_call(
        attend_kernel,
        out_shape=(
            jax.ShapeDtypeStruct(x_full.shape, BF16),
            jax.ShapeDtypeStruct((rows, q_width), BF16),
            jax.ShapeDtypeStruct((heads, rows, SLAB), BF16),
            jax.ShapeDtypeStruct((heads, rows, SLAB), BF16),
            jax.ShapeDtypeStruct((rows, q_width), BF16),
            jax.ShapeDtypeStruct((q_width // HEAD_SIZE, rows), F32),
        ),
        in_specs=vmem_specs(1) + [pl.BlockSpec(memory_space=pl.ANY)] + vmem_specs(4),
        out_specs=tuple(vmem_specs(6)),
        scratch_shapes=[
            pltpu.VMEM((SPAN, rows), F32),
            pltpu.VMEM((rows, SLAB), F32),
            pltpu.VMEM((x_full.shape[1], w_qkv.shape[2]), BF16),
            pltpu.SemaphoreType.DMA((w_qkv.shape[0],)),
        ],
        compiler_params=params(),
        cost_estimate=pl.CostEstimate(flops=flops, bytes_accessed=1 << 24, transcendentals=1 << 23),
        name="attend",
    )(x_full, w_qkv, gain, cosine, sine, start)


SUBS = 4
BLOCK = 1024


class Line:
    def __init__(self, count):
        self.count = count
        self.place = lax.axis_index("tensor")
        self.has = (self.place < count - 1, self.place > 0)
        self.neighbour = (self.place + 1, self.place - 1)
        other = count - 1 - self.place
        self.lag = jnp.where(self.place > other, self.place, other)

    def greet(self, semaphore):
        for way in (0, 1):
            @pl.when(self.has[way])
            def _(way=way):
                pl.semaphore_signal(semaphore, 1, device_id={"tensor": self.neighbour[way]})
        ends = (self.place == 0) | (self.place == self.count - 1)
        return jnp.where(ends, 1, 2)

    def barrier(self):
        semaphore = pltpu.get_barrier_semaphore()
        pl.semaphore_wait(semaphore, self.greet(semaphore))

    def copy(self, source, target, send, receive, way):
        return pltpu.make_async_remote_copy(
            src_ref=source, dst_ref=target, send_sem=send, recv_sem=receive,
            device_id={"tensor": self.neighbour[way]},
        )


class Gather:
    def __init__(self, line, full, send, receive, chunk_rows, pieces, lags=None, stride=1):
        self.line, self.full, self.send, self.receive = line, full, send, receive
        self.chunk_rows, self.size, self.pieces = chunk_rows, chunk_rows // pieces, pieces
        self.lags, self.stride = lags or [0] * line.count, stride

    def rows(self, chunk, piece):
        start = chunk * self.chunk_rows + piece * self.size
        return pl.ds(pl.multiple_of(start, self.size), self.size)

    def copy(self, chunk, piece, way, source=None):
        target = self.full.at[self.rows(chunk, piece)]
        return self.line.copy(
            target if source is None else source, target,
            self.send.at[way, chunk, piece], self.receive.at[way, chunk, piece], way,
        )

    def start(self, piece, source=None):
        for way in (0, 1):
            @pl.when(self.line.has[way])
            def _(way=way):
                self.copy(self.line.place, piece, way, source).start()

    def turn(self, turn):
        line = self.line
        for chunk in range(line.count):
            for way in (0, 1):
                hop = line.place - chunk if way == 0 else chunk - line.place
                since = turn - self.lags[chunk] - hop
                piece = since // self.stride
                inside = (since >= 0) & (piece < self.pieces) & (since % self.stride == 0)

                @pl.when((hop > 0) & inside)
                def _(way=way, chunk=chunk, piece=piece):
                    self.copy(chunk, piece, way).wait_recv()

                    @pl.when(line.has[way])
                    def _():
                        self.copy(chunk, piece, way).start()

    def finish(self, source=None):
        line = self.line

        @pl.loop(0, self.pieces)
        def _(piece):
            for chunk in range(line.count):
                @pl.when(line.has[0] & (chunk <= line.place))
                def _(chunk=chunk):
                    self.copy(chunk, piece, 0, source).wait_send()

                @pl.when(line.has[1] & (chunk >= line.place))
                def _(chunk=chunk):
                    self.copy(chunk, piece, 1, source).wait_send()


class Scatter:
    def __init__(self, line, partial, landing, send, receive, chunk_rows, pieces):
        self.line, self.partial, self.landing = line, partial, landing
        self.send, self.receive = send, receive
        self.chunk_rows, self.size, self.pieces = chunk_rows, chunk_rows // pieces, pieces

    def rows(self, chunk, piece):
        start = chunk * self.chunk_rows + piece * self.size
        return pl.ds(pl.multiple_of(start, self.size), self.size)

    def landed(self, chunk, piece, way, owner):
        if way == 1:
            chunk = jnp.where(chunk == owner, self.line.count, chunk)
        return self.rows(chunk, piece)

    def copy(self, chunk, piece, way, owner=None):
        owner = self.line.neighbour[way] if owner is None else owner
        return self.line.copy(
            self.partial.at[self.rows(chunk, piece)],
            self.landing.at[self.landed(chunk, piece, way, owner)],
            self.send.at[way, chunk, piece], self.receive.at[way, chunk, piece], way,
        )

    def wait(self, chunk, piece, way):
        self.copy(chunk, piece, way, self.line.place).wait_recv()

    def forward(self, piece, way):
        line = self.line
        for step in range(line.count - 1):
            chunk = line.count - 1 - step if way == 0 else step
            beyond = chunk > line.place if way == 0 else chunk < line.place

            @pl.when(beyond)
            def _(chunk=chunk):
                @pl.when(line.has[1 - way])
                def _():
                    self.wait(chunk, piece, way)
                    rows = self.rows(chunk, piece)
                    total = self.partial[rows, :].astype(F32)
                    total = total + self.landing[rows, :].astype(F32)
                    self.partial[rows, :] = total.astype(BF16)

                self.copy(chunk, piece, way).start()

    def turn(self, turn):
        line = self.line
        for way, lag in ((0, line.place), (1, line.count - 1 - line.place)):
            piece = turn - lag

            @pl.when((piece >= 0) & (piece < self.pieces))
            def _(way=way, piece=piece):
                self.forward(piece, way)

    def settle(self, turn, use):
        piece = turn - self.line.lag

        @pl.when((piece >= 0) & (piece < self.pieces))
        def _():
            for way in (0, 1):
                @pl.when(self.line.has[1 - way])
                def _(way=way):
                    self.wait(self.line.place, piece, way)
            use(piece)

    def total(self, piece):
        place = self.line.place
        total = self.partial[self.rows(place, piece), :].astype(F32)
        for way in (0, 1):
            got = self.landing[self.landed(place, piece, way, place), :].astype(F32)
            total = total + jnp.where(self.line.has[1 - way], got, 0.0)
        return total

    def finish(self):
        line = self.line

        @pl.loop(0, self.pieces)
        def _(piece):
            for chunk in range(line.count):
                @pl.when(chunk > line.place)
                def _(chunk=chunk):
                    self.copy(chunk, piece, 0).wait_send()

                @pl.when(chunk < line.place)
                def _(chunk=chunk):
                    self.copy(chunk, piece, 1).wait_send()


class Fold:
    def __init__(self, replicas, sums, traded, arrived, pair_sems, sends, receives):
        self.halves = replicas // 2
        self.sums, self.traded, self.arrived = sums, traded, arrived
        self.pair_sems, self.sends, self.receives = pair_sems, sends, receives
        replica = lax.axis_index("dp")
        self.side, self.mine = replica % 2, replica // 2
        self.partner = replica + 1 - 2 * self.side

    def greet(self, semaphore):
        pl.semaphore_signal(semaphore, 1, device_id={"dp": self.partner})
        for step in range(1, self.halves):
            peer = 2 * ((self.mine + step) % self.halves) + self.side
            pl.semaphore_signal(semaphore, 1, device_id={"dp": peer})
        return self.halves

    def pair(self):
        return pltpu.make_async_remote_copy(
            src_ref=self.sums.at[:, 1 - self.side], dst_ref=self.traded,
            send_sem=self.pair_sems.at[0], recv_sem=self.pair_sems.at[1],
            device_id={"dp": self.partner},
        )

    def peer(self, half, landing):
        return pltpu.make_async_remote_copy(
            src_ref=self.sums.at[half, self.side], dst_ref=self.arrived.at[landing],
            send_sem=self.sends.at[half], recv_sem=self.receives.at[landing],
            device_id={"dp": 2 * half + self.side},
        )

    def others(self):
        return [(self.mine + step) % self.halves for step in range(1, self.halves)]

    def spread(self):
        self.pair().wait_recv()

        @pl.loop(0, self.halves)
        def _(half):
            total = self.sums[half, self.side].astype(F32) + self.traded[half].astype(F32)
            self.sums[half, self.side] = total.astype(BF16)

        for half in self.others():
            self.peer(half, self.mine).start()

    def total(self):
        total = self.sums[self.mine, self.side].astype(F32)
        for half in self.others():
            self.peer(half, half).wait_recv()
            total = total + self.arrived[half].astype(F32)
        return total

    def finish(self):
        self.pair().wait_send()
        for half in self.others():
            self.peer(half, self.mine).wait_send()


def fold_scratch(replicas, rows, width):
    halves = replicas // 2
    return [
        pltpu.VMEM((halves, 2, rows, width), BF16),
        pltpu.VMEM((halves, rows, width), BF16),
        pltpu.VMEM((halves, rows, width), BF16),
        pltpu.SemaphoreType.DMA((2,)),
        pltpu.SemaphoreType.DMA((halves,)),
        pltpu.SemaphoreType.DMA((halves,)),
    ]


def attend_back_kernel(
    replicas, branch_ref, w_ref, mixed_ref, q_ref, k_ref, v_ref, lse_ref, cos_ref, sin_ref,
    start_ref, dqkv_ref, weight_grad_ref, dmix_ref, bias_ref, dq_ref, dk_ref, dv_ref,
    sums, traded, arrived, pair_sems, sends, receives,
):
    fold = Fold(replicas, sums, traded, arrived, pair_sems, sends, receives)
    semaphore = pltpu.get_barrier_semaphore()
    pl.semaphore_wait(semaphore, fold.greet(semaphore))
    weight_rows = sums.shape[2]
    for step in range(mixed_ref.shape[1] // SLAB):
        first = step * SLAB
        product = row_contract(mixed_ref[:, first : first + SLAB], branch_ref[...]).astype(BF16)
        for row in range(0, SLAB, weight_rows):
            owner = (first + row) // weight_rows
            sums[owner // 2, owner % 2] = product[row : row + weight_rows]
    fold.pair().start()

    rows_all = branch_ref.shape[0]
    q_width = q_ref.shape[1]
    slabs = q_width // SLAB
    kv_heads = k_ref.shape[0]
    members = slabs // kv_heads
    scale = HEAD_SIZE ** (-0.5)

    @pl.loop(0, rows_all // SPAN)
    def _(step):
        rows = pl.ds(step * SPAN, SPAN)
        dmix_ref[rows, :] = project_back(branch_ref[rows, :], w_ref[...]).astype(BF16)

    fold.spread()
    dk_ref[...] = jnp.zeros_like(dk_ref)
    dv_ref[...] = jnp.zeros_like(dv_ref)
    for tile in range(rows_all // SPAN):
        first, span = tile * SPAN, (tile + 1) * SPAN
        key_ids = lax.broadcasted_iota(jnp.int32, (span, SPAN), 0)
        row_ids = first + lanes((span, SPAN))
        allowed = (key_ids >= start_ref[:, first : first + SPAN]) & (key_ids <= row_ids)
        bias_ref[:span, :] = jnp.where(allowed, 0.0, mask_fill)

        @pl.loop(0, slabs)
        def _(slab):
            at = pl.ds(pl.multiple_of(slab * SLAB, SLAB), SLAB)
            head = slab // members
            queries = head_pair(q_ref[first : first + SPAN, at])
            grads = head_pair(dmix_ref[first : first + SPAN, at])
            keys = k_ref[head, :span, :]
            scores = project_back(keys, queries)
            bias = bias_ref[:span, :]
            logs = jnp.concatenate(
                [
                    lse_ref[pl.ds(2 * slab, 1), first : first + SPAN],
                    lse_ref[pl.ds(2 * slab + 1, 1), first : first + SPAN],
                ],
                axis=1,
            )
            chances = jnp.exp(scores + jnp.concatenate([bias, bias], axis=1) - logs)
            chances_grad = project_back(v_ref[head, :span, :], grads)
            shared = jnp.sum(chances * chances_grad, axis=0, keepdims=True)
            score_grad = (chances * (chances_grad - shared)).astype(BF16)
            dv_ref[head, :span, :] += project(chances.astype(BF16), grads)
            dk_ref[head, :span, :] += project(score_grad, queries)
            dq_ref[first : first + SPAN, at] = join_pair(row_contract(score_grad, keys)) * scale

    left = lanes((SPAN, SLAB)) < HEAD_SIZE

    @pl.loop(0, rows_all // SPAN)
    def _(step):
        rows = pl.ds(step * SPAN, SPAN)
        cosine, sine = cos_ref[rows, :], sin_ref[rows, :]
        for slab in range(slabs):
            part = dq_ref[rows, slab * SLAB : (slab + 1) * SLAB]
            part = part * cosine - turned(part) * sine
            dqkv_ref[rows, slab * SLAB : (slab + 1) * SLAB] = part.astype(BF16)
        for pair in range(kv_heads // 2):
            joined = []
            for ref in (dk_ref, dv_ref):
                sums = []
                for head in (2 * pair, 2 * pair + 1):
                    full = ref[head, rows, :]
                    sums.append(full + pltpu.roll(full, HEAD_SIZE, 1))
                joined.append(jnp.where(left, sums[0], sums[1]))
            key, value = joined
            key = key * cosine - turned(key) * sine
            at = q_width + pair * SLAB
            dqkv_ref[rows, at : at + SLAB] = key.astype(BF16)
            at = at + (kv_heads // 2) * SLAB
            dqkv_ref[rows, at : at + SLAB] = value.astype(BF16)

    weight_grad_ref[...] = fold.total()
    fold.finish()


def attend_back(
    branch_full, w_out, mixed, queries, keys, values, lse, cosine, sine, start,
    replicas, collective_id,
):
    rows, q_width = queries.shape
    kv_heads = keys.shape[0]
    width = q_width + kv_heads * SLAB
    flops = 2 * rows * branch_full.shape[1] * q_width + 20 * rows * rows * q_width
    return pl.pallas_call(
        functools.partial(attend_back_kernel, replicas),
        out_shape=(
            jax.ShapeDtypeStruct((rows, width), BF16),
            jax.ShapeDtypeStruct((q_width // replicas, branch_full.shape[1]), F32),
        ),
        in_specs=vmem_specs(10),
        out_specs=tuple(vmem_specs(2)),
        scratch_shapes=[
            pltpu.VMEM((rows, q_width), BF16),
            pltpu.VMEM((rows, SPAN), F32),
            pltpu.VMEM((rows, q_width), F32),
            pltpu.VMEM((kv_heads, rows, SLAB), F32),
            pltpu.VMEM((kv_heads, rows, SLAB), F32),
        ]
        + fold_scratch(replicas, q_width // replicas, branch_full.shape[1]),
        compiler_params=params(collective_id=collective_id, has_side_effects=True),
        cost_estimate=pl.CostEstimate(flops=flops, bytes_accessed=1 << 24, transcendentals=1 << 23),
        name="attend_back",
    )(branch_full, w_out, mixed, queries, keys, values, lse, cosine, sine, start)


def landing_rows(count, chunk_rows):
    return (count + 1) * chunk_rows


def copy_sems(count, pieces):
    return pltpu.SemaphoreType.DMA((2, count, pieces))


def settle_lags(count):
    return [max(place, count - 1 - place) for place in range(count)]


def gather_kernel(
    count, pieces, x_ref, freqs_ref, lengths_ref, perm_ref, starts_ref,
    full_ref, cos_ref, sin_ref, column_ref, row_ref, send, receive, local,
):
    line = Line(count)
    chunk_rows = x_ref.shape[0]
    own = pl.ds(pl.multiple_of(line.place * chunk_rows, chunk_rows), chunk_rows)
    keep = pltpu.make_async_copy(x_ref, full_ref.at[own], local)
    keep.start()
    line.barrier()
    gather = Gather(line, full_ref, send, receive, chunk_rows, pieces)
    for piece in range(pieces):
        gather.start(piece, x_ref.at[gather.rows(0, piece)])
    row_ref[...] = segment_starts(lengths_ref, perm_ref, starts_ref, lanes(row_ref.shape))
    size = count * chunk_rows // pieces

    @pl.loop(1, pieces + count - 1)
    def _(turn):
        gather.turn(turn)

        @pl.when(turn <= pieces)
        def _():
            first = pl.multiple_of((turn - 1) * size, size)
            rows = first + lax.broadcasted_iota(jnp.int32, (size, SLAB), 0)
            start = segment_starts(lengths_ref, perm_ref, starts_ref, rows)
            angles = (rows - start).astype(F32) * freqs_ref[...]
            low_half = lanes(rows.shape) % HEAD_SIZE < HEAD_SIZE // 2
            sines = jnp.sin(angles)
            cos_ref[pl.ds(first, size), :] = jnp.cos(angles)
            sin_ref[pl.ds(first, size), :] = jnp.where(low_half, -sines, sines)
            column_ref[pl.ds(first, size), :] = start[:, 0:1]

    gather.finish(x_ref.at[gather.rows(0, 0)])
    keep.wait()


def line_gather(x, freqs, lengths, perm, starts, count, collective_id, pieces=8):
    rows, width = x.shape
    total = count * rows
    return pl.pallas_call(
        functools.partial(gather_kernel, count, pieces),
        out_shape=(
            jax.ShapeDtypeStruct((total, width), x.dtype),
            jax.ShapeDtypeStruct((total, SLAB), F32),
            jax.ShapeDtypeStruct((total, SLAB), F32),
            jax.ShapeDtypeStruct((total, 1), jnp.int32),
            jax.ShapeDtypeStruct((1, total), jnp.int32),
        ),
        in_specs=vmem_specs(2) + [pl.BlockSpec(memory_space=pltpu.SMEM)] * 3,
        out_specs=(pl.BlockSpec(memory_space=pl.ANY),) + tuple(vmem_specs(4)),
        scratch_shapes=[
            copy_sems(count, pieces), copy_sems(count, pieces), pltpu.SemaphoreType.DMA
        ],
        compiler_params=params(collective_id=collective_id, has_side_effects=True),
        cost_estimate=pl.CostEstimate(
            flops=0, bytes_accessed=200 * rows * width, transcendentals=0
        ),
        name="line_gather",
    )(x, freqs, lengths, perm, starts)


def forward_turn_kernel(
    count, pieces, mixed_ref, w_ref, x_ref, gain_ref, middle_ref, full_ref,
    partial, landing, rs_send, rs_receive, ag_send, ag_receive,
):
    line = Line(count)
    chunk_rows = x_ref.shape[0]
    line.barrier()

    @pl.loop(0, partial.shape[0] // SPAN)
    def _(step):
        rows = pl.ds(pl.multiple_of(step * SPAN, SPAN), SPAN)
        partial[rows, :] = project(mixed_ref[rows, :], w_ref[...]).astype(BF16)

    scatter = Scatter(line, partial, landing, rs_send, rs_receive, chunk_rows, pieces)
    gather = Gather(
        line, full_ref, ag_send, ag_receive, chunk_rows, pieces, settle_lags(count)
    )
    size = chunk_rows // pieces

    def settle(piece):
        local = pl.ds(pl.multiple_of(piece * size, size), size)
        middle = x_ref[local, :].astype(F32) + scatter.total(piece)
        middle_ref[local, :] = middle
        inverse = lax.rsqrt(jnp.mean(middle * middle, axis=-1, keepdims=True) + norm_epsilon)
        normed = (middle * inverse * gain_ref[...]).astype(BF16)
        full_ref[gather.rows(line.place, piece), :] = normed
        gather.start(piece)

    @pl.loop(0, pieces + 2 * (count - 1))
    def _(turn):
        scatter.turn(turn)
        gather.turn(turn)
        scatter.settle(turn, settle)

    scatter.finish()
    gather.finish()


def forward_turn(mixed, w_out, x, gain, count, collective_id, pieces=16):
    chunk_rows, width = x.shape
    rows = count * chunk_rows
    return pl.pallas_call(
        functools.partial(forward_turn_kernel, count, pieces),
        out_shape=(
            jax.ShapeDtypeStruct((chunk_rows, width), F32),
            jax.ShapeDtypeStruct((rows, width), BF16),
        ),
        in_specs=vmem_specs(4),
        out_specs=tuple(vmem_specs(2)),
        scratch_shapes=[
            pltpu.VMEM((rows, width), BF16),
            pltpu.VMEM((landing_rows(count, chunk_rows), width), BF16),
        ]
        + [copy_sems(count, pieces)] * 4,
        compiler_params=params(collective_id=collective_id, has_side_effects=True),
        cost_estimate=pl.CostEstimate(
            flops=2 * rows * width * mixed.shape[1],
            bytes_accessed=300 * chunk_rows * width, transcendentals=0,
        ),
        name="forward_turn",
    )(mixed, w_out, x, gain)


def hidden_kernel(
    count, pieces, normed_ref, own_ref, middle_ref, gate_ref, up_ref, down_ref,
    full_ref, active_ref, gate_grad_ref, up_grad_ref, back_ref, out_ref,
    gate, up, down, normed, dy, active, slope, value, up_grad, back,
    partial, landing, rs_send, rs_receive, ag_send, ag_receive, loads, stores,
):
    line = Line(count)
    chunk_rows = own_ref.shape[0]
    hidden = gate_ref.shape[1]
    width = gate_ref.shape[0]
    sub = chunk_rows // SUBS
    fetches = [
        pltpu.make_async_copy(source, target, loads.at[at])
        for at, (source, target) in enumerate(
            ((normed_ref, normed), (gate_ref, gate), (up_ref, up), (down_ref, down))
        )
    ]
    for fetch in fetches:
        fetch.start()
    line.barrier()
    gather = Gather(line, dy, ag_send, ag_receive, chunk_rows, SUBS)
    scatter = Scatter(line, partial, landing, rs_send, rs_receive, chunk_rows, pieces)
    for piece in range(SUBS):
        gather.start(piece, own_ref.at[gather.rows(0, piece)])
    own = pl.ds(pl.multiple_of(line.place * chunk_rows, chunk_rows), chunk_rows)
    place_own = pltpu.make_async_copy(own_ref, dy.at[own], loads.at[4])
    place_own.start()
    gate_grad = active
    outs = ((active, active_ref), (gate_grad, gate_grad_ref), (up_grad, up_grad_ref),
            (back, back_ref))

    def store(which, step):
        source, target = outs[which]
        rows = pl.ds(pl.multiple_of(step * sub, sub), sub)
        return pltpu.make_async_copy(source, target.at[:, rows], stores.at[which])

    def rows_of(chunk, step):
        return pl.ds(pl.multiple_of(chunk * chunk_rows + step * sub, sub), sub)

    def picked(ref, step, at=slice(None)):
        return jnp.concatenate([ref[rows_of(chunk, step), at] for chunk in range(count)], axis=0)

    def put(ref, at, rows):
        for chunk in range(count):
            ref[chunk, :, at] = rows[chunk * sub : (chunk + 1) * sub]

    def whole(ref):
        return jnp.concatenate([ref[chunk] for chunk in range(count)], axis=0)

    def settle(piece):
        size = chunk_rows // pieces
        local = pl.ds(pl.multiple_of(piece * size, size), size)
        out_ref[local, :] = (middle_ref[local, :] + scatter.total(piece)).astype(BF16)

    def exchange(turn):
        scatter.turn(turn)
        gather.turn(turn)
        scatter.settle(turn, settle)

    for at in range(3):
        fetches[at].wait()

    @pl.loop(0, SUBS)
    def _(step):
        @pl.when(step > 0)
        def _():
            store(0, step - 1).wait()

        @pl.loop(0, hidden // BLOCK)
        def _(block):
            at = pl.ds(pl.multiple_of(block * BLOCK, BLOCK), BLOCK)
            source = picked(normed, step)
            gate_pre = project(source, gate[:, at])
            up_pre = project(source, up[:, at])
            chance = 1.0 / (1.0 + jnp.exp(-gate_pre))
            silu = gate_pre * chance
            put(active, at, (silu * up_pre).astype(BF16))
            put(value.at[step], at, silu.astype(BF16))
            raised = up_pre * chance * (1.0 + gate_pre * (1.0 - chance))
            put(slope.at[step], at, raised.astype(BF16))

        store(0, step).start()

        @pl.when(step == 0)
        def _():
            fetches[3].wait()

        @pl.loop(0, width // BLOCK)
        def _(block):
            at = pl.ds(pl.multiple_of(block * BLOCK, BLOCK), BLOCK)
            product = project(whole(active), down[:, at]).astype(BF16)
            for chunk in range(count):
                partial[rows_of(chunk, step), at] = product[chunk * sub : (chunk + 1) * sub]

        exchange(step)

    @pl.loop(0, SUBS)
    def _(step):
        @pl.when(step == 0)
        def _():
            store(0, SUBS - 1).wait()
            place_own.wait()

        @pl.when(step > 0)
        def _():
            for which in (1, 2, 3):
                store(which, step - 1).wait()

        @pl.loop(0, hidden // BLOCK)
        def _(block):
            at = pl.ds(pl.multiple_of(block * BLOCK, BLOCK), BLOCK)
            active_grad = project_back(picked(dy, step), down[at, :])
            for chunk in range(count):
                grad = active_grad[chunk * sub : (chunk + 1) * sub]
                here = (grad * slope[step, chunk, :, at].astype(F32)).astype(BF16)
                gate_grad[chunk, :, at] = here
                here = (grad * value[step, chunk, :, at].astype(F32)).astype(BF16)
                up_grad[chunk, :, at] = here

        for which in (1, 2):
            store(which, step).start()
        exchange(SUBS + 2 * step)

        @pl.loop(0, width // BLOCK)
        def _(block):
            at = pl.ds(pl.multiple_of(block * BLOCK, BLOCK), BLOCK)
            total = project_back(whole(gate_grad), gate[at, :])
            total = total + project_back(whole(up_grad), up[at, :])
            put(back, at, total.astype(BF16))

        store(3, step).start()
        exchange(SUBS + 2 * step + 1)

    keep = pltpu.make_async_copy(dy, full_ref, loads.at[0])
    keep.start()

    @pl.loop(3 * SUBS, pieces + count - 1)
    def _(turn):
        exchange(turn)

    for which in (1, 2, 3):
        store(which, SUBS - 1).wait()
    keep.wait()
    scatter.finish()
    gather.finish(own_ref.at[gather.rows(0, 0)])


def hidden_layer(normed, own, middle, w_gate, w_up, w_down, count, collective_id, pieces=8):
    chunk_rows, width = own.shape
    hidden = w_gate.shape[1]
    rows = count * chunk_rows
    sub = chunk_rows // SUBS
    tall = jax.ShapeDtypeStruct((count, chunk_rows, hidden), BF16)
    hbm = pl.BlockSpec(memory_space=pl.ANY)
    outs = pl.pallas_call(
        functools.partial(hidden_kernel, count, pieces),
        out_shape=(
            jax.ShapeDtypeStruct((rows, width), BF16), tall, tall, tall,
            jax.ShapeDtypeStruct((count, chunk_rows, width), BF16),
            jax.ShapeDtypeStruct((chunk_rows, width), BF16),
        ),
        in_specs=[hbm, hbm] + vmem_specs(1) + [hbm, hbm, hbm],
        out_specs=(hbm, hbm, hbm, hbm, hbm, vmem_specs(1)[0]),
        scratch_shapes=[
            pltpu.VMEM((width, hidden), BF16),
            pltpu.VMEM((width, hidden), BF16),
            pltpu.VMEM((hidden, width), BF16),
            pltpu.VMEM((rows, width), BF16),
            pltpu.VMEM((rows, width), BF16),
            pltpu.VMEM((count, sub, hidden), BF16),
            pltpu.VMEM((SUBS, count, sub, hidden), BF16),
            pltpu.VMEM((SUBS, count, sub, hidden), BF16),
            pltpu.VMEM((count, sub, hidden), BF16),
            pltpu.VMEM((count, sub, width), BF16),
            pltpu.VMEM((rows, width), BF16),
            pltpu.VMEM((landing_rows(count, chunk_rows), width), BF16),
            copy_sems(count, pieces), copy_sems(count, pieces),
            copy_sems(count, SUBS), copy_sems(count, SUBS),
            pltpu.SemaphoreType.DMA((5,)), pltpu.SemaphoreType.DMA((4,)),
        ],
        compiler_params=params(collective_id=collective_id, has_side_effects=True),
        cost_estimate=pl.CostEstimate(
            flops=12 * rows * width * hidden, bytes_accessed=1 << 26, transcendentals=rows * hidden
        ),
        name="hidden_layer",
    )(normed, own, middle, w_gate, w_up, w_down)
    return [outs[0]] + [out.reshape(rows, out.shape[-1]) for out in outs[1:5]] + [outs[5]]


def backward_turn_kernel(
    count, pieces, given_ref, dy_ref, middle_ref, gain_ref,
    normed_full_ref, gate_grad_ref, up_grad_ref, active_ref, dy_full_ref,
    grad_ref, full_ref, gain_grad_ref, sums_ref, down_grad_ref, traded_ref,
    partial, landing, tiles, traded, normed, gate_grad, active, dy_full, kept, arrived,
    rs_send, rs_receive, ag_send, ag_receive, load, trade_send, trade_receive, fetches, stores,
    peer_send, peer_receive, operands,
):
    line = Line(count)
    chunk_rows = dy_ref.shape[0]
    fetch = pltpu.make_async_copy(given_ref, partial, load)
    fetch.start()
    brought = [
        pltpu.make_async_copy(source, target, operands.at[at])
        for at, (source, target) in enumerate((
            (active_ref, active), (dy_full_ref, dy_full), (normed_full_ref, normed),
            (gate_grad_ref, gate_grad), (up_grad_ref, active),
        ))
    ]
    for copy in brought[:4]:
        copy.start()
    replica = lax.axis_index("dp")
    side, mine = replica % 2, replica // 2
    partner = replica + 1 - 2 * side
    halves = kept.shape[0]
    others = [(mine + step) % halves for step in range(1, halves)]
    semaphore = pltpu.get_barrier_semaphore()
    pl.semaphore_signal(semaphore, 1, device_id={"dp": partner})
    for half in others:
        pl.semaphore_signal(semaphore, 1, device_id={"dp": 2 * half + side})
    pl.semaphore_wait(semaphore, line.greet(semaphore) + halves)
    fetch.wait()
    scatter = Scatter(line, partial, landing, rs_send, rs_receive, chunk_rows, pieces)
    gather = Gather(
        line, full_ref, ag_send, ag_receive, chunk_rows, pieces, settle_lags(count)
    )
    size = chunk_rows // pieces
    gain_grad_ref[...] = jnp.zeros_like(gain_grad_ref)

    def settle(piece):
        local = pl.ds(pl.multiple_of(piece * size, size), size)
        grad, gain_grad = norm_back(scatter.total(piece), middle_ref[local, :], gain_ref[...])
        grad = grad + dy_ref[local, :].astype(F32)
        gain_grad_ref[...] += gain_grad
        grad_ref[local, :] = grad
        full_ref[gather.rows(line.place, piece), :] = grad.astype(BF16)
        gather.start(piece)

    block = traded.shape[0]
    width = traded.shape[1]
    products = ((active, dy_full), (normed, gate_grad), (normed, active))
    needed = ((0, 1), (2, 3), (4,))
    pairs = halves * len(products)
    theirs = pl.ds(pl.multiple_of((1 - side) * block, block), block)
    ours = pl.ds(pl.multiple_of(side * block, block), block)

    def trade(pair):
        return pltpu.make_async_remote_copy(
            src_ref=tiles.at[pair % 2, theirs], dst_ref=traded_ref.at[pair],
            send_sem=trade_send.at[pair], recv_sem=trade_receive.at[pair],
            device_id={"dp": partner},
        )

    def bring(pair):
        return pltpu.make_async_copy(traded_ref.at[pair], traded, fetches)

    def put(pair):
        rows = pl.ds(pl.multiple_of((pair % halves) * block, block), block)
        columns = pl.ds(pl.multiple_of((pair // halves - 1) * width, width), width)
        return pltpu.make_async_copy(
            tiles.at[pair % 2, ours], sums_ref.at[rows, columns], stores.at[pair % 2]
        )

    def peer(half, place):
        return pltpu.make_async_remote_copy(
            src_ref=kept.at[half], dst_ref=arrived.at[place],
            send_sem=peer_send.at[half], recv_sem=peer_receive.at[place],
            device_id={"dp": 2 * half + side},
        )

    def beside(pair):
        @pl.when((pair >= 2) & (pair < pairs))
        def _():
            trade(pair - 2).wait_send()

            @pl.when(pair - 2 >= halves)
            def _():
                put(pair - 2).wait()

        @pl.when((pair >= 1) & (pair <= pairs))
        def _():
            trade(pair - 1).wait_recv()
            bring(pair - 1).start()

        at = pl.ds(pl.multiple_of((pair % halves) * 2 * block, 2 * block), 2 * block)
        for which, (left, right) in enumerate(products):
            @pl.when(pair == which * halves)
            def _(which=which):
                for operand in needed[which]:
                    brought[operand].wait()
                if which == 1:
                    brought[4].start()

            @pl.when(pair // halves == which)
            def _(left=left, right=right):
                tiles[pair % 2] = row_contract(left[:, at], right[...]).astype(BF16)

        @pl.when(pair < pairs)
        def _():
            trade(pair).start()

        @pl.when((pair >= 1) & (pair <= pairs))
        def _():
            last = pair - 1
            bring(last).wait()
            slot = last % 2
            total = tiles[slot, ours].astype(F32) + traded[...].astype(F32)

            @pl.when(last < halves)
            def _():
                kept[last % halves] = total.astype(BF16)

                @pl.when(last != mine)
                def _():
                    peer(last, mine).start()

            @pl.when(last >= halves)
            def _():
                tiles[slot, ours] = total.astype(BF16)
                put(last).start()

    turns = pieces + 2 * (count - 1)

    @pl.loop(0, max(turns, pairs + 1))
    def _(turn):
        scatter.turn(turn)
        gather.turn(turn)
        scatter.settle(turn, settle)
        beside(turn)

    for pair in range(pairs - 2, pairs):
        trade(pair).wait_send()
        put(pair).wait()
    total = kept[mine].astype(F32)
    for half in others:
        peer(half, half).wait_recv()
        total = total + arrived[half].astype(F32)
    down_grad_ref[...] = total
    for half in others:
        peer(half, mine).wait_send()
    scatter.finish()
    gather.finish()


def norm_back(grad, rows, gain):
    inverse = lax.rsqrt(jnp.mean(rows * rows, axis=-1, keepdims=True) + norm_epsilon)
    scaled = grad * gain
    common = jnp.mean(scaled * rows, axis=-1, keepdims=True) * (inverse * inverse * inverse)
    gain_grad = jnp.sum(grad * (rows * inverse), axis=0, keepdims=True)
    return inverse * scaled - rows * common, gain_grad


def backward_turn(
    given, dy, middle, gain, normed_full, gate_grad, up_grad, active, dy_full,
    count, replicas, collective_id, pieces=16,
):
    chunk_rows, width = dy.shape
    rows = count * chunk_rows
    block = width // replicas
    kept_rows = width // 2
    pairs = 3 * kept_rows // block
    hbm = pl.BlockSpec(memory_space=pl.ANY)
    return pl.pallas_call(
        functools.partial(backward_turn_kernel, count, pieces),
        out_shape=(
            jax.ShapeDtypeStruct((chunk_rows, width), F32),
            jax.ShapeDtypeStruct((rows, width), BF16),
            jax.ShapeDtypeStruct((1, width), F32),
            jax.ShapeDtypeStruct((kept_rows, 2 * width), BF16),
            jax.ShapeDtypeStruct((block, width), F32),
            jax.ShapeDtypeStruct((pairs, block, width), BF16),
        ),
        in_specs=[hbm] + vmem_specs(3) + [hbm] * 5,
        out_specs=tuple(vmem_specs(3)) + (hbm, vmem_specs(1)[0], hbm),
        scratch_shapes=[
            pltpu.VMEM((rows, width), BF16),
            pltpu.VMEM((landing_rows(count, chunk_rows), width), BF16),
            pltpu.VMEM((2, 2 * block, width), BF16),
            pltpu.VMEM((block, width), BF16),
        ]
        + [pltpu.VMEM((rows, width), BF16)] * 4
        + [pltpu.VMEM((replicas // 2, block, width), BF16)] * 2
        + [copy_sems(count, pieces)] * 4
        + [
            pltpu.SemaphoreType.DMA,
            pltpu.SemaphoreType.DMA((pairs,)),
            pltpu.SemaphoreType.DMA((pairs,)),
            pltpu.SemaphoreType.DMA,
            pltpu.SemaphoreType.DMA((2,)),
            pltpu.SemaphoreType.DMA((replicas // 2,)),
            pltpu.SemaphoreType.DMA((replicas // 2,)),
            pltpu.SemaphoreType.DMA((5,)),
        ],
        compiler_params=params(collective_id=collective_id, has_side_effects=True),
        cost_estimate=pl.CostEstimate(
            flops=6 * rows * width * width, bytes_accessed=1 << 26, transcendentals=0
        ),
        name="backward_turn",
    )(given, dy, middle, gain, normed_full, gate_grad, up_grad, active, dy_full)


def last_turn_kernel(
    count, pieces, replicas, dqkv_ref, packed_ref, normed_ref, middle_grad_ref, x_ref, gain_ref,
    gain_two_ref, grad_ref, query_grad_ref, key_grad_ref, value_grad_ref, gain_one_out, gain_two_out,
    w_ref, sems,
    partial, landing, sums, traded, arrived, pair_sems, sends, receives,
    gain_own, gain_row, gain_land, gains_ref, gain_line,
    rs_send, rs_receive, dp_send, dp_receive, line_send, line_receive,
):
    line = Line(count)
    chunk_rows = x_ref.shape[0]
    fetches = weight_fetches(packed_ref, w_ref, sems)
    for fetch in fetches:
        fetch.start()
    replica = lax.axis_index("dp")
    semaphore = pltpu.get_barrier_semaphore()
    for step in range(1, replicas):
        pl.semaphore_signal(semaphore, 1, device_id={"dp": (replica + step) % replicas})
    for step in range(1, count):
        pl.semaphore_signal(semaphore, 1, device_id={"tensor": (line.place + step) % count})
    pl.semaphore_wait(semaphore, replicas - 1 + count - 1)
    fold = Fold(replicas, sums, traded, arrived, pair_sems, sends, receives)
    for fetch in fetches:
        fetch.wait()

    @pl.loop(0, partial.shape[0] // SPAN)
    def _(step):
        rows = pl.ds(pl.multiple_of(step * SPAN, SPAN), SPAN)
        partial[rows, :] = project_back(dqkv_ref[rows, :], w_ref[...]).astype(BF16)

    scatter = Scatter(line, partial, landing, rs_send, rs_receive, chunk_rows, pieces)
    size = chunk_rows // pieces
    gain_own[...] = jnp.zeros_like(gain_own)

    def settle(piece):
        local = pl.ds(pl.multiple_of(piece * size, size), size)
        total = scatter.total(piece)
        grad, gain_grad = norm_back(total, x_ref[local, :].astype(F32), gain_ref[...])
        gain_own[...] += gain_grad
        grad_ref[local, :] = (grad + middle_grad_ref[local, :]).astype(BF16)

    block = sums.shape[2]

    @pl.loop(0, pieces + count - 1)
    def _(turn):
        scatter.turn(turn)
        scatter.settle(turn, settle)

        @pl.when(turn == 0)
        def _():
            @pl.loop(0, replicas // 2)
            def _(half):
                at = pl.ds(pl.multiple_of(half * 2 * block, 2 * block), 2 * block)
                product = row_contract(normed_ref[:, at], dqkv_ref[...]).astype(BF16)
                for side in range(2):
                    sums[half, side] = product[side * block : (side + 1) * block]

            fold.pair().start()

        @pl.when(turn == 2)
        def _():
            fold.spread()

    gain_row[0:1, :] = gain_own[...]
    gain_row[1:2, :] = gain_two_ref[...]

    def share(peer, landing):
        return pltpu.make_async_remote_copy(
            src_ref=gain_row, dst_ref=gain_land.at[landing],
            send_sem=dp_send.at[peer], recv_sem=dp_receive.at[landing], device_id={"dp": peer},
        )

    def pass_line(peer, landing):
        return pltpu.make_async_remote_copy(
            src_ref=gains_ref, dst_ref=gain_line.at[landing],
            send_sem=line_send.at[peer], recv_sem=line_receive.at[landing],
            device_id={"tensor": peer},
        )

    peers = [(replica + step) % replicas for step in range(1, replicas)]
    places = [(line.place + step) % count for step in range(1, count)]
    for peer in peers:
        share(peer, replica).start()
    total = fold.total()
    at = 0
    for ref in (query_grad_ref, key_grad_ref, value_grad_ref):
        ref[...] = total[:, at : at + ref.shape[1]]
        at += ref.shape[1]
    total = gain_row[...]
    for peer in peers:
        share(peer, peer).wait_recv()
        total = total + gain_land[peer]
    gains_ref[...] = total
    for peer in places:
        pass_line(peer, line.place).start()
    scatter.finish()
    fold.finish()
    for peer in peers:
        share(peer, replica).wait_send()
    for peer in places:
        pass_line(peer, peer).wait_recv()
        total = total + gain_line[peer]
    for peer in places:
        pass_line(peer, line.place).wait_send()
    own = gain_one_out.shape[1]
    kept = jnp.zeros((2, own), F32)
    for owner in range(replicas):
        part = total[:, owner * own : (owner + 1) * own]
        kept = kept + jnp.where(replica == owner, part, 0.0)
    gain_one_out[...] = kept[0:1]
    gain_two_out[...] = kept[1:2]


def last_turn(
    dqkv, w_qkv, normed, middle_grad, x, gain, gain_two_grad, widths, count, replicas,
    collective_id, pieces=8,
):
    chunk_rows, width = x.shape
    rows = count * chunk_rows
    block = width // replicas
    return pl.pallas_call(
        functools.partial(last_turn_kernel, count, pieces, replicas),
        out_shape=(
            jax.ShapeDtypeStruct((chunk_rows, width), BF16),
        )
        + tuple(jax.ShapeDtypeStruct((block, part), F32) for part in widths)
        + (jax.ShapeDtypeStruct((1, block), F32),) * 2,
        in_specs=vmem_specs(1) + [pl.BlockSpec(memory_space=pl.ANY)] + vmem_specs(5),
        out_specs=tuple(vmem_specs(6)),
        scratch_shapes=[
            pltpu.VMEM((width, dqkv.shape[1]), BF16),
            pltpu.SemaphoreType.DMA((replicas,)),
            pltpu.VMEM((rows, width), BF16),
            pltpu.VMEM((landing_rows(count, chunk_rows), width), BF16),
        ]
        + fold_scratch(replicas, block, dqkv.shape[1])
        + [
            pltpu.VMEM((1, width), F32),
            pltpu.VMEM((2, width), F32),
            pltpu.VMEM((replicas, 2, width), F32),
            pltpu.VMEM((2, width), F32),
            pltpu.VMEM((count, 2, width), F32),
        ]
        + [copy_sems(count, pieces)] * 2
        + [pltpu.SemaphoreType.DMA((replicas,))] * 2
        + [pltpu.SemaphoreType.DMA((count,))] * 2,
        compiler_params=params(collective_id=collective_id, has_side_effects=True),
        cost_estimate=pl.CostEstimate(
            flops=4 * rows * width * dqkv.shape[1],
            bytes_accessed=200 * chunk_rows * width, transcendentals=0,
        ),
        name="last_turn",
    )(dqkv, w_qkv, normed, middle_grad, x, gain, gain_two_grad)


def shards(
    inputs, cotangent, attn_gain, w_query, w_key, w_value, w_out, mlp_gain, w_gate, w_up, w_down,
    seq_lengths, group_perm, group_starts,
):
    count = lax.axis_size("tensor")
    q_width, kv_width = w_query.shape[1], w_key.shape[1]
    qkv_width = q_width + 2 * kv_width
    own = attn_gain.shape[0]
    gains = jnp.concatenate([attn_gain, mlp_gain])[None]
    gains = jnp.pad(gains, ((0, GAIN_ROWS - 1), (0, qkv_width - 2 * own)))
    packed = jnp.concatenate([w_query, w_key, w_value], axis=1)
    packed = jnp.concatenate([packed, gains], axis=0)
    qkv_full = lax.all_gather(packed[None], "dp", axis=0, tiled=True)
    out_full = lax.all_gather(w_out, "dp", axis=0, tiled=True)
    gate_full = lax.all_gather(w_gate, "dp", axis=0, tiled=True)
    up_full = lax.all_gather(w_up, "dp", axis=0, tiled=True)
    down_full = lax.all_gather(w_down, "dp", axis=0, tiled=True)
    gain_rows = qkv_full[:, own, : 2 * own].reshape(-1, 2, own).astype(F32)
    gain_rows = jnp.transpose(gain_rows, (1, 0, 2)).reshape(2, -1)
    gain_one, gain_two = gain_rows[0:1], gain_rows[1:2]

    x_full, cosine, sine, start_column, start_row = line_gather(
        inputs, rotary_freqs()[None], seq_lengths, group_perm, group_starts, count, 0
    )
    normed_full, queries, keys, values, mixed, lse = attend(
        x_full, qkv_full, gain_one, cosine, sine, start_column, q_width, kv_width
    )
    replicas = lax.axis_size("dp")
    middle, normed_two_full = forward_turn(mixed, out_full, inputs, gain_two, count, 1)
    grad_full, active, gate_grad, up_grad, norm_two_grad, outputs = hidden_layer(
        normed_two_full, cotangent, middle, gate_full, up_full, down_full, count, 4
    )
    middle_grad, branch_full, gain_two_grad, sums, down_grad, _ = backward_turn(
        norm_two_grad, cotangent, middle, gain_two, normed_two_full, gate_grad, up_grad, active,
        grad_full, count, replicas, 2,
    )
    sides = [list(range(side, replicas, 2)) for side in range(2)]
    hidden_grads = lax.psum_scatter(
        sums, "dp", scatter_dimension=0, axis_index_groups=sides, tiled=True
    ).astype(F32)
    gate_weight_grad, up_weight_grad = jnp.split(hidden_grads, 2, axis=1)
    dqkv, out_grad = attend_back(
        branch_full, out_full, mixed, queries, keys, values, lse, cosine, sine, start_row,
        replicas, 5,
    )
    input_grad, query_grad, key_grad, value_grad, gain_one_grad, gain_two_grad = last_turn(
        dqkv, qkv_full, normed_full, middle_grad, inputs, gain_one, gain_two_grad,
        (q_width, kv_width, kv_width), count, replicas, 3,
    )
    return (
        outputs,
        input_grad,
        gain_one_grad[0],
        query_grad,
        key_grad,
        value_grad,
        out_grad,
        gain_two_grad[0],
        gate_weight_grad,
        up_weight_grad,
        down_grad,
    )


def solution(mesh):
    in_specs = (
        P(("dp", "tensor"), None),
        P(("dp", "tensor"), None),
        P("dp"),
        P("dp", "tensor"),
        P("dp", "tensor"),
        P("dp", "tensor"),
        P(("tensor", "dp"), None),
        P("dp"),
        P("dp", "tensor"),
        P("dp", "tensor"),
        P(("tensor", "dp"), None),
        P(),
        P(),
        P(),
    )
    out_specs = (
        P(("dp", "tensor"), None),
        P(("dp", "tensor"), None),
        P("dp"),
        P("dp", "tensor"),
        P("dp", "tensor"),
        P("dp", "tensor"),
        P(("tensor", "dp"), None),
        P("dp"),
        P("dp", "tensor"),
        P("dp", "tensor"),
        P(("tensor", "dp"), None),
    )
    return jax.shard_map(shards, mesh=mesh, in_specs=in_specs, out_specs=out_specs, check_vma=False)
```

```python
import functools
import math

import jax
import jax.numpy as jnp
from jax import lax
from jax.experimental import pallas as pl
from jax.experimental.pallas import tpu as pltpu
from jax.sharding import PartitionSpec as P

HEAD_SIZE = 64
MOST_SEQS = 2
SLAB = 128
SPAN = 256
GAIN_ROWS = 16

norm_epsilon = 1e-05
rope_theta = 500000.0
rope_factor = 32.0
low_factor = 1.0
high_factor = 4.0
context_span = 8192.0
mask_fill = -1e30

F32 = jnp.float32
BF16 = jnp.bfloat16
VMEM_LIMIT = 60 * 1024 * 1024


def rotary_freqs():
    half = HEAD_SIZE // 2
    index = jnp.tile(jnp.arange(half, dtype=jnp.float32), SLAB // half)
    inverse = 1.0 / jnp.power(jnp.float32(rope_theta), 2.0 * index / HEAD_SIZE)
    wavelength = 2.0 * math.pi / inverse
    smooth = (context_span / wavelength - low_factor) / (high_factor - low_factor)
    blended = (1.0 - smooth) * inverse / rope_factor + smooth * inverse
    scaled = jnp.where(wavelength > context_span / low_factor, inverse / rope_factor, blended)
    return jnp.where(wavelength < context_span / high_factor, inverse, scaled)


def segment_starts(lengths_ref, perm_ref, starts_ref, rows):
    group = lax.axis_index("dp")
    opening, closing = starts_ref[group], starts_ref[group + 1]
    finish = jnp.int32(0)
    start = jnp.zeros_like(rows)
    for slot in range(MOST_SEQS):
        place = opening + slot
        sequence = perm_ref[jnp.minimum(place, perm_ref.shape[0] - 1)]
        finish = finish + jnp.where(place < closing, lengths_ref[sequence], 0)
        start = jnp.where(rows >= finish, finish, start)
    return start


def project(left, right):
    return jnp.dot(left, right, preferred_element_type=F32)


def project_back(left, right):
    return lax.dot_general(left, right, (((1,), (1,)), ((), ())), preferred_element_type=F32)


def row_contract(left, right):
    return lax.dot_general(left, right, (((0,), (0,)), ((), ())), preferred_element_type=F32)


def lanes(shape):
    return lax.broadcasted_iota(jnp.int32, shape, len(shape) - 1)


def turned(slab):
    half = HEAD_SIZE // 2
    ahead = pltpu.roll(slab, SLAB - half, 1)
    behind = pltpu.roll(slab, half, 1)
    return jnp.where(lanes(slab.shape) % HEAD_SIZE < half, ahead, behind)


def head_pair(slab):
    left = lanes(slab.shape) < HEAD_SIZE
    zero = jnp.zeros_like(slab)
    return jnp.concatenate([jnp.where(left, slab, zero), jnp.where(left, zero, slab)], axis=0)


def join_pair(stacked):
    half = stacked.shape[0] // 2
    left = lanes((half, SLAB)) < HEAD_SIZE
    return jnp.where(left, stacked[:half], stacked[half:])


def params(**kwargs):
    return pltpu.CompilerParams(vmem_limit_bytes=VMEM_LIMIT, **kwargs)


def vmem_specs(count):
    return [pl.BlockSpec(memory_space=pltpu.VMEM)] * count


def weight_fetches(packed, target, sems):
    rows = target.shape[0] // packed.shape[0]
    return [
        pltpu.make_async_copy(
            packed.at[block, :rows], target.at[block * rows : (block + 1) * rows], sems.at[block]
        )
        for block in range(packed.shape[0])
    ]


def attend_kernel(
    count, x_ref, packed_ref, gain_ref, cos_ref, sin_ref, start_ref, dy_ref,
    normed_ref, q_ref, k_ref, v_ref, mixed_ref, lse_ref, near_ref, bias_ref, stat_ref, w_ref, sems,
    near_send, near_receive,
):
    fetches = weight_fetches(packed_ref, w_ref, sems)
    for fetch in fetches:
        fetch.start()
    line = Line(count)
    line.barrier()
    gather = Gather(line, near_ref, near_send, near_receive, dy_ref.shape[0], 1)
    gather.start(0, dy_ref)
    for fetch in fetches:
        fetch.wait()
    rows_all = x_ref.shape[0]
    q_width = q_ref.shape[1]
    kv_slabs = v_ref.shape[0] // 2
    slabs = q_width // SLAB
    scale = HEAD_SIZE ** (-0.5)

    @pl.loop(0, rows_all // SPAN)
    def _(step):
        rows = pl.ds(step * SPAN, SPAN)
        x = x_ref[rows, :].astype(F32)
        inverse = lax.rsqrt(jnp.mean(x * x, axis=-1, keepdims=True) + norm_epsilon)
        normed = (x * inverse * gain_ref[...]).astype(BF16)
        normed_ref[rows, :] = normed
        pre = project(normed, w_ref[...])
        cosine, sine = cos_ref[rows, :], sin_ref[rows, :]
        for slab in range(slabs):
            part = pre[:, slab * SLAB : (slab + 1) * SLAB]
            part = (part * cosine + turned(part) * sine).astype(BF16)
            q_ref[rows, slab * SLAB : (slab + 1) * SLAB] = (part.astype(F32) * scale).astype(BF16)
        left = lanes((SPAN, SLAB)) < HEAD_SIZE
        for pair in range(kv_slabs):
            at = q_width + pair * SLAB
            key = pre[:, at : at + SLAB]
            key = key * cosine + turned(key) * sine
            at = at + kv_slabs * SLAB
            value = pre[:, at : at + SLAB]
            for ref, full in ((k_ref, key), (v_ref, value)):
                other = pltpu.roll(full, HEAD_SIZE, 1)
                ref[2 * pair, rows, :] = jnp.where(left, full, other).astype(BF16)
                ref[2 * pair + 1, rows, :] = jnp.where(left, other, full).astype(BF16)

    members = slabs // (2 * kv_slabs)
    for tile in range(rows_all // SPAN):
        first, span = tile * SPAN, (tile + 1) * SPAN
        columns = lanes((SPAN, span))
        row_ids = first + lax.broadcasted_iota(jnp.int32, (SPAN, span), 0)
        allowed = (columns >= start_ref[first : first + SPAN, :]) & (columns <= row_ids)
        bias_ref[:, :span] = jnp.where(allowed, 0.0, mask_fill)

        @pl.loop(0, slabs)
        def _(slab):
            at = pl.ds(pl.multiple_of(slab * SLAB, SLAB), SLAB)
            head = slab // members
            stacked = head_pair(q_ref[first : first + SPAN, at])
            scores = project_back(stacked, k_ref[head, :span, :])
            bias = bias_ref[:, :span]
            scores = scores + jnp.concatenate([bias, bias], axis=0)
            top = jnp.max(scores, axis=-1, keepdims=True)
            weights = jnp.exp(scores - top)
            total = jnp.sum(weights, axis=-1, keepdims=True)
            mixed = project(weights.astype(BF16), v_ref[head, :span, :]) / total
            mixed_ref[first : first + SPAN, at] = join_pair(mixed).astype(BF16)
            logs = top + jnp.log(total)
            old = stat_ref[first : first + SPAN, :]
            lane = lanes(old.shape)
            old = jnp.where(lane == 2 * slab, logs[:SPAN], old)
            stat_ref[first : first + SPAN, :] = jnp.where(lane == 2 * slab + 1, logs[SPAN:], old)

    lse_ref[...] = jnp.transpose(stat_ref[...])[: lse_ref.shape[0], :]
    for way in (0, 1):
        @pl.when(line.has[1 - way])
        def _(way=way):
            gather.copy(line.neighbour[1 - way], 0, way).wait_recv()

        @pl.when(line.has[way])
        def _(way=way):
            gather.copy(line.place, 0, way, dy_ref).wait_send()


def attend(
    x_full, w_qkv, gain, cosine, sine, start, dy, q_width, kv_width, count, collective_id
):
    rows = x_full.shape[0]
    heads = 2 * (kv_width // SLAB)
    hbm = pl.BlockSpec(memory_space=pl.ANY)
    flops = 2 * rows * x_full.shape[1] * (q_width + 2 * kv_width) + 8 * rows * rows * q_width
    return pl.pallas_call(
        functools.partial(attend_kernel, count),
        out_shape=(
            jax.ShapeDtypeStruct(x_full.shape, BF16),
            jax.ShapeDtypeStruct((rows, q_width), BF16),
            jax.ShapeDtypeStruct((heads, rows, SLAB), BF16),
            jax.ShapeDtypeStruct((heads, rows, SLAB), BF16),
            jax.ShapeDtypeStruct((rows, q_width), BF16),
            jax.ShapeDtypeStruct((q_width // HEAD_SIZE, rows), F32),
            jax.ShapeDtypeStruct(x_full.shape, BF16),
        ),
        in_specs=vmem_specs(1) + [hbm] + vmem_specs(4) + [hbm],
        out_specs=tuple(vmem_specs(6)) + (hbm,),
        scratch_shapes=[
            pltpu.VMEM((SPAN, rows), F32),
            pltpu.VMEM((rows, SLAB), F32),
            pltpu.VMEM((x_full.shape[1], w_qkv.shape[2]), BF16),
            pltpu.SemaphoreType.DMA((w_qkv.shape[0],)),
            copy_sems(count, 1), copy_sems(count, 1),
        ],
        compiler_params=params(collective_id=collective_id, has_side_effects=True),
        cost_estimate=pl.CostEstimate(flops=flops, bytes_accessed=1 << 24, transcendentals=1 << 23),
        name="attend",
    )(x_full, w_qkv, gain, cosine, sine, start, dy)


SUBS = 4
BLOCK = 1024


class Line:
    def __init__(self, count):
        self.count = count
        self.place = lax.axis_index("tensor")
        self.has = (self.place < count - 1, self.place > 0)
        self.neighbour = (self.place + 1, self.place - 1)
        other = count - 1 - self.place
        self.lag = jnp.where(self.place > other, self.place, other)

    def greet(self, semaphore):
        for way in (0, 1):
            @pl.when(self.has[way])
            def _(way=way):
                pl.semaphore_signal(semaphore, 1, device_id={"tensor": self.neighbour[way]})
        ends = (self.place == 0) | (self.place == self.count - 1)
        return jnp.where(ends, 1, 2)

    def barrier(self):
        semaphore = pltpu.get_barrier_semaphore()
        pl.semaphore_wait(semaphore, self.greet(semaphore))

    def copy(self, source, target, send, receive, way):
        return pltpu.make_async_remote_copy(
            src_ref=source, dst_ref=target, send_sem=send, recv_sem=receive,
            device_id={"tensor": self.neighbour[way]},
        )


class Gather:
    def __init__(self, line, full, send, receive, chunk_rows, pieces, lags=None, near=0):
        self.line, self.full, self.send, self.receive = line, full, send, receive
        self.chunk_rows, self.size, self.pieces = chunk_rows, chunk_rows // pieces, pieces
        self.lags, self.near = lags or [0] * line.count, near

    def rows(self, chunk, piece):
        start = chunk * self.chunk_rows + piece * self.size
        return pl.ds(pl.multiple_of(start, self.size), self.size)

    def copy(self, chunk, piece, way, source=None):
        target = self.full.at[self.rows(chunk, piece)]
        return self.line.copy(
            target if source is None else source, target,
            self.send.at[way, chunk, piece], self.receive.at[way, chunk, piece], way,
        )

    def start(self, piece, source=None):
        for way in (0, 1):
            @pl.when(self.line.has[way])
            def _(way=way):
                self.copy(self.line.place, piece, way, source).start()

    def start_near(self, piece, source):
        line = self.line
        for way, chunk in ((0, line.place - 1), (1, line.place + 1)):
            @pl.when(line.has[0] & line.has[1])
            def _(way=way, chunk=chunk):
                self.copy(chunk, piece, way, source.at[self.rows(chunk, piece)]).start()

    def turn(self, turn):
        line = self.line
        for chunk in range(line.count):
            for way in (0, 1):
                hop = (line.place - chunk if way == 0 else chunk - line.place) - self.near
                piece = turn - self.lags[chunk] - hop

                @pl.when((hop > 0) & (piece >= 0) & (piece < self.pieces))
                def _(way=way, chunk=chunk, piece=piece):
                    self.copy(chunk, piece, way).wait_recv()

                    @pl.when(line.has[way])
                    def _():
                        self.copy(chunk, piece, way).start()

    def finish(self, source=None):
        line = self.line

        @pl.loop(0, self.pieces)
        def _(piece):
            for chunk in range(line.count):
                @pl.when(line.has[0] & (chunk <= line.place - self.near))
                def _(chunk=chunk):
                    self.copy(chunk, piece, 0, source).wait_send()

                @pl.when(line.has[1] & (chunk >= line.place + self.near))
                def _(chunk=chunk):
                    self.copy(chunk, piece, 1, source).wait_send()


class Scatter:
    def __init__(self, line, partial, landing, send, receive, chunk_rows, pieces):
        self.line, self.partial, self.landing = line, partial, landing
        self.send, self.receive = send, receive
        self.chunk_rows, self.size, self.pieces = chunk_rows, chunk_rows // pieces, pieces
        self.lag = line.lag

    def rows(self, chunk, piece):
        start = chunk * self.chunk_rows + piece * self.size
        return pl.ds(pl.multiple_of(start, self.size), self.size)

    def landed(self, chunk, piece, way, owner):
        if way == 1:
            chunk = jnp.where(chunk == owner, self.line.count, chunk)
        return self.rows(chunk, piece)

    def copy(self, chunk, piece, way, owner=None):
        owner = self.line.neighbour[way] if owner is None else owner
        return self.line.copy(
            self.partial.at[self.rows(chunk, piece)],
            self.landing.at[self.landed(chunk, piece, way, owner)],
            self.send.at[way, chunk, piece], self.receive.at[way, chunk, piece], way,
        )

    def wait(self, chunk, piece, way):
        self.copy(chunk, piece, way, self.line.place).wait_recv()

    def forward(self, piece, way):
        line = self.line
        for step in range(line.count - 1):
            chunk = line.count - 1 - step if way == 0 else step
            beyond = chunk > line.place if way == 0 else chunk < line.place

            @pl.when(beyond)
            def _(chunk=chunk):
                @pl.when(line.has[1 - way])
                def _():
                    self.wait(chunk, piece, way)
                    rows = self.rows(chunk, piece)
                    total = self.partial[rows, :].astype(F32)
                    total = total + self.landing[rows, :].astype(F32)
                    self.partial[rows, :] = total.astype(BF16)

                self.copy(chunk, piece, way).start()

    def turn(self, turn):
        line = self.line
        for way, lag in ((0, line.place), (1, line.count - 1 - line.place)):
            piece = turn - lag

            @pl.when((piece >= 0) & (piece < self.pieces))
            def _(way=way, piece=piece):
                self.forward(piece, way)

    def settle(self, turn, use):
        piece = turn - self.lag

        @pl.when((piece >= 0) & (piece < self.pieces))
        def _():
            for way in (0, 1):
                @pl.when(self.line.has[1 - way])
                def _(way=way):
                    self.wait(self.line.place, piece, way)
            use(piece)

    def total(self, piece):
        place = self.line.place
        total = self.partial[self.rows(place, piece), :].astype(F32)
        for way in (0, 1):
            got = self.landing[self.landed(place, piece, way, place), :].astype(F32)
            total = total + jnp.where(self.line.has[1 - way], got, 0.0)
        return total

    def finish(self):
        line = self.line

        @pl.loop(0, self.pieces)
        def _(piece):
            for chunk in range(line.count):
                @pl.when(chunk > line.place)
                def _(chunk=chunk):
                    self.copy(chunk, piece, 0).wait_send()

                @pl.when(chunk < line.place)
                def _(chunk=chunk):
                    self.copy(chunk, piece, 1).wait_send()


class Stream(Scatter):
    def __init__(self, line, partial, landing, send, receive, chunk_rows, pieces, offset, hop):
        super().__init__(line, partial, landing, send, receive, chunk_rows, pieces)
        self.offset, self.hop = offset, hop
        count = line.count
        self.lag = 0
        for place in range(count):
            up = (count - 1 - place) * pieces + hop * place
            down = (count - 2 - place) * pieces + offset + hop * (count - 1 - place)
            late = max(up if place > 0 else 0, down if place < count - 1 else 0)
            self.lag = self.lag + jnp.where(line.place == place, late, 0)
        self.turns = (count - 1) * (pieces + hop) + offset

    def turn(self, turn):
        line, pieces = self.line, self.pieces
        last = line.count - 1
        lags = (self.hop * line.place, self.offset + self.hop * (last - line.place))
        for way, lag in enumerate(lags):
            since = turn - lag
            piece = since % pieces
            chunk = last - way - since // pieces
            beyond = chunk > line.place if way == 0 else chunk < line.place

            @pl.when((since >= 0) & (since < last * pieces) & beyond)
            def _(way=way, piece=piece, chunk=chunk):
                @pl.when(line.has[1 - way])
                def _():
                    self.wait(chunk, piece, way)
                    rows = self.rows(chunk, piece)
                    total = self.partial[rows, :].astype(F32)
                    total = total + self.landing[rows, :].astype(F32)
                    self.partial[rows, :] = total.astype(BF16)

                self.copy(chunk, piece, way).start()


class Fold:
    def __init__(self, replicas, sums, traded, arrived, pair_sems, sends, receives):
        self.halves = replicas // 2
        self.sums, self.traded, self.arrived = sums, traded, arrived
        self.pair_sems, self.sends, self.receives = pair_sems, sends, receives
        replica = lax.axis_index("dp")
        self.side, self.mine = replica % 2, replica // 2
        self.partner = replica + 1 - 2 * self.side

    def greet(self, semaphore):
        pl.semaphore_signal(semaphore, 1, device_id={"dp": self.partner})
        for step in range(1, self.halves):
            peer = 2 * ((self.mine + step) % self.halves) + self.side
            pl.semaphore_signal(semaphore, 1, device_id={"dp": peer})
        return self.halves

    def pair(self):
        return pltpu.make_async_remote_copy(
            src_ref=self.sums.at[:, 1 - self.side], dst_ref=self.traded,
            send_sem=self.pair_sems.at[0], recv_sem=self.pair_sems.at[1],
            device_id={"dp": self.partner},
        )

    def peer(self, half, landing):
        return pltpu.make_async_remote_copy(
            src_ref=self.sums.at[half, self.side], dst_ref=self.arrived.at[landing],
            send_sem=self.sends.at[half], recv_sem=self.receives.at[landing],
            device_id={"dp": 2 * half + self.side},
        )

    def others(self):
        return [(self.mine + step) % self.halves for step in range(1, self.halves)]

    def spread(self):
        self.pair().wait_recv()

        @pl.loop(0, self.halves)
        def _(half):
            total = self.sums[half, self.side].astype(F32) + self.traded[half].astype(F32)
            self.sums[half, self.side] = total.astype(BF16)

        for half in self.others():
            self.peer(half, self.mine).start()

    def total(self):
        total = self.sums[self.mine, self.side].astype(F32)
        for half in self.others():
            self.peer(half, half).wait_recv()
            total = total + self.arrived[half].astype(F32)
        return total

    def finish(self):
        self.pair().wait_send()
        for half in self.others():
            self.peer(half, self.mine).wait_send()


def fold_scratch(replicas, rows, width):
    halves = replicas // 2
    return [
        pltpu.VMEM((halves, 2, rows, width), BF16),
        pltpu.VMEM((halves, rows, width), BF16),
        pltpu.VMEM((halves, rows, width), BF16),
        pltpu.SemaphoreType.DMA((2,)),
        pltpu.SemaphoreType.DMA((halves,)),
        pltpu.SemaphoreType.DMA((halves,)),
    ]


def landing_rows(count, chunk_rows):
    return (count + 1) * chunk_rows


def copy_sems(count, pieces):
    return pltpu.SemaphoreType.DMA((2, count, pieces))


def settle_lags(count):
    return [max(place, count - 1 - place) for place in range(count)]


def gather_kernel(
    count, pieces, x_ref, freqs_ref, lengths_ref, perm_ref, starts_ref,
    full_ref, cos_ref, sin_ref, column_ref, row_ref, send, receive, local,
):
    line = Line(count)
    chunk_rows = x_ref.shape[0]
    own = pl.ds(pl.multiple_of(line.place * chunk_rows, chunk_rows), chunk_rows)
    keep = pltpu.make_async_copy(x_ref, full_ref.at[own], local)
    keep.start()
    line.barrier()
    gather = Gather(line, full_ref, send, receive, chunk_rows, pieces)
    for piece in range(pieces):
        gather.start(piece, x_ref.at[gather.rows(0, piece)])
    row_ref[...] = segment_starts(lengths_ref, perm_ref, starts_ref, lanes(row_ref.shape))
    size = count * chunk_rows // pieces

    @pl.loop(1, pieces + count - 1)
    def _(turn):
        gather.turn(turn)

        @pl.when(turn <= pieces)
        def _():
            first = pl.multiple_of((turn - 1) * size, size)
            rows = first + lax.broadcasted_iota(jnp.int32, (size, SLAB), 0)
            start = segment_starts(lengths_ref, perm_ref, starts_ref, rows)
            angles = (rows - start).astype(F32) * freqs_ref[...]
            low_half = lanes(rows.shape) % HEAD_SIZE < HEAD_SIZE // 2
            sines = jnp.sin(angles)
            cos_ref[pl.ds(first, size), :] = jnp.cos(angles)
            sin_ref[pl.ds(first, size), :] = jnp.where(low_half, -sines, sines)
            column_ref[pl.ds(first, size), :] = start[:, 0:1]

    gather.finish(x_ref.at[gather.rows(0, 0)])
    keep.wait()


def line_gather(x, freqs, lengths, perm, starts, count, collective_id, pieces=8):
    rows, width = x.shape
    total = count * rows
    return pl.pallas_call(
        functools.partial(gather_kernel, count, pieces),
        out_shape=(
            jax.ShapeDtypeStruct((total, width), x.dtype),
            jax.ShapeDtypeStruct((total, SLAB), F32),
            jax.ShapeDtypeStruct((total, SLAB), F32),
            jax.ShapeDtypeStruct((total, 1), jnp.int32),
            jax.ShapeDtypeStruct((1, total), jnp.int32),
        ),
        in_specs=vmem_specs(2) + [pl.BlockSpec(memory_space=pltpu.SMEM)] * 3,
        out_specs=(pl.BlockSpec(memory_space=pl.ANY),) + tuple(vmem_specs(4)),
        scratch_shapes=[
            copy_sems(count, pieces), copy_sems(count, pieces), pltpu.SemaphoreType.DMA
        ],
        compiler_params=params(collective_id=collective_id, has_side_effects=True),
        cost_estimate=pl.CostEstimate(
            flops=0, bytes_accessed=200 * rows * width, transcendentals=0
        ),
        name="line_gather",
    )(x, freqs, lengths, perm, starts)


def forward_turn_kernel(
    count, pieces, mixed_ref, w_ref, x_ref, gain_ref, middle_ref, full_ref,
    partial, landing, rs_send, rs_receive, ag_send, ag_receive,
):
    line = Line(count)
    chunk_rows = x_ref.shape[0]
    line.barrier()

    @pl.loop(0, partial.shape[0] // SPAN)
    def _(step):
        rows = pl.ds(pl.multiple_of(step * SPAN, SPAN), SPAN)
        partial[rows, :] = project(mixed_ref[rows, :], w_ref[...]).astype(BF16)

    scatter = Scatter(line, partial, landing, rs_send, rs_receive, chunk_rows, pieces)
    gather = Gather(
        line, full_ref, ag_send, ag_receive, chunk_rows, pieces, settle_lags(count)
    )
    size = chunk_rows // pieces

    def settle(piece):
        local = pl.ds(pl.multiple_of(piece * size, size), size)
        middle = x_ref[local, :].astype(F32) + scatter.total(piece)
        middle_ref[local, :] = middle
        inverse = lax.rsqrt(jnp.mean(middle * middle, axis=-1, keepdims=True) + norm_epsilon)
        normed = (middle * inverse * gain_ref[...]).astype(BF16)
        full_ref[gather.rows(line.place, piece), :] = normed
        gather.start(piece)

    @pl.loop(0, pieces + 2 * (count - 1))
    def _(turn):
        scatter.turn(turn)
        gather.turn(turn)
        scatter.settle(turn, settle)

    scatter.finish()
    gather.finish()


def forward_turn(mixed, w_out, x, gain, count, collective_id, pieces=16):
    chunk_rows, width = x.shape
    rows = count * chunk_rows
    return pl.pallas_call(
        functools.partial(forward_turn_kernel, count, pieces),
        out_shape=(
            jax.ShapeDtypeStruct((chunk_rows, width), F32),
            jax.ShapeDtypeStruct((rows, width), BF16),
        ),
        in_specs=vmem_specs(4),
        out_specs=tuple(vmem_specs(2)),
        scratch_shapes=[
            pltpu.VMEM((rows, width), BF16),
            pltpu.VMEM((landing_rows(count, chunk_rows), width), BF16),
        ]
        + [copy_sems(count, pieces)] * 4,
        compiler_params=params(collective_id=collective_id, has_side_effects=True),
        cost_estimate=pl.CostEstimate(
            flops=2 * rows * width * mixed.shape[1],
            bytes_accessed=300 * chunk_rows * width, transcendentals=0,
        ),
        name="forward_turn",
    )(mixed, w_out, x, gain)


def hidden_kernel(
    count, pieces, normed_ref, own_ref, near_ref, middle_ref, gate_ref, up_ref, down_ref,
    full_ref, active_ref, gate_grad_ref, up_grad_ref, back_ref, out_ref,
    gate, up, down, normed, dy, active, slope, value, up_grad, back,
    partial, landing, rs_send, rs_receive, ag_send, ag_receive, loads, stores,
):
    line = Line(count)
    chunk_rows = own_ref.shape[0]
    hidden = gate_ref.shape[1]
    width = gate_ref.shape[0]
    sub = chunk_rows // SUBS
    fetches = [
        pltpu.make_async_copy(source, target, loads.at[at])
        for at, (source, target) in enumerate(
            ((normed_ref, normed), (gate_ref, gate), (up_ref, up), (down_ref, down))
        )
    ]
    for fetch in fetches:
        fetch.start()
    line.barrier()
    gather = Gather(line, dy, ag_send, ag_receive, chunk_rows, SUBS, near=1)
    scatter = Scatter(line, partial, landing, rs_send, rs_receive, chunk_rows, pieces)
    for piece in range(SUBS):
        gather.start_near(piece, near_ref)

    def chunk_at(chunk):
        return pl.ds(pl.multiple_of(chunk * chunk_rows, chunk_rows), chunk_rows)

    def place_near(way):
        rows = chunk_at(line.neighbour[way])
        return pltpu.make_async_copy(near_ref.at[rows], dy.at[rows], loads.at[5 + way])

    place_own = pltpu.make_async_copy(own_ref, dy.at[chunk_at(line.place)], loads.at[4])
    place_own.start()
    for way in (0, 1):
        @pl.when(line.has[way])
        def _(way=way):
            place_near(way).start()
    gate_grad = active
    outs = ((active, active_ref), (gate_grad, gate_grad_ref), (up_grad, up_grad_ref),
            (back, back_ref))

    def store(which, step):
        source, target = outs[which]
        rows = pl.ds(pl.multiple_of(step * sub, sub), sub)
        return pltpu.make_async_copy(source, target.at[:, rows], stores.at[which])

    def rows_of(chunk, step):
        return pl.ds(pl.multiple_of(chunk * chunk_rows + step * sub, sub), sub)

    def picked(ref, step, at=slice(None)):
        return jnp.concatenate([ref[rows_of(chunk, step), at] for chunk in range(count)], axis=0)

    def put(ref, at, rows):
        for chunk in range(count):
            ref[chunk, :, at] = rows[chunk * sub : (chunk + 1) * sub]

    def whole(ref):
        return jnp.concatenate([ref[chunk] for chunk in range(count)], axis=0)

    def settle(piece):
        size = chunk_rows // pieces
        local = pl.ds(pl.multiple_of(piece * size, size), size)
        out_ref[local, :] = (middle_ref[local, :] + scatter.total(piece)).astype(BF16)

    def exchange(turn):
        scatter.turn(turn)
        gather.turn(turn)
        scatter.settle(turn, settle)

    for at in range(3):
        fetches[at].wait()

    @pl.loop(0, SUBS)
    def _(step):
        @pl.when(step > 0)
        def _():
            store(0, step - 1).wait()

        @pl.loop(0, hidden // BLOCK)
        def _(block):
            at = pl.ds(pl.multiple_of(block * BLOCK, BLOCK), BLOCK)
            source = picked(normed, step)
            gate_pre = project(source, gate[:, at])
            up_pre = project(source, up[:, at])
            chance = 1.0 / (1.0 + jnp.exp(-gate_pre))
            silu = gate_pre * chance
            put(active, at, (silu * up_pre).astype(BF16))
            put(value.at[step], at, silu.astype(BF16))
            raised = up_pre * chance * (1.0 + gate_pre * (1.0 - chance))
            put(slope.at[step], at, raised.astype(BF16))

        store(0, step).start()

        @pl.when(step == 0)
        def _():
            fetches[3].wait()

        @pl.loop(0, width // BLOCK)
        def _(block):
            at = pl.ds(pl.multiple_of(block * BLOCK, BLOCK), BLOCK)
            product = project(whole(active), down[:, at]).astype(BF16)
            for chunk in range(count):
                partial[rows_of(chunk, step), at] = product[chunk * sub : (chunk + 1) * sub]

        exchange(step)

    @pl.loop(0, SUBS)
    def _(step):
        @pl.when(step == 0)
        def _():
            store(0, SUBS - 1).wait()
            place_own.wait()
            for way in (0, 1):
                @pl.when(line.has[way])
                def _(way=way):
                    place_near(way).wait()

        @pl.when(step > 0)
        def _():
            for which in (1, 2, 3):
                store(which, step - 1).wait()

        @pl.loop(0, hidden // BLOCK)
        def _(block):
            at = pl.ds(pl.multiple_of(block * BLOCK, BLOCK), BLOCK)
            active_grad = project_back(picked(dy, step), down[at, :])
            for chunk in range(count):
                grad = active_grad[chunk * sub : (chunk + 1) * sub]
                here = (grad * slope[step, chunk, :, at].astype(F32)).astype(BF16)
                gate_grad[chunk, :, at] = here
                here = (grad * value[step, chunk, :, at].astype(F32)).astype(BF16)
                up_grad[chunk, :, at] = here

        for which in (1, 2):
            store(which, step).start()
        exchange(SUBS + 2 * step)

        @pl.loop(0, width // BLOCK)
        def _(block):
            at = pl.ds(pl.multiple_of(block * BLOCK, BLOCK), BLOCK)
            total = project_back(whole(gate_grad), gate[at, :])
            total = total + project_back(whole(up_grad), up[at, :])
            put(back, at, total.astype(BF16))

        store(3, step).start()
        exchange(SUBS + 2 * step + 1)

    keep = pltpu.make_async_copy(dy, full_ref, loads.at[0])
    keep.start()

    @pl.loop(3 * SUBS, pieces + count - 1)
    def _(turn):
        exchange(turn)

    for which in (1, 2, 3):
        store(which, SUBS - 1).wait()
    keep.wait()
    scatter.finish()
    gather.finish()


def hidden_layer(
    normed, own, near, middle, w_gate, w_up, w_down, count, collective_id, pieces=8
):
    chunk_rows, width = own.shape
    hidden = w_gate.shape[1]
    rows = count * chunk_rows
    sub = chunk_rows // SUBS
    tall = jax.ShapeDtypeStruct((count, chunk_rows, hidden), BF16)
    hbm = pl.BlockSpec(memory_space=pl.ANY)
    outs = pl.pallas_call(
        functools.partial(hidden_kernel, count, pieces),
        out_shape=(
            jax.ShapeDtypeStruct((rows, width), BF16), tall, tall, tall,
            jax.ShapeDtypeStruct((count, chunk_rows, width), BF16),
            jax.ShapeDtypeStruct((chunk_rows, width), BF16),
        ),
        in_specs=[hbm] * 3 + vmem_specs(1) + [hbm] * 3,
        out_specs=(hbm, hbm, hbm, hbm, hbm, vmem_specs(1)[0]),
        scratch_shapes=[
            pltpu.VMEM((width, hidden), BF16),
            pltpu.VMEM((width, hidden), BF16),
            pltpu.VMEM((hidden, width), BF16),
            pltpu.VMEM((rows, width), BF16),
            pltpu.VMEM((rows, width), BF16),
            pltpu.VMEM((count, sub, hidden), BF16),
            pltpu.VMEM((SUBS, count, sub, hidden), BF16),
            pltpu.VMEM((SUBS, count, sub, hidden), BF16),
            pltpu.VMEM((count, sub, hidden), BF16),
            pltpu.VMEM((count, sub, width), BF16),
            pltpu.VMEM((rows, width), BF16),
            pltpu.VMEM((landing_rows(count, chunk_rows), width), BF16),
            copy_sems(count, pieces), copy_sems(count, pieces),
            copy_sems(count, SUBS), copy_sems(count, SUBS),
            pltpu.SemaphoreType.DMA((7,)), pltpu.SemaphoreType.DMA((4,)),
        ],
        compiler_params=params(collective_id=collective_id, has_side_effects=True),
        cost_estimate=pl.CostEstimate(
            flops=12 * rows * width * hidden, bytes_accessed=1 << 26, transcendentals=rows * hidden
        ),
        name="hidden_layer",
    )(normed, own, near, middle, w_gate, w_up, w_down)
    return [outs[0]] + [out.reshape(rows, out.shape[-1]) for out in outs[1:5]] + [outs[5]]


def backward_turn_kernel(
    count, pieces, given_ref, dy_ref, middle_ref, gain_ref,
    normed_full_ref, gate_grad_ref, up_grad_ref, active_ref, dy_full_ref,
    grad_ref, full_ref, gain_grad_ref, sums_ref, down_grad_ref, gate_out_ref, traded_ref,
    partial, landing, tiles, traded, normed, gate_grad, active, dy_full, kept, arrived,
    arrived_two, summed, rs_send, rs_receive, ag_send, ag_receive, load, trade_send, trade_receive, fetches, stores,
    peer_send, peer_receive, operands, summed_out,
):
    line = Line(count)
    chunk_rows = dy_ref.shape[0]
    fetch = pltpu.make_async_copy(given_ref, partial, load)
    fetch.start()
    brought = [
        pltpu.make_async_copy(source, target, operands.at[at])
        for at, (source, target) in enumerate((
            (active_ref, active), (dy_full_ref, dy_full), (normed_full_ref, normed),
            (gate_grad_ref, gate_grad), (up_grad_ref, active),
        ))
    ]
    for copy in brought[:4]:
        copy.start()
    replica = lax.axis_index("dp")
    side, mine = replica % 2, replica // 2
    partner = replica + 1 - 2 * side
    halves = kept.shape[0] // traded.shape[0]
    others = [(mine + step) % halves for step in range(1, halves)]
    semaphore = pltpu.get_barrier_semaphore()
    pl.semaphore_signal(semaphore, 1, device_id={"dp": partner})
    for half in others:
        pl.semaphore_signal(semaphore, 1, device_id={"dp": 2 * half + side})
    pl.semaphore_wait(semaphore, line.greet(semaphore) + halves)
    fetch.wait()
    scatter = Scatter(line, partial, landing, rs_send, rs_receive, chunk_rows, pieces)
    gather = Gather(
        line, full_ref, ag_send, ag_receive, chunk_rows, pieces, settle_lags(count)
    )
    size = chunk_rows // pieces
    gain_grad_ref[...] = jnp.zeros_like(gain_grad_ref)

    def settle(piece):
        local = pl.ds(pl.multiple_of(piece * size, size), size)
        grad, gain_grad = norm_back(scatter.total(piece), middle_ref[local, :], gain_ref[...])
        grad = grad + dy_ref[local, :].astype(F32)
        gain_grad_ref[...] += gain_grad
        grad_ref[local, :] = grad
        full_ref[gather.rows(line.place, piece), :] = grad.astype(BF16)
        gather.start(piece)

    block = traded.shape[0]
    width = traded.shape[1]
    products = ((active, dy_full), (normed, gate_grad), (normed, active))
    needed = ((0, 1), (2, 3), (4,))
    pairs = halves * len(products)
    theirs = pl.ds(pl.multiple_of((1 - side) * block, block), block)
    ours = pl.ds(pl.multiple_of(side * block, block), block)

    def trade(pair):
        return pltpu.make_async_remote_copy(
            src_ref=tiles.at[pair % 2, theirs], dst_ref=traded_ref.at[pair],
            send_sem=trade_send.at[pair], recv_sem=trade_receive.at[pair],
            device_id={"dp": partner},
        )

    def bring(pair):
        return pltpu.make_async_copy(traded_ref.at[pair], traded, fetches)

    def put(pair):
        rows = pl.ds(pl.multiple_of((pair % halves) * block, block), block)
        return pltpu.make_async_copy(
            tiles.at[pair % 2, ours], sums_ref.at[rows], stores.at[pair % 2]
        )

    folds = ((kept, arrived), (dy_full, arrived_two))

    def kept_rows(half):
        return pl.ds(pl.multiple_of(half * block, block), block)

    def peer(which, half, slot):
        source, landing = folds[which]
        return pltpu.make_async_remote_copy(
            src_ref=source.at[kept_rows(half)], dst_ref=landing.at[slot],
            send_sem=peer_send.at[which, half], recv_sem=peer_receive.at[which, slot],
            device_id={"dp": 2 * half + side},
        )

    def slot_of(sender, owner):
        return (sender - owner + halves - 1) % halves

    def beside(pair):
        @pl.when((pair >= 2) & (pair < pairs))
        def _():
            trade(pair - 2).wait_send()

            @pl.when(pair - 2 >= 2 * halves)
            def _():
                put(pair - 2).wait()

        @pl.when((pair >= 1) & (pair <= pairs))
        def _():
            trade(pair - 1).wait_recv()
            bring(pair - 1).start()

        at = pl.ds(pl.multiple_of((pair % halves) * 2 * block, 2 * block), 2 * block)
        for which, (left, right) in enumerate(products):
            @pl.when(pair == which * halves)
            def _(which=which):
                for operand in needed[which]:
                    brought[operand].wait()
                if which == 1:
                    brought[4].start()

            @pl.when(pair // halves == which)
            def _(left=left, right=right):
                tiles[pair % 2] = row_contract(left[:, at], right[...]).astype(BF16)

        @pl.when(pair < pairs)
        def _():
            trade(pair).start()

        @pl.when((pair >= 1) & (pair <= pairs))
        def _():
            last = pair - 1
            bring(last).wait()
            slot = last % 2
            total = tiles[slot, ours].astype(F32) + traded[...].astype(F32)

            for which in range(2):
                @pl.when(last // halves == which)
                def _(which=which):
                    half = last % halves
                    folds[which][0][kept_rows(half), :] = total.astype(BF16)

                    @pl.when(half != mine)
                    def _():
                        peer(which, half, slot_of(mine, half)).start()

            @pl.when(last >= 2 * halves)
            def _():
                tiles[slot, ours] = total.astype(BF16)
                put(last).start()

    def add_up(which):
        total = folds[which][0][kept_rows(mine), :].astype(F32)
        for half in others:
            slot = slot_of(half, mine)
            peer(which, half, slot).wait_recv()
            total = total + folds[which][1][slot].astype(F32)
        summed[...] = total
        for half in others:
            peer(which, half, slot_of(mine, half)).wait_send()

    def hand_out(which):
        return pltpu.make_async_copy(summed, (down_grad_ref, gate_out_ref)[which], summed_out)

    turns = max(pieces + 2 * (count - 1), pairs + 1)

    @pl.loop(0, turns)
    def _(turn):
        scatter.turn(turn)
        gather.turn(turn)
        scatter.settle(turn, settle)
        beside(turn)

        @pl.when(turn == turns - 1)
        def _():
            add_up(0)
            hand_out(0).start()

    for pair in range(pairs - 2, pairs):
        trade(pair).wait_send()
        put(pair).wait()
    hand_out(0).wait()
    add_up(1)
    hand_out(1).start()
    scatter.finish()
    gather.finish()
    hand_out(1).wait()


def norm_back(grad, rows, gain):
    inverse = lax.rsqrt(jnp.mean(rows * rows, axis=-1, keepdims=True) + norm_epsilon)
    scaled = grad * gain
    common = jnp.mean(scaled * rows, axis=-1, keepdims=True) * (inverse * inverse * inverse)
    gain_grad = jnp.sum(grad * (rows * inverse), axis=0, keepdims=True)
    return inverse * scaled - rows * common, gain_grad


def backward_turn(
    given, dy, middle, gain, normed_full, gate_grad, up_grad, active, dy_full,
    count, replicas, collective_id, pieces=16,
):
    chunk_rows, width = dy.shape
    rows = count * chunk_rows
    block = width // replicas
    kept_rows = width // 2
    pairs = 3 * kept_rows // block
    hbm = pl.BlockSpec(memory_space=pl.ANY)
    return pl.pallas_call(
        functools.partial(backward_turn_kernel, count, pieces),
        out_shape=(
            jax.ShapeDtypeStruct((chunk_rows, width), F32),
            jax.ShapeDtypeStruct((rows, width), BF16),
            jax.ShapeDtypeStruct((1, width), F32),
            jax.ShapeDtypeStruct((kept_rows, width), BF16),
            jax.ShapeDtypeStruct((block, width), F32),
            jax.ShapeDtypeStruct((block, width), F32),
            jax.ShapeDtypeStruct((pairs, block, width), BF16),
        ),
        in_specs=[hbm] + vmem_specs(3) + [hbm] * 5,
        out_specs=tuple(vmem_specs(3)) + (hbm,) * 4,
        scratch_shapes=[
            pltpu.VMEM((rows, width), BF16),
            pltpu.VMEM((landing_rows(count, chunk_rows), width), BF16),
            pltpu.VMEM((2, 2 * block, width), BF16),
            pltpu.VMEM((block, width), BF16),
        ]
        + [pltpu.VMEM((rows, width), BF16)] * 4
        + [pltpu.VMEM((kept_rows, width), BF16)]
        + [pltpu.VMEM((replicas // 2 - 1, block, width), BF16)] * 2
        + [pltpu.VMEM((block, width), F32)]
        + [copy_sems(count, pieces)] * 4
        + [
            pltpu.SemaphoreType.DMA,
            pltpu.SemaphoreType.DMA((pairs,)),
            pltpu.SemaphoreType.DMA((pairs,)),
            pltpu.SemaphoreType.DMA,
            pltpu.SemaphoreType.DMA((2,)),
            pltpu.SemaphoreType.DMA((2, replicas // 2)),
            pltpu.SemaphoreType.DMA((2, replicas // 2)),
            pltpu.SemaphoreType.DMA((5,)),
            pltpu.SemaphoreType.DMA,
        ],
        compiler_params=params(collective_id=collective_id, has_side_effects=True),
        cost_estimate=pl.CostEstimate(
            flops=6 * rows * width * width, bytes_accessed=1 << 26, transcendentals=0
        ),
        name="backward_turn",
    )(given, dy, middle, gain, normed_full, gate_grad, up_grad, active, dy_full)


STREAM_OFFSET = 4
STREAM_HOP = 2


def last_turn_kernel(
    count, pieces, replicas, branch_ref, out_ref, mixed_ref, q_ref, k_ref, v_ref, lse_ref, cos_ref,
    sin_ref, start_ref, packed_ref, normed_in, middle_grad_in, x_in, gain_ref, gain_two_ref,
    grad_ref, out_grad_ref, query_grad_ref, key_grad_ref, value_grad_ref, gain_one_out, gain_two_out,
    dqkv_ref, dmix_ref, bias_ref, dq_ref, dk_ref, dv_ref, w_ref, sems,
    normed_ref, middle_grad_ref, x_ref, operands, partial, landing,
    out_sums, out_traded, out_arrived, out_pair, out_sends, out_receives,
    sums, traded, arrived, pair_sems, sends, receives,
    gain_own, gain_row, gain_land, gains_ref, gain_line,
    rs_send, rs_receive, dp_send, dp_receive, line_send, line_receive,
):
    line = Line(count)
    chunk_rows = x_ref.shape[0]
    q_width = q_ref.shape[1]
    slabs = q_width // SLAB
    kv_heads = k_ref.shape[0]
    members = slabs // kv_heads
    scale = HEAD_SIZE ** (-0.5)
    fetches = weight_fetches(packed_ref, w_ref, sems)
    for at, (source, target) in enumerate(
        ((middle_grad_in, middle_grad_ref), (x_in, x_ref), (normed_in, normed_ref))
    ):
        fetches.append(pltpu.make_async_copy(source, target, operands.at[at]))
    for fetch in fetches:
        fetch.start()
    replica = lax.axis_index("dp")
    semaphore = pltpu.get_barrier_semaphore()
    for step in range(1, replicas):
        pl.semaphore_signal(semaphore, 1, device_id={"dp": (replica + step) % replicas})
    for step in range(1, count):
        pl.semaphore_signal(semaphore, 1, device_id={"tensor": (line.place + step) % count})
    out_fold = Fold(replicas, out_sums, out_traded, out_arrived, out_pair, out_sends, out_receives)
    fold = Fold(replicas, sums, traded, arrived, pair_sems, sends, receives)
    stream = Stream(
        line, partial, landing, rs_send, rs_receive, chunk_rows, pieces, STREAM_OFFSET, STREAM_HOP
    )
    size = chunk_rows // pieces
    gain_own[...] = jnp.zeros_like(gain_own)
    dk_ref[...] = jnp.zeros_like(dk_ref)
    dv_ref[...] = jnp.zeros_like(dv_ref)

    def settle(piece):
        local = pl.ds(pl.multiple_of(piece * size, size), size)
        total = stream.total(piece)
        grad, gain_grad = norm_back(total, x_ref[local, :].astype(F32), gain_ref[...])
        gain_own[...] += gain_grad
        grad_ref[local, :] = (grad + middle_grad_ref[local, :]).astype(BF16)

    def exchange(turn):
        stream.turn(turn)
        stream.settle(turn, settle)

    left = lanes((SPAN, SLAB)) < HEAD_SIZE

    def attend_tile(tile, done):
        first, span = tile * SPAN, (tile + 1) * SPAN
        rows = slice(first, first + SPAN)
        dmix_ref[...] = project_back(branch_ref[rows, :], out_ref[...]).astype(BF16)
        key_ids = lax.broadcasted_iota(jnp.int32, (span, SPAN), 0)
        row_ids = first + lanes((span, SPAN))
        allowed = (key_ids >= start_ref[:, rows]) & (key_ids <= row_ids)
        bias_ref[:span, :] = jnp.where(allowed, 0.0, mask_fill)

        @pl.loop(0, slabs)
        def _(slab):
            at = pl.ds(pl.multiple_of(slab * SLAB, SLAB), SLAB)
            head = slab // members
            queries = head_pair(q_ref[rows, at])
            grads = head_pair(dmix_ref[:, at])
            keys = k_ref[head, :span, :]
            scores = project_back(keys, queries)
            bias = bias_ref[:span, :]
            logs = jnp.concatenate(
                [lse_ref[pl.ds(2 * slab, 1), rows], lse_ref[pl.ds(2 * slab + 1, 1), rows]], axis=1
            )
            chances = jnp.exp(scores + jnp.concatenate([bias, bias], axis=1) - logs)
            chances_grad = project_back(v_ref[head, :span, :], grads)
            shared = jnp.sum(chances * chances_grad, axis=0, keepdims=True)
            score_grad = (chances * (chances_grad - shared)).astype(BF16)
            dv_ref[head, :span, :] += project(chances.astype(BF16), grads)
            dk_ref[head, :span, :] += project(score_grad, queries)
            dq_ref[:, at] = join_pair(row_contract(score_grad, keys)) * scale
            if done is not None:
                @pl.when(slab < STREAM_OFFSET - 1)
                def _():
                    exchange(done + slab)

        cosine, sine = cos_ref[rows, :], sin_ref[rows, :]
        for slab in range(slabs):
            part = dq_ref[:, slab * SLAB : (slab + 1) * SLAB]
            part = part * cosine - turned(part) * sine
            dqkv_ref[rows, slab * SLAB : (slab + 1) * SLAB] = part.astype(BF16)
        for pair in range(kv_heads // 2):
            joined = []
            for ref in (dk_ref, dv_ref):
                both = []
                for head in (2 * pair, 2 * pair + 1):
                    full = ref[head, rows, :]
                    both.append(full + pltpu.roll(full, HEAD_SIZE, 1))
                joined.append(jnp.where(left, both[0], both[1]))
            key, value = joined
            key = key * cosine - turned(key) * sine
            at = q_width + pair * SLAB
            dqkv_ref[rows, at : at + SLAB] = key.astype(BF16)
            at = at + (kv_heads // 2) * SLAB
            dqkv_ref[rows, at : at + SLAB] = value.astype(BF16)
        if tile == tiles - 1:
            for fetch in fetches:
                fetch.wait()
            pl.semaphore_wait(semaphore, replicas - 1 + count - 1)
        partial[rows, :] = project_back(dqkv_ref[rows, :], w_ref[...]).astype(BF16)

    tiles = branch_ref.shape[0] // SPAN
    done = 0
    for tile in reversed(range(tiles)):
        attend_tile(tile, done if tile < tiles - 1 else None)
        if tile < tiles - 1:
            done += min(slabs, STREAM_OFFSET - 1)
        exchange(done)
        done += 1

    block = sums.shape[2]
    out_rows = out_sums.shape[2]

    @pl.loop(done, stream.turns)
    def _(turn):
        exchange(turn)

        @pl.when(turn == done)
        def _():
            for step in range(q_width // SLAB):
                first = step * SLAB
                product = row_contract(mixed_ref[:, first : first + SLAB], branch_ref[...])
                product = product.astype(BF16)
                for row in range(0, SLAB, out_rows):
                    owner = (first + row) // out_rows
                    out_sums[owner // 2, owner % 2] = product[row : row + out_rows]
            out_fold.pair().start()

        @pl.when(turn == done + 1)
        def _():
            @pl.loop(0, replicas // 2)
            def _(half):
                at = pl.ds(pl.multiple_of(half * 2 * block, 2 * block), 2 * block)
                product = row_contract(normed_ref[:, at], dqkv_ref[...]).astype(BF16)
                for side in range(2):
                    sums[half, side] = product[side * block : (side + 1) * block]

            fold.pair().start()

        @pl.when(turn == done + 3)
        def _():
            out_fold.spread()

        @pl.when(turn == done + 4)
        def _():
            fold.spread()

    gain_row[0:1, :] = gain_own[...]
    gain_row[1:2, :] = gain_two_ref[...]

    def share(peer, landing):
        return pltpu.make_async_remote_copy(
            src_ref=gain_row, dst_ref=gain_land.at[landing],
            send_sem=dp_send.at[peer], recv_sem=dp_receive.at[landing], device_id={"dp": peer},
        )

    def pass_line(peer, landing):
        return pltpu.make_async_remote_copy(
            src_ref=gains_ref, dst_ref=gain_line.at[landing],
            send_sem=line_send.at[peer], recv_sem=line_receive.at[landing],
            device_id={"tensor": peer},
        )

    peers = [(replica + step) % replicas for step in range(1, replicas)]
    places = [(line.place + step) % count for step in range(1, count)]
    for peer in peers:
        share(peer, replica).start()
    out_grad_ref[...] = out_fold.total()
    total = fold.total()
    at = 0
    for ref in (query_grad_ref, key_grad_ref, value_grad_ref):
        ref[...] = total[:, at : at + ref.shape[1]]
        at += ref.shape[1]
    total = gain_row[...]
    for peer in peers:
        share(peer, peer).wait_recv()
        total = total + gain_land[peer]
    gains_ref[...] = total
    for peer in places:
        pass_line(peer, line.place).start()
    stream.finish()
    out_fold.finish()
    fold.finish()
    for peer in peers:
        share(peer, replica).wait_send()
    for peer in places:
        pass_line(peer, peer).wait_recv()
        total = total + gain_line[peer]
    for peer in places:
        pass_line(peer, line.place).wait_send()
    own = gain_one_out.shape[1]
    kept = jnp.zeros((2, own), F32)
    for owner in range(replicas):
        part = total[:, owner * own : (owner + 1) * own]
        kept = kept + jnp.where(replica == owner, part, 0.0)
    gain_one_out[...] = kept[0:1]
    gain_two_out[...] = kept[1:2]


def last_turn(
    branch, w_out, mixed, queries, keys, values, lse, cosine, sine, start,
    w_qkv, normed, middle_grad, x, gain, gain_two_grad, widths, count, replicas, collective_id,
    pieces=8,
):
    chunk_rows, width = x.shape
    rows, q_width = queries.shape
    kv_heads = keys.shape[0]
    block = width // replicas
    qkv_width = sum(widths)
    out_rows = q_width // replicas
    flops = 2 * rows * width * (2 * q_width + 2 * qkv_width) + 20 * rows * rows * q_width
    return pl.pallas_call(
        functools.partial(last_turn_kernel, count, pieces, replicas),
        out_shape=(
            jax.ShapeDtypeStruct((chunk_rows, width), BF16),
            jax.ShapeDtypeStruct((out_rows, width), F32),
        )
        + tuple(jax.ShapeDtypeStruct((block, part), F32) for part in widths)
        + (jax.ShapeDtypeStruct((1, block), F32),) * 2,
        in_specs=vmem_specs(10) + [pl.BlockSpec(memory_space=pl.ANY)] * 4 + vmem_specs(2),
        out_specs=tuple(vmem_specs(7)),
        scratch_shapes=[
            pltpu.VMEM((rows, qkv_width), BF16),
            pltpu.VMEM((SPAN, q_width), BF16),
            pltpu.VMEM((rows, SPAN), F32),
            pltpu.VMEM((SPAN, q_width), F32),
            pltpu.VMEM((kv_heads, rows, SLAB), F32),
            pltpu.VMEM((kv_heads, rows, SLAB), F32),
            pltpu.VMEM((width, qkv_width), BF16),
            pltpu.SemaphoreType.DMA((replicas,)),
            pltpu.VMEM((rows, width), BF16),
            pltpu.VMEM((chunk_rows, width), F32),
            pltpu.VMEM((chunk_rows, width), BF16),
            pltpu.SemaphoreType.DMA((3,)),
            pltpu.VMEM((rows, width), BF16),
            pltpu.VMEM((landing_rows(count, chunk_rows), width), BF16),
        ]
        + fold_scratch(replicas, out_rows, width)
        + fold_scratch(replicas, block, qkv_width)
        + [
            pltpu.VMEM((1, width), F32),
            pltpu.VMEM((2, width), F32),
            pltpu.VMEM((replicas, 2, width), F32),
            pltpu.VMEM((2, width), F32),
            pltpu.VMEM((count, 2, width), F32),
        ]
        + [copy_sems(count, pieces)] * 2
        + [pltpu.SemaphoreType.DMA((replicas,))] * 2
        + [pltpu.SemaphoreType.DMA((count,))] * 2,
        compiler_params=params(collective_id=collective_id, has_side_effects=True),
        cost_estimate=pl.CostEstimate(
            flops=flops, bytes_accessed=1 << 25, transcendentals=1 << 23
        ),
        name="last_turn",
    )(
        branch, w_out, mixed, queries, keys, values, lse, cosine, sine, start,
        w_qkv, normed, middle_grad, x, gain, gain_two_grad,
    )


def shards(
    inputs, cotangent, attn_gain, w_query, w_key, w_value, w_out, mlp_gain, w_gate, w_up, w_down,
    seq_lengths, group_perm, group_starts,
):
    count = lax.axis_size("tensor")
    q_width, kv_width = w_query.shape[1], w_key.shape[1]
    qkv_width = q_width + 2 * kv_width
    own = attn_gain.shape[0]
    gains = jnp.concatenate([attn_gain, mlp_gain])[None]
    gains = jnp.pad(gains, ((0, GAIN_ROWS - 1), (0, qkv_width - 2 * own)))
    packed = jnp.concatenate([w_query, w_key, w_value], axis=1)
    packed = jnp.concatenate([packed, gains], axis=0)
    qkv_full = lax.all_gather(packed[None], "dp", axis=0, tiled=True)
    out_full = lax.all_gather(w_out, "dp", axis=0, tiled=True)
    gate_full = lax.all_gather(w_gate, "dp", axis=0, tiled=True)
    up_full = lax.all_gather(w_up, "dp", axis=0, tiled=True)
    down_full = lax.all_gather(w_down, "dp", axis=0, tiled=True)
    gain_rows = qkv_full[:, own, : 2 * own].reshape(-1, 2, own).astype(F32)
    gain_rows = jnp.transpose(gain_rows, (1, 0, 2)).reshape(2, -1)
    gain_one, gain_two = gain_rows[0:1], gain_rows[1:2]

    x_full, cosine, sine, start_column, start_row = line_gather(
        inputs, rotary_freqs()[None], seq_lengths, group_perm, group_starts, count, 0
    )
    normed_full, queries, keys, values, mixed, lse, near = attend(
        x_full, qkv_full, gain_one, cosine, sine, start_column, cotangent,
        q_width, kv_width, count, 5,
    )
    replicas = lax.axis_size("dp")
    middle, normed_two_full = forward_turn(mixed, out_full, inputs, gain_two, count, 1)
    grad_full, active, gate_grad, up_grad, norm_two_grad, outputs = hidden_layer(
        normed_two_full, cotangent, near, middle, gate_full, up_full, down_full, count, 4
    )
    middle_grad, branch_full, gain_two_grad, sums, down_grad, gate_weight_grad, _ = backward_turn(
        norm_two_grad, cotangent, middle, gain_two, normed_two_full, gate_grad, up_grad, active,
        grad_full, count, replicas, 2,
    )
    sides = [list(range(side, replicas, 2)) for side in range(2)]
    up_weight_grad = lax.psum_scatter(
        sums, "dp", scatter_dimension=0, axis_index_groups=sides, tiled=True
    ).astype(F32)
    input_grad, out_grad, query_grad, key_grad, value_grad, gain_one_grad, gain_two_grad = last_turn(
        branch_full, out_full, mixed, queries, keys, values, lse, cosine, sine, start_row,
        qkv_full, normed_full, middle_grad, inputs, gain_one, gain_two_grad,
        (q_width, kv_width, kv_width), count, replicas, 3,
    )
    return (
        outputs,
        input_grad,
        gain_one_grad[0],
        query_grad,
        key_grad,
        value_grad,
        out_grad,
        gain_two_grad[0],
        gate_weight_grad,
        up_weight_grad,
        down_grad,
    )


def solution(mesh):
    in_specs = (
        P(("dp", "tensor"), None),
        P(("dp", "tensor"), None),
        P("dp"),
        P("dp", "tensor"),
        P("dp", "tensor"),
        P("dp", "tensor"),
        P(("tensor", "dp"), None),
        P("dp"),
        P("dp", "tensor"),
        P("dp", "tensor"),
        P(("tensor", "dp"), None),
        P(),
        P(),
        P(),
    )
    out_specs = (
        P(("dp", "tensor"), None),
        P(("dp", "tensor"), None),
        P("dp"),
        P("dp", "tensor"),
        P("dp", "tensor"),
        P("dp", "tensor"),
        P(("tensor", "dp"), None),
        P("dp"),
        P("dp", "tensor"),
        P("dp", "tensor"),
        P(("tensor", "dp"), None),
    )
    return jax.shard_map(shards, mesh=mesh, in_specs=in_specs, out_specs=out_specs, check_vma=False)
```

```python
import functools
import math

import jax
import jax.numpy as jnp
from jax import lax
from jax.experimental import pallas as pl
from jax.experimental.pallas import tpu as pltpu
from jax.sharding import PartitionSpec as P

HEAD_SIZE = 64
MOST_SEQS = 2
SLAB = 128
SPAN = 256
GAIN_ROWS = 16

norm_epsilon = 1e-05
rope_theta = 500000.0
rope_factor = 32.0
low_factor = 1.0
high_factor = 4.0
context_span = 8192.0
mask_fill = -1e30

F32 = jnp.float32
BF16 = jnp.bfloat16
VMEM_LIMIT = 60 * 1024 * 1024


def rotary_freqs():
    half = HEAD_SIZE // 2
    index = jnp.tile(jnp.arange(half, dtype=jnp.float32), SLAB // half)
    inverse = 1.0 / jnp.power(jnp.float32(rope_theta), 2.0 * index / HEAD_SIZE)
    wavelength = 2.0 * math.pi / inverse
    smooth = (context_span / wavelength - low_factor) / (high_factor - low_factor)
    blended = (1.0 - smooth) * inverse / rope_factor + smooth * inverse
    scaled = jnp.where(wavelength > context_span / low_factor, inverse / rope_factor, blended)
    return jnp.where(wavelength < context_span / high_factor, inverse, scaled)


def segment_starts(lengths_ref, perm_ref, starts_ref, rows):
    group = lax.axis_index("dp")
    opening, closing = starts_ref[group], starts_ref[group + 1]
    finish = jnp.int32(0)
    start = jnp.zeros_like(rows)
    for slot in range(MOST_SEQS):
        place = opening + slot
        sequence = perm_ref[jnp.minimum(place, perm_ref.shape[0] - 1)]
        finish = finish + jnp.where(place < closing, lengths_ref[sequence], 0)
        start = jnp.where(rows >= finish, finish, start)
    return start


def project(left, right):
    return jnp.dot(left, right, preferred_element_type=F32)


def project_back(left, right):
    return lax.dot_general(left, right, (((1,), (1,)), ((), ())), preferred_element_type=F32)


def row_contract(left, right):
    return lax.dot_general(left, right, (((0,), (0,)), ((), ())), preferred_element_type=F32)


def lanes(shape):
    return lax.broadcasted_iota(jnp.int32, shape, len(shape) - 1)


def turned(slab):
    half = HEAD_SIZE // 2
    ahead = pltpu.roll(slab, SLAB - half, 1)
    behind = pltpu.roll(slab, half, 1)
    return jnp.where(lanes(slab.shape) % HEAD_SIZE < half, ahead, behind)


def head_pair(slab):
    left = lanes(slab.shape) < HEAD_SIZE
    zero = jnp.zeros_like(slab)
    return jnp.concatenate([jnp.where(left, slab, zero), jnp.where(left, zero, slab)], axis=0)


def join_pair(stacked):
    half = stacked.shape[0] // 2
    left = lanes((half, SLAB)) < HEAD_SIZE
    return jnp.where(left, stacked[:half], stacked[half:])


def params(**kwargs):
    return pltpu.CompilerParams(vmem_limit_bytes=VMEM_LIMIT, **kwargs)


def vmem_specs(count):
    return [pl.BlockSpec(memory_space=pltpu.VMEM)] * count


def weight_fetches(packed, target, sems):
    rows = target.shape[0] // packed.shape[0]
    return [
        pltpu.make_async_copy(
            packed.at[block, :rows], target.at[block * rows : (block + 1) * rows], sems.at[block]
        )
        for block in range(packed.shape[0])
    ]


def attend_kernel(
    count, x_ref, packed_ref, gain_ref, cos_ref, sin_ref, start_ref, dy_ref,
    normed_ref, q_ref, k_ref, v_ref, mixed_ref, lse_ref, near_ref, bias_ref, stat_ref, w_ref, sems,
    near_send, near_receive,
):
    fetches = weight_fetches(packed_ref, w_ref, sems)
    for fetch in fetches:
        fetch.start()
    line = Line(count)
    line.barrier()
    gather = Gather(line, near_ref, near_send, near_receive, dy_ref.shape[0], 1)
    gather.start(0, dy_ref)
    for fetch in fetches:
        fetch.wait()
    rows_all = x_ref.shape[0]
    q_width = q_ref.shape[1]
    kv_slabs = v_ref.shape[0] // 2
    slabs = q_width // SLAB
    scale = HEAD_SIZE ** (-0.5)

    @pl.loop(0, rows_all // SPAN)
    def _(step):
        rows = pl.ds(step * SPAN, SPAN)
        x = x_ref[rows, :].astype(F32)
        inverse = lax.rsqrt(jnp.mean(x * x, axis=-1, keepdims=True) + norm_epsilon)
        normed = (x * inverse * gain_ref[...]).astype(BF16)
        normed_ref[rows, :] = normed
        pre = project(normed, w_ref[...])
        cosine, sine = cos_ref[rows, :], sin_ref[rows, :]
        for slab in range(slabs):
            part = pre[:, slab * SLAB : (slab + 1) * SLAB]
            part = (part * cosine + turned(part) * sine).astype(BF16)
            q_ref[rows, slab * SLAB : (slab + 1) * SLAB] = (part.astype(F32) * scale).astype(BF16)
        left = lanes((SPAN, SLAB)) < HEAD_SIZE
        for pair in range(kv_slabs):
            at = q_width + pair * SLAB
            key = pre[:, at : at + SLAB]
            key = key * cosine + turned(key) * sine
            at = at + kv_slabs * SLAB
            value = pre[:, at : at + SLAB]
            for ref, full in ((k_ref, key), (v_ref, value)):
                other = pltpu.roll(full, HEAD_SIZE, 1)
                ref[2 * pair, rows, :] = jnp.where(left, full, other).astype(BF16)
                ref[2 * pair + 1, rows, :] = jnp.where(left, other, full).astype(BF16)

    members = slabs // (2 * kv_slabs)
    for tile in range(rows_all // SPAN):
        first, span = tile * SPAN, (tile + 1) * SPAN
        columns = lanes((SPAN, span))
        row_ids = first + lax.broadcasted_iota(jnp.int32, (SPAN, span), 0)
        allowed = (columns >= start_ref[first : first + SPAN, :]) & (columns <= row_ids)
        bias_ref[:, :span] = jnp.where(allowed, 0.0, mask_fill)

        @pl.loop(0, slabs)
        def _(slab):
            at = pl.ds(pl.multiple_of(slab * SLAB, SLAB), SLAB)
            head = slab // members
            stacked = head_pair(q_ref[first : first + SPAN, at])
            scores = project_back(stacked, k_ref[head, :span, :])
            bias = bias_ref[:, :span]
            scores = scores + jnp.concatenate([bias, bias], axis=0)
            top = jnp.max(scores, axis=-1, keepdims=True)
            weights = jnp.exp(scores - top)
            total = jnp.sum(weights, axis=-1, keepdims=True)
            mixed = project(weights.astype(BF16), v_ref[head, :span, :]) / total
            mixed_ref[first : first + SPAN, at] = join_pair(mixed).astype(BF16)
            logs = top + jnp.log(total)
            old = stat_ref[first : first + SPAN, :]
            lane = lanes(old.shape)
            old = jnp.where(lane == 2 * slab, logs[:SPAN], old)
            stat_ref[first : first + SPAN, :] = jnp.where(lane == 2 * slab + 1, logs[SPAN:], old)

    lse_ref[...] = jnp.transpose(stat_ref[...])[: lse_ref.shape[0], :]
    for way in (0, 1):
        @pl.when(line.has[1 - way])
        def _(way=way):
            gather.copy(line.neighbour[1 - way], 0, way).wait_recv()

        @pl.when(line.has[way])
        def _(way=way):
            gather.copy(line.place, 0, way, dy_ref).wait_send()


def attend(
    x_full, w_qkv, gain, cosine, sine, start, dy, q_width, kv_width, count, collective_id
):
    rows = x_full.shape[0]
    heads = 2 * (kv_width // SLAB)
    hbm = pl.BlockSpec(memory_space=pl.ANY)
    flops = 2 * rows * x_full.shape[1] * (q_width + 2 * kv_width) + 8 * rows * rows * q_width
    return pl.pallas_call(
        functools.partial(attend_kernel, count),
        out_shape=(
            jax.ShapeDtypeStruct(x_full.shape, BF16),
            jax.ShapeDtypeStruct((rows, q_width), BF16),
            jax.ShapeDtypeStruct((heads, rows, SLAB), BF16),
            jax.ShapeDtypeStruct((heads, rows, SLAB), BF16),
            jax.ShapeDtypeStruct((rows, q_width), BF16),
            jax.ShapeDtypeStruct((q_width // HEAD_SIZE, rows), F32),
            jax.ShapeDtypeStruct(x_full.shape, BF16),
        ),
        in_specs=vmem_specs(1) + [hbm] + vmem_specs(4) + [hbm],
        out_specs=tuple(vmem_specs(6)) + (hbm,),
        scratch_shapes=[
            pltpu.VMEM((SPAN, rows), F32),
            pltpu.VMEM((rows, SLAB), F32),
            pltpu.VMEM((x_full.shape[1], w_qkv.shape[2]), BF16),
            pltpu.SemaphoreType.DMA((w_qkv.shape[0],)),
            copy_sems(count, 1), copy_sems(count, 1),
        ],
        compiler_params=params(collective_id=collective_id, has_side_effects=True),
        cost_estimate=pl.CostEstimate(flops=flops, bytes_accessed=1 << 24, transcendentals=1 << 23),
        name="attend",
    )(x_full, w_qkv, gain, cosine, sine, start, dy)


SUBS = 4
BLOCK = 1024


class Line:
    def __init__(self, count):
        self.count = count
        self.place = lax.axis_index("tensor")
        self.has = (self.place < count - 1, self.place > 0)
        self.neighbour = (self.place + 1, self.place - 1)
        other = count - 1 - self.place
        self.lag = jnp.where(self.place > other, self.place, other)

    def greet(self, semaphore):
        for way in (0, 1):
            @pl.when(self.has[way])
            def _(way=way):
                pl.semaphore_signal(semaphore, 1, device_id={"tensor": self.neighbour[way]})
        ends = (self.place == 0) | (self.place == self.count - 1)
        return jnp.where(ends, 1, 2)

    def barrier(self):
        semaphore = pltpu.get_barrier_semaphore()
        pl.semaphore_wait(semaphore, self.greet(semaphore))

    def copy(self, source, target, send, receive, way):
        return pltpu.make_async_remote_copy(
            src_ref=source, dst_ref=target, send_sem=send, recv_sem=receive,
            device_id={"tensor": self.neighbour[way]},
        )


class Gather:
    def __init__(
        self, line, full, send, receive, chunk_rows, pieces, lags=None, near=0, late=True
    ):
        self.line, self.full, self.send, self.receive = line, full, send, receive
        self.chunk_rows, self.size, self.pieces = chunk_rows, chunk_rows // pieces, pieces
        self.lags, self.near, self.late = lags or [0] * line.count, near, late

    def rows(self, chunk, piece):
        start = chunk * self.chunk_rows + piece * self.size
        return pl.ds(pl.multiple_of(start, self.size), self.size)

    def copy(self, chunk, piece, way, source=None):
        target = self.full.at[self.rows(chunk, piece)]
        return self.line.copy(
            target if source is None else source, target,
            self.send.at[way, chunk, piece], self.receive.at[way, chunk, piece], way,
        )

    def start(self, piece, source=None):
        for way in (0, 1):
            @pl.when(self.line.has[way])
            def _(way=way):
                self.copy(self.line.place, piece, way, source).start()

    def start_near(self, piece, source):
        line = self.line
        for way, chunk in ((0, line.place - 1), (1, line.place + 1)):
            @pl.when(line.has[0] & line.has[1])
            def _(way=way, chunk=chunk):
                self.copy(chunk, piece, way, source.at[self.rows(chunk, piece)]).start()

    def turn(self, turn):
        line = self.line
        for chunk in range(line.count):
            for way in (0, 1):
                hop = (line.place - chunk if way == 0 else chunk - line.place) - self.near
                piece = turn - self.lags[chunk] - hop

                @pl.when((hop > 0) & (piece >= 0) & (piece < self.pieces))
                def _(way=way, chunk=chunk, piece=piece):
                    if not self.late:
                        self.copy(chunk, piece, way).wait_recv()

                    @pl.when(line.has[way])
                    def _():
                        if self.late:
                            self.copy(chunk, piece, way).wait_recv()
                        self.copy(chunk, piece, way).start()

    def finish(self, source=None):
        line = self.line

        @pl.loop(0, self.pieces)
        def _(piece):
            for chunk in range(line.count if self.late else 0):
                for way, end in ((0, line.count - 1), (1, 0)):
                    hop = line.place - chunk if way == 0 else chunk - line.place

                    @pl.when((line.place == end) & (hop > self.near))
                    def _(way=way, chunk=chunk):
                        self.copy(chunk, piece, way).wait_recv()

            for chunk in range(line.count):
                @pl.when(line.has[0] & (chunk <= line.place - self.near))
                def _(chunk=chunk):
                    self.copy(chunk, piece, 0, source).wait_send()

                @pl.when(line.has[1] & (chunk >= line.place + self.near))
                def _(chunk=chunk):
                    self.copy(chunk, piece, 1, source).wait_send()


class Scatter:
    def __init__(self, line, partial, landing, send, receive, chunk_rows, pieces):
        self.line, self.partial, self.landing = line, partial, landing
        self.send, self.receive = send, receive
        self.chunk_rows, self.size, self.pieces = chunk_rows, chunk_rows // pieces, pieces
        self.lag = line.lag

    def rows(self, chunk, piece):
        start = chunk * self.chunk_rows + piece * self.size
        return pl.ds(pl.multiple_of(start, self.size), self.size)

    def landed(self, chunk, piece, way, owner):
        if way == 1:
            chunk = jnp.where(chunk == owner, self.line.count, chunk)
        return self.rows(chunk, piece)

    def copy(self, chunk, piece, way, owner=None):
        owner = self.line.neighbour[way] if owner is None else owner
        return self.line.copy(
            self.partial.at[self.rows(chunk, piece)],
            self.landing.at[self.landed(chunk, piece, way, owner)],
            self.send.at[way, chunk, piece], self.receive.at[way, chunk, piece], way,
        )

    def wait(self, chunk, piece, way):
        self.copy(chunk, piece, way, self.line.place).wait_recv()

    def forward(self, piece, way):
        line = self.line
        for step in range(line.count - 1):
            chunk = line.count - 1 - step if way == 0 else step
            beyond = chunk > line.place if way == 0 else chunk < line.place

            @pl.when(beyond)
            def _(chunk=chunk):
                @pl.when(line.has[1 - way])
                def _():
                    self.wait(chunk, piece, way)
                    rows = self.rows(chunk, piece)
                    total = self.partial[rows, :].astype(F32)
                    total = total + self.landing[rows, :].astype(F32)
                    self.partial[rows, :] = total.astype(BF16)

                self.copy(chunk, piece, way).start()

    def turn(self, turn):
        line = self.line
        for way, lag in ((0, line.place), (1, line.count - 1 - line.place)):
            piece = turn - lag

            @pl.when((piece >= 0) & (piece < self.pieces))
            def _(way=way, piece=piece):
                self.forward(piece, way)

    def settle(self, turn, use):
        piece = turn - self.lag

        @pl.when((piece >= 0) & (piece < self.pieces))
        def _():
            for way in (0, 1):
                @pl.when(self.line.has[1 - way])
                def _(way=way):
                    self.wait(self.line.place, piece, way)
            use(piece)

    def total(self, piece):
        place = self.line.place
        total = self.partial[self.rows(place, piece), :].astype(F32)
        for way in (0, 1):
            got = self.landing[self.landed(place, piece, way, place), :].astype(F32)
            total = total + jnp.where(self.line.has[1 - way], got, 0.0)
        return total

    def finish(self):
        line = self.line

        @pl.loop(0, self.pieces)
        def _(piece):
            for chunk in range(line.count):
                @pl.when(chunk > line.place)
                def _(chunk=chunk):
                    self.copy(chunk, piece, 0).wait_send()

                @pl.when(chunk < line.place)
                def _(chunk=chunk):
                    self.copy(chunk, piece, 1).wait_send()


class Stream(Scatter):
    def __init__(self, line, partial, landing, send, receive, chunk_rows, pieces, offset, hop):
        super().__init__(line, partial, landing, send, receive, chunk_rows, pieces)
        self.offset, self.hop = offset, hop
        count = line.count
        self.lag = 0
        for place in range(count):
            up = (count - 1 - place) * pieces + hop * place
            down = (count - 2 - place) * pieces + offset + hop * (count - 1 - place)
            late = max(up if place > 0 else 0, down if place < count - 1 else 0)
            self.lag = self.lag + jnp.where(line.place == place, late, 0)
        self.turns = (count - 1) * (pieces + hop) + offset

    def turn(self, turn):
        line, pieces = self.line, self.pieces
        last = line.count - 1
        lags = (self.hop * line.place, self.offset + self.hop * (last - line.place))
        for way, lag in enumerate(lags):
            since = turn - lag
            piece = since % pieces
            chunk = last - way - since // pieces
            beyond = chunk > line.place if way == 0 else chunk < line.place

            @pl.when((since >= 0) & (since < last * pieces) & beyond)
            def _(way=way, piece=piece, chunk=chunk):
                @pl.when(line.has[1 - way])
                def _():
                    self.wait(chunk, piece, way)
                    rows = self.rows(chunk, piece)
                    total = self.partial[rows, :].astype(F32)
                    total = total + self.landing[rows, :].astype(F32)
                    self.partial[rows, :] = total.astype(BF16)

                self.copy(chunk, piece, way).start()


class Fold:
    def __init__(self, replicas, sums, traded, arrived, pair_sems, sends, receives):
        self.halves = replicas // 2
        self.sums, self.traded, self.arrived = sums, traded, arrived
        self.pair_sems, self.sends, self.receives = pair_sems, sends, receives
        replica = lax.axis_index("dp")
        self.side, self.mine = replica % 2, replica // 2
        self.partner = replica + 1 - 2 * self.side

    def greet(self, semaphore):
        pl.semaphore_signal(semaphore, 1, device_id={"dp": self.partner})
        for step in range(1, self.halves):
            peer = 2 * ((self.mine + step) % self.halves) + self.side
            pl.semaphore_signal(semaphore, 1, device_id={"dp": peer})
        return self.halves

    def pair(self):
        return pltpu.make_async_remote_copy(
            src_ref=self.sums.at[:, 1 - self.side], dst_ref=self.traded,
            send_sem=self.pair_sems.at[0], recv_sem=self.pair_sems.at[1],
            device_id={"dp": self.partner},
        )

    def peer(self, half, landing):
        return pltpu.make_async_remote_copy(
            src_ref=self.sums.at[half, self.side], dst_ref=self.arrived.at[landing],
            send_sem=self.sends.at[half], recv_sem=self.receives.at[landing],
            device_id={"dp": 2 * half + self.side},
        )

    def others(self):
        return [(self.mine + step) % self.halves for step in range(1, self.halves)]

    def spread(self):
        self.pair().wait_recv()

        @pl.loop(0, self.halves)
        def _(half):
            total = self.sums[half, self.side].astype(F32) + self.traded[half].astype(F32)
            self.sums[half, self.side] = total.astype(BF16)

        for half in self.others():
            self.peer(half, self.mine).start()

    def total(self):
        total = self.sums[self.mine, self.side].astype(F32)
        for half in self.others():
            self.peer(half, half).wait_recv()
            total = total + self.arrived[half].astype(F32)
        return total

    def finish(self):
        self.pair().wait_send()
        for half in self.others():
            self.peer(half, self.mine).wait_send()


def fold_scratch(replicas, rows, width):
    halves = replicas // 2
    return [
        pltpu.VMEM((halves, 2, rows, width), BF16),
        pltpu.VMEM((halves, rows, width), BF16),
        pltpu.VMEM((halves, rows, width), BF16),
        pltpu.SemaphoreType.DMA((2,)),
        pltpu.SemaphoreType.DMA((halves,)),
        pltpu.SemaphoreType.DMA((halves,)),
    ]


def landing_rows(count, chunk_rows):
    return (count + 1) * chunk_rows


def copy_sems(count, pieces):
    return pltpu.SemaphoreType.DMA((2, count, pieces))


def settle_lags(count):
    return [max(place, count - 1 - place) for place in range(count)]


def gather_kernel(
    count, replicas, pieces, x_ref, freqs_ref, out_ref, lengths_ref, perm_ref, starts_ref,
    full_ref, cos_ref, sin_ref, column_ref, row_ref, out_full_ref, send, receive, local,
    deal_send, deal_receive,
):
    line = Line(count)
    chunk_rows = x_ref.shape[0]
    own = pl.ds(pl.multiple_of(line.place * chunk_rows, chunk_rows), chunk_rows)
    keep = pltpu.make_async_copy(x_ref, full_ref.at[own], local.at[0])
    keep.start()
    replica = lax.axis_index("dp")
    peers = [(replica + step) % replicas for step in range(1, replicas)]
    out_rows = out_ref.shape[0]

    def out_at(owner):
        return out_full_ref.at[pl.ds(pl.multiple_of(owner * out_rows, out_rows), out_rows)]

    def deal(peer, owner):
        return pltpu.make_async_remote_copy(
            src_ref=out_ref, dst_ref=out_at(owner), send_sem=deal_send.at[peer],
            recv_sem=deal_receive.at[owner], device_id={"dp": peer},
        )

    keep_out = pltpu.make_async_copy(out_ref, out_at(replica), local.at[1])
    keep_out.start()
    semaphore = pltpu.get_barrier_semaphore()
    for peer in peers:
        pl.semaphore_signal(semaphore, 1, device_id={"dp": peer})
    pl.semaphore_wait(semaphore, line.greet(semaphore) + replicas - 1)
    for peer in peers:
        deal(peer, replica).start()
    gather = Gather(line, full_ref, send, receive, chunk_rows, pieces)
    for piece in range(pieces):
        gather.start(piece, x_ref.at[gather.rows(0, piece)])
    row_ref[...] = segment_starts(lengths_ref, perm_ref, starts_ref, lanes(row_ref.shape))
    size = count * chunk_rows // pieces

    @pl.loop(1, pieces + count - 1)
    def _(turn):
        gather.turn(turn)

        @pl.when(turn <= pieces)
        def _():
            first = pl.multiple_of((turn - 1) * size, size)
            rows = first + lax.broadcasted_iota(jnp.int32, (size, SLAB), 0)
            start = segment_starts(lengths_ref, perm_ref, starts_ref, rows)
            angles = (rows - start).astype(F32) * freqs_ref[...]
            low_half = lanes(rows.shape) % HEAD_SIZE < HEAD_SIZE // 2
            sines = jnp.sin(angles)
            cos_ref[pl.ds(first, size), :] = jnp.cos(angles)
            sin_ref[pl.ds(first, size), :] = jnp.where(low_half, -sines, sines)
            column_ref[pl.ds(first, size), :] = start[:, 0:1]

    gather.finish(x_ref.at[gather.rows(0, 0)])
    for peer in peers:
        deal(peer, peer).wait_recv()
        deal(peer, replica).wait_send()
    keep.wait()
    keep_out.wait()


def line_gather(
    x, freqs, w_out, lengths, perm, starts, count, replicas, collective_id, pieces=8
):
    rows, width = x.shape
    total = count * rows
    hbm = pl.BlockSpec(memory_space=pl.ANY)
    return pl.pallas_call(
        functools.partial(gather_kernel, count, replicas, pieces),
        out_shape=(
            jax.ShapeDtypeStruct((total, width), x.dtype),
            jax.ShapeDtypeStruct((total, SLAB), F32),
            jax.ShapeDtypeStruct((total, SLAB), F32),
            jax.ShapeDtypeStruct((total, 1), jnp.int32),
            jax.ShapeDtypeStruct((1, total), jnp.int32),
            jax.ShapeDtypeStruct((replicas * w_out.shape[0], w_out.shape[1]), w_out.dtype),
        ),
        in_specs=vmem_specs(2) + [hbm] + [pl.BlockSpec(memory_space=pltpu.SMEM)] * 3,
        out_specs=(hbm,) + tuple(vmem_specs(4)) + (hbm,),
        scratch_shapes=[
            copy_sems(count, pieces), copy_sems(count, pieces), pltpu.SemaphoreType.DMA((2,)),
            pltpu.SemaphoreType.DMA((replicas,)), pltpu.SemaphoreType.DMA((replicas,)),
        ],
        compiler_params=params(collective_id=collective_id, has_side_effects=True),
        cost_estimate=pl.CostEstimate(
            flops=0, bytes_accessed=200 * rows * width, transcendentals=0
        ),
        name="line_gather",
    )(x, freqs, w_out, lengths, perm, starts)


def forward_turn_kernel(
    count, pieces, mixed_ref, w_ref, x_ref, gain_ref, middle_ref, full_ref,
    partial, landing, rs_send, rs_receive, ag_send, ag_receive,
):
    line = Line(count)
    chunk_rows = x_ref.shape[0]
    line.barrier()

    @pl.loop(0, partial.shape[0] // SPAN)
    def _(step):
        rows = pl.ds(pl.multiple_of(step * SPAN, SPAN), SPAN)
        partial[rows, :] = project(mixed_ref[rows, :], w_ref[...]).astype(BF16)

    scatter = Scatter(line, partial, landing, rs_send, rs_receive, chunk_rows, pieces)
    gather = Gather(
        line, full_ref, ag_send, ag_receive, chunk_rows, pieces, settle_lags(count)
    )
    size = chunk_rows // pieces

    def settle(piece):
        local = pl.ds(pl.multiple_of(piece * size, size), size)
        middle = x_ref[local, :].astype(F32) + scatter.total(piece)
        middle_ref[local, :] = middle
        inverse = lax.rsqrt(jnp.mean(middle * middle, axis=-1, keepdims=True) + norm_epsilon)
        normed = (middle * inverse * gain_ref[...]).astype(BF16)
        full_ref[gather.rows(line.place, piece), :] = normed
        gather.start(piece)

    @pl.loop(0, pieces + 2 * (count - 1))
    def _(turn):
        scatter.turn(turn)
        gather.turn(turn)
        scatter.settle(turn, settle)

    scatter.finish()
    gather.finish()


def forward_turn(mixed, w_out, x, gain, count, collective_id, pieces=16):
    chunk_rows, width = x.shape
    rows = count * chunk_rows
    return pl.pallas_call(
        functools.partial(forward_turn_kernel, count, pieces),
        out_shape=(
            jax.ShapeDtypeStruct((chunk_rows, width), F32),
            jax.ShapeDtypeStruct((rows, width), BF16),
        ),
        in_specs=vmem_specs(4),
        out_specs=tuple(vmem_specs(2)),
        scratch_shapes=[
            pltpu.VMEM((rows, width), BF16),
            pltpu.VMEM((landing_rows(count, chunk_rows), width), BF16),
        ]
        + [copy_sems(count, pieces)] * 4,
        compiler_params=params(collective_id=collective_id, has_side_effects=True),
        cost_estimate=pl.CostEstimate(
            flops=2 * rows * width * mixed.shape[1],
            bytes_accessed=300 * chunk_rows * width, transcendentals=0,
        ),
        name="forward_turn",
    )(mixed, w_out, x, gain)


def hidden_kernel(
    count, pieces, normed_ref, own_ref, near_ref, middle_ref, gate_ref, up_ref, down_ref,
    full_ref, active_ref, gate_grad_ref, up_grad_ref, back_ref, out_ref,
    gate, up, down, normed, dy, active, slope, value, up_grad, back,
    partial, landing, rs_send, rs_receive, ag_send, ag_receive, loads, stores,
):
    line = Line(count)
    chunk_rows = own_ref.shape[0]
    hidden = gate_ref.shape[1]
    width = gate_ref.shape[0]
    sub = chunk_rows // SUBS
    fetches = [
        pltpu.make_async_copy(source, target, loads.at[at])
        for at, (source, target) in enumerate(
            ((normed_ref, normed), (gate_ref, gate), (up_ref, up), (down_ref, down))
        )
    ]
    for fetch in fetches:
        fetch.start()
    line.barrier()
    gather = Gather(
        line, dy, ag_send, ag_receive, chunk_rows, SUBS, near=1, late=False
    )
    scatter = Scatter(line, partial, landing, rs_send, rs_receive, chunk_rows, pieces)
    for piece in range(SUBS):
        gather.start_near(piece, near_ref)

    def chunk_at(chunk):
        return pl.ds(pl.multiple_of(chunk * chunk_rows, chunk_rows), chunk_rows)

    def place_near(way):
        rows = chunk_at(line.neighbour[way])
        return pltpu.make_async_copy(near_ref.at[rows], dy.at[rows], loads.at[5 + way])

    place_own = pltpu.make_async_copy(own_ref, dy.at[chunk_at(line.place)], loads.at[4])
    place_own.start()
    for way in (0, 1):
        @pl.when(line.has[way])
        def _(way=way):
            place_near(way).start()
    gate_grad = active
    outs = ((active, active_ref), (gate_grad, gate_grad_ref), (up_grad, up_grad_ref),
            (back, back_ref))

    def store(which, step):
        source, target = outs[which]
        rows = pl.ds(pl.multiple_of(step * sub, sub), sub)
        return pltpu.make_async_copy(source, target.at[:, rows], stores.at[which])

    def rows_of(chunk, step):
        return pl.ds(pl.multiple_of(chunk * chunk_rows + step * sub, sub), sub)

    def picked(ref, step, at=slice(None)):
        return jnp.concatenate([ref[rows_of(chunk, step), at] for chunk in range(count)], axis=0)

    def put(ref, at, rows):
        for chunk in range(count):
            ref[chunk, :, at] = rows[chunk * sub : (chunk + 1) * sub]

    def whole(ref):
        return jnp.concatenate([ref[chunk] for chunk in range(count)], axis=0)

    def settle(piece):
        size = chunk_rows // pieces
        local = pl.ds(pl.multiple_of(piece * size, size), size)
        out_ref[local, :] = (middle_ref[local, :] + scatter.total(piece)).astype(BF16)

    def exchange(turn):
        scatter.turn(turn)
        gather.turn(turn)
        scatter.settle(turn, settle)

    for at in range(3):
        fetches[at].wait()

    @pl.loop(0, SUBS)
    def _(step):
        @pl.when(step > 0)
        def _():
            store(0, step - 1).wait()

        @pl.loop(0, hidden // BLOCK)
        def _(block):
            at = pl.ds(pl.multiple_of(block * BLOCK, BLOCK), BLOCK)
            source = picked(normed, step)
            gate_pre = project(source, gate[:, at])
            up_pre = project(source, up[:, at])
            chance = 1.0 / (1.0 + jnp.exp(-gate_pre))
            silu = gate_pre * chance
            put(active, at, (silu * up_pre).astype(BF16))
            put(value.at[step], at, silu.astype(BF16))
            raised = up_pre * chance * (1.0 + gate_pre * (1.0 - chance))
            put(slope.at[step], at, raised.astype(BF16))

        store(0, step).start()

        @pl.when(step == 0)
        def _():
            fetches[3].wait()

        @pl.loop(0, width // BLOCK)
        def _(block):
            at = pl.ds(pl.multiple_of(block * BLOCK, BLOCK), BLOCK)
            product = project(whole(active), down[:, at]).astype(BF16)
            for chunk in range(count):
                partial[rows_of(chunk, step), at] = product[chunk * sub : (chunk + 1) * sub]

        exchange(step)

    @pl.loop(0, SUBS)
    def _(step):
        @pl.when(step == 0)
        def _():
            store(0, SUBS - 1).wait()
            place_own.wait()
            for way in (0, 1):
                @pl.when(line.has[way])
                def _(way=way):
                    place_near(way).wait()

        @pl.when(step > 0)
        def _():
            for which in (1, 2, 3):
                store(which, step - 1).wait()

        @pl.loop(0, hidden // BLOCK)
        def _(block):
            at = pl.ds(pl.multiple_of(block * BLOCK, BLOCK), BLOCK)
            active_grad = project_back(picked(dy, step), down[at, :])
            for chunk in range(count):
                grad = active_grad[chunk * sub : (chunk + 1) * sub]
                here = (grad * slope[step, chunk, :, at].astype(F32)).astype(BF16)
                gate_grad[chunk, :, at] = here
                here = (grad * value[step, chunk, :, at].astype(F32)).astype(BF16)
                up_grad[chunk, :, at] = here

        for which in (1, 2):
            store(which, step).start()
        exchange(SUBS + 2 * step)

        @pl.loop(0, width // BLOCK)
        def _(block):
            at = pl.ds(pl.multiple_of(block * BLOCK, BLOCK), BLOCK)
            total = project_back(whole(gate_grad), gate[at, :])
            total = total + project_back(whole(up_grad), up[at, :])
            put(back, at, total.astype(BF16))

        store(3, step).start()
        exchange(SUBS + 2 * step + 1)

    keep = pltpu.make_async_copy(dy, full_ref, loads.at[0])
    keep.start()

    @pl.loop(3 * SUBS, pieces + count - 1)
    def _(turn):
        exchange(turn)

    for which in (1, 2, 3):
        store(which, SUBS - 1).wait()
    keep.wait()
    scatter.finish()
    gather.finish()


def hidden_layer(
    normed, own, near, middle, w_gate, w_up, w_down, count, collective_id, pieces=8
):
    chunk_rows, width = own.shape
    hidden = w_gate.shape[1]
    rows = count * chunk_rows
    sub = chunk_rows // SUBS
    tall = jax.ShapeDtypeStruct((count, chunk_rows, hidden), BF16)
    hbm = pl.BlockSpec(memory_space=pl.ANY)
    outs = pl.pallas_call(
        functools.partial(hidden_kernel, count, pieces),
        out_shape=(
            jax.ShapeDtypeStruct((rows, width), BF16), tall, tall, tall,
            jax.ShapeDtypeStruct((count, chunk_rows, width), BF16),
            jax.ShapeDtypeStruct((chunk_rows, width), BF16),
        ),
        in_specs=[hbm] * 3 + vmem_specs(1) + [hbm] * 3,
        out_specs=(hbm, hbm, hbm, hbm, hbm, vmem_specs(1)[0]),
        scratch_shapes=[
            pltpu.VMEM((width, hidden), BF16),
            pltpu.VMEM((width, hidden), BF16),
            pltpu.VMEM((hidden, width), BF16),
            pltpu.VMEM((rows, width), BF16),
            pltpu.VMEM((rows, width), BF16),
            pltpu.VMEM((count, sub, hidden), BF16),
            pltpu.VMEM((SUBS, count, sub, hidden), BF16),
            pltpu.VMEM((SUBS, count, sub, hidden), BF16),
            pltpu.VMEM((count, sub, hidden), BF16),
            pltpu.VMEM((count, sub, width), BF16),
            pltpu.VMEM((rows, width), BF16),
            pltpu.VMEM((landing_rows(count, chunk_rows), width), BF16),
            copy_sems(count, pieces), copy_sems(count, pieces),
            copy_sems(count, SUBS), copy_sems(count, SUBS),
            pltpu.SemaphoreType.DMA((7,)), pltpu.SemaphoreType.DMA((4,)),
        ],
        compiler_params=params(collective_id=collective_id, has_side_effects=True),
        cost_estimate=pl.CostEstimate(
            flops=12 * rows * width * hidden, bytes_accessed=1 << 26, transcendentals=rows * hidden
        ),
        name="hidden_layer",
    )(normed, own, near, middle, w_gate, w_up, w_down)
    return [outs[0]] + [out.reshape(rows, out.shape[-1]) for out in outs[1:5]] + [outs[5]]


def backward_turn_kernel(
    count, pieces, given_ref, dy_ref, middle_ref, gain_ref,
    normed_full_ref, gate_grad_ref, up_grad_ref, active_ref, dy_full_ref,
    grad_ref, full_ref, gain_grad_ref, sums_ref, down_grad_ref, gate_out_ref, traded_ref,
    partial, landing, tiles, traded, normed, gate_grad, active, dy_full, kept, arrived,
    arrived_two, summed, rs_send, rs_receive, ag_send, ag_receive, load, trade_send, trade_receive, fetches, stores,
    peer_send, peer_receive, operands, summed_out,
):
    line = Line(count)
    chunk_rows = dy_ref.shape[0]
    fetch = pltpu.make_async_copy(given_ref, partial, load)
    fetch.start()
    brought = [
        pltpu.make_async_copy(source, target, operands.at[at])
        for at, (source, target) in enumerate((
            (active_ref, active), (dy_full_ref, dy_full), (normed_full_ref, normed),
            (gate_grad_ref, gate_grad), (up_grad_ref, active),
        ))
    ]
    for copy in brought[:4]:
        copy.start()
    replica = lax.axis_index("dp")
    side, mine = replica % 2, replica // 2
    partner = replica + 1 - 2 * side
    halves = kept.shape[0] // traded.shape[0]
    others = [(mine + step) % halves for step in range(1, halves)]
    semaphore = pltpu.get_barrier_semaphore()
    pl.semaphore_signal(semaphore, 1, device_id={"dp": partner})
    for half in others:
        pl.semaphore_signal(semaphore, 1, device_id={"dp": 2 * half + side})
    pl.semaphore_wait(semaphore, line.greet(semaphore) + halves)
    fetch.wait()
    scatter = Scatter(line, partial, landing, rs_send, rs_receive, chunk_rows, pieces)
    gather = Gather(
        line, full_ref, ag_send, ag_receive, chunk_rows, pieces, settle_lags(count)
    )
    size = chunk_rows // pieces
    gain_grad_ref[...] = jnp.zeros_like(gain_grad_ref)

    def settle(piece):
        local = pl.ds(pl.multiple_of(piece * size, size), size)
        grad, gain_grad = norm_back(scatter.total(piece), middle_ref[local, :], gain_ref[...])
        grad = grad + dy_ref[local, :].astype(F32)
        gain_grad_ref[...] += gain_grad
        grad_ref[local, :] = grad
        full_ref[gather.rows(line.place, piece), :] = grad.astype(BF16)
        gather.start(piece)

    block = traded.shape[0]
    width = traded.shape[1]
    products = ((active, dy_full), (normed, gate_grad), (normed, active))
    needed = ((0, 1), (2, 3), (4,))
    pairs = halves * len(products)
    theirs = pl.ds(pl.multiple_of((1 - side) * block, block), block)
    ours = pl.ds(pl.multiple_of(side * block, block), block)

    def trade(pair):
        return pltpu.make_async_remote_copy(
            src_ref=tiles.at[pair % 2, theirs], dst_ref=traded_ref.at[pair],
            send_sem=trade_send.at[pair], recv_sem=trade_receive.at[pair],
            device_id={"dp": partner},
        )

    def bring(pair):
        return pltpu.make_async_copy(traded_ref.at[pair], traded, fetches)

    def put(pair):
        rows = pl.ds(pl.multiple_of((pair % halves) * block, block), block)
        return pltpu.make_async_copy(
            tiles.at[pair % 2, ours], sums_ref.at[rows], stores.at[pair % 2]
        )

    folds = ((kept, arrived), (dy_full, arrived_two))

    def kept_rows(half):
        return pl.ds(pl.multiple_of(half * block, block), block)

    def peer(which, half, slot):
        source, landing = folds[which]
        return pltpu.make_async_remote_copy(
            src_ref=source.at[kept_rows(half)], dst_ref=landing.at[slot],
            send_sem=peer_send.at[which, half], recv_sem=peer_receive.at[which, slot],
            device_id={"dp": 2 * half + side},
        )

    def slot_of(sender, owner):
        return (sender - owner + halves - 1) % halves

    def beside(pair):
        @pl.when((pair >= 2) & (pair < pairs))
        def _():
            trade(pair - 2).wait_send()

            @pl.when(pair - 2 >= 2 * halves)
            def _():
                put(pair - 2).wait()

        @pl.when((pair >= 1) & (pair <= pairs))
        def _():
            trade(pair - 1).wait_recv()
            bring(pair - 1).start()

        at = pl.ds(pl.multiple_of((pair % halves) * 2 * block, 2 * block), 2 * block)
        for which, (left, right) in enumerate(products):
            @pl.when(pair == which * halves)
            def _(which=which):
                for operand in needed[which]:
                    brought[operand].wait()
                if which == 1:
                    brought[4].start()

            @pl.when(pair // halves == which)
            def _(left=left, right=right):
                tiles[pair % 2] = row_contract(left[:, at], right[...]).astype(BF16)

        @pl.when(pair < pairs)
        def _():
            trade(pair).start()

        @pl.when((pair >= 1) & (pair <= pairs))
        def _():
            last = pair - 1
            bring(last).wait()
            slot = last % 2
            total = tiles[slot, ours].astype(F32) + traded[...].astype(F32)

            for which in range(2):
                @pl.when(last // halves == which)
                def _(which=which):
                    half = last % halves
                    folds[which][0][kept_rows(half), :] = total.astype(BF16)

                    @pl.when(half != mine)
                    def _():
                        peer(which, half, slot_of(mine, half)).start()

            @pl.when(last >= 2 * halves)
            def _():
                tiles[slot, ours] = total.astype(BF16)
                put(last).start()

    def add_up(which):
        total = folds[which][0][kept_rows(mine), :].astype(F32)
        for half in others:
            slot = slot_of(half, mine)
            peer(which, half, slot).wait_recv()
            total = total + folds[which][1][slot].astype(F32)
        summed[...] = total
        for half in others:
            peer(which, half, slot_of(mine, half)).wait_send()

    def hand_out(which):
        return pltpu.make_async_copy(summed, (down_grad_ref, gate_out_ref)[which], summed_out)

    turns = max(pieces + 2 * (count - 1), pairs + 1)

    @pl.loop(0, turns)
    def _(turn):
        scatter.turn(turn)
        gather.turn(turn)
        scatter.settle(turn, settle)
        beside(turn)

        @pl.when(turn == turns - 1)
        def _():
            add_up(0)
            hand_out(0).start()

    for pair in range(pairs - 2, pairs):
        trade(pair).wait_send()
        put(pair).wait()
    hand_out(0).wait()
    add_up(1)
    hand_out(1).start()
    scatter.finish()
    gather.finish()
    hand_out(1).wait()


def norm_back(grad, rows, gain):
    inverse = lax.rsqrt(jnp.mean(rows * rows, axis=-1, keepdims=True) + norm_epsilon)
    scaled = grad * gain
    common = jnp.mean(scaled * rows, axis=-1, keepdims=True) * (inverse * inverse * inverse)
    gain_grad = jnp.sum(grad * (rows * inverse), axis=0, keepdims=True)
    return inverse * scaled - rows * common, gain_grad


def backward_turn(
    given, dy, middle, gain, normed_full, gate_grad, up_grad, active, dy_full,
    count, replicas, collective_id, pieces=16,
):
    chunk_rows, width = dy.shape
    rows = count * chunk_rows
    block = width // replicas
    kept_rows = width // 2
    pairs = 3 * kept_rows // block
    hbm = pl.BlockSpec(memory_space=pl.ANY)
    return pl.pallas_call(
        functools.partial(backward_turn_kernel, count, pieces),
        out_shape=(
            jax.ShapeDtypeStruct((chunk_rows, width), F32),
            jax.ShapeDtypeStruct((rows, width), BF16),
            jax.ShapeDtypeStruct((1, width), F32),
            jax.ShapeDtypeStruct((kept_rows, width), BF16),
            jax.ShapeDtypeStruct((block, width), F32),
            jax.ShapeDtypeStruct((block, width), F32),
            jax.ShapeDtypeStruct((pairs, block, width), BF16),
        ),
        in_specs=[hbm] + vmem_specs(3) + [hbm] * 5,
        out_specs=tuple(vmem_specs(3)) + (hbm,) * 4,
        scratch_shapes=[
            pltpu.VMEM((rows, width), BF16),
            pltpu.VMEM((landing_rows(count, chunk_rows), width), BF16),
            pltpu.VMEM((2, 2 * block, width), BF16),
            pltpu.VMEM((block, width), BF16),
        ]
        + [pltpu.VMEM((rows, width), BF16)] * 4
        + [pltpu.VMEM((kept_rows, width), BF16)]
        + [pltpu.VMEM((replicas // 2 - 1, block, width), BF16)] * 2
        + [pltpu.VMEM((block, width), F32)]
        + [copy_sems(count, pieces)] * 4
        + [
            pltpu.SemaphoreType.DMA,
            pltpu.SemaphoreType.DMA((pairs,)),
            pltpu.SemaphoreType.DMA((pairs,)),
            pltpu.SemaphoreType.DMA,
            pltpu.SemaphoreType.DMA((2,)),
            pltpu.SemaphoreType.DMA((2, replicas // 2)),
            pltpu.SemaphoreType.DMA((2, replicas // 2)),
            pltpu.SemaphoreType.DMA((5,)),
            pltpu.SemaphoreType.DMA,
        ],
        compiler_params=params(collective_id=collective_id, has_side_effects=True),
        cost_estimate=pl.CostEstimate(
            flops=6 * rows * width * width, bytes_accessed=1 << 26, transcendentals=0
        ),
        name="backward_turn",
    )(given, dy, middle, gain, normed_full, gate_grad, up_grad, active, dy_full)


STREAM_OFFSET = 4
STREAM_HOP = 2


def last_turn_kernel(
    count, pieces, replicas, branch_ref, out_ref, mixed_ref, q_ref, k_ref, v_ref, lse_ref, cos_ref,
    sin_ref, start_ref, packed_ref, normed_in, middle_grad_in, x_in, gain_ref, gain_two_ref,
    grad_ref, out_grad_ref, query_grad_ref, key_grad_ref, value_grad_ref, gain_one_out, gain_two_out,
    dqkv_ref, dmix_ref, bias_ref, dq_ref, dk_ref, dv_ref, w_ref, sems,
    normed_ref, middle_grad_ref, x_ref, operands, partial, landing,
    out_sums, out_traded, out_arrived, out_pair, out_sends, out_receives,
    sums, traded, arrived, pair_sems, sends, receives,
    gain_own, gain_row, gain_land, gains_ref, gain_line,
    rs_send, rs_receive, dp_send, dp_receive, line_send, line_receive,
):
    line = Line(count)
    chunk_rows = x_ref.shape[0]
    q_width = q_ref.shape[1]
    slabs = q_width // SLAB
    kv_heads = k_ref.shape[0]
    members = slabs // kv_heads
    scale = HEAD_SIZE ** (-0.5)
    fetches = weight_fetches(packed_ref, w_ref, sems)
    for at, (source, target) in enumerate(
        ((middle_grad_in, middle_grad_ref), (x_in, x_ref), (normed_in, normed_ref))
    ):
        fetches.append(pltpu.make_async_copy(source, target, operands.at[at]))
    for fetch in fetches:
        fetch.start()
    replica = lax.axis_index("dp")
    semaphore = pltpu.get_barrier_semaphore()
    for step in range(1, replicas):
        pl.semaphore_signal(semaphore, 1, device_id={"dp": (replica + step) % replicas})
    for step in range(1, count):
        pl.semaphore_signal(semaphore, 1, device_id={"tensor": (line.place + step) % count})
    out_fold = Fold(replicas, out_sums, out_traded, out_arrived, out_pair, out_sends, out_receives)
    fold = Fold(replicas, sums, traded, arrived, pair_sems, sends, receives)
    stream = Stream(
        line, partial, landing, rs_send, rs_receive, chunk_rows, pieces, STREAM_OFFSET, STREAM_HOP
    )
    size = chunk_rows // pieces
    gain_own[...] = jnp.zeros_like(gain_own)
    dk_ref[...] = jnp.zeros_like(dk_ref)
    dv_ref[...] = jnp.zeros_like(dv_ref)

    def settle(piece):
        local = pl.ds(pl.multiple_of(piece * size, size), size)
        total = stream.total(piece)
        grad, gain_grad = norm_back(total, x_ref[local, :].astype(F32), gain_ref[...])
        gain_own[...] += gain_grad
        grad_ref[local, :] = (grad + middle_grad_ref[local, :]).astype(BF16)

    def exchange(turn):
        stream.turn(turn)
        stream.settle(turn, settle)

    left = lanes((SPAN, SLAB)) < HEAD_SIZE

    def attend_tile(tile, done):
        first, span = tile * SPAN, (tile + 1) * SPAN
        rows = slice(first, first + SPAN)
        dmix_ref[...] = project_back(branch_ref[rows, :], out_ref[...]).astype(BF16)
        key_ids = lax.broadcasted_iota(jnp.int32, (span, SPAN), 0)
        row_ids = first + lanes((span, SPAN))
        allowed = (key_ids >= start_ref[:, rows]) & (key_ids <= row_ids)
        bias_ref[:span, :] = jnp.where(allowed, 0.0, mask_fill)

        @pl.loop(0, slabs)
        def _(slab):
            at = pl.ds(pl.multiple_of(slab * SLAB, SLAB), SLAB)
            head = slab // members
            queries = head_pair(q_ref[rows, at])
            grads = head_pair(dmix_ref[:, at])
            keys = k_ref[head, :span, :]
            scores = project_back(keys, queries)
            bias = bias_ref[:span, :]
            logs = jnp.concatenate(
                [lse_ref[pl.ds(2 * slab, 1), rows], lse_ref[pl.ds(2 * slab + 1, 1), rows]], axis=1
            )
            chances = jnp.exp(scores + jnp.concatenate([bias, bias], axis=1) - logs)
            chances_grad = project_back(v_ref[head, :span, :], grads)
            shared = jnp.sum(chances * chances_grad, axis=0, keepdims=True)
            score_grad = (chances * (chances_grad - shared)).astype(BF16)
            dv_ref[head, :span, :] += project(chances.astype(BF16), grads)
            dk_ref[head, :span, :] += project(score_grad, queries)
            dq_ref[:, at] = join_pair(row_contract(score_grad, keys)) * scale
            if done is not None:
                @pl.when(slab < STREAM_OFFSET - 1)
                def _():
                    exchange(done + slab)

        cosine, sine = cos_ref[rows, :], sin_ref[rows, :]
        for slab in range(slabs):
            part = dq_ref[:, slab * SLAB : (slab + 1) * SLAB]
            part = part * cosine - turned(part) * sine
            dqkv_ref[rows, slab * SLAB : (slab + 1) * SLAB] = part.astype(BF16)
        for pair in range(kv_heads // 2):
            joined = []
            for ref in (dk_ref, dv_ref):
                both = []
                for head in (2 * pair, 2 * pair + 1):
                    full = ref[head, rows, :]
                    both.append(full + pltpu.roll(full, HEAD_SIZE, 1))
                joined.append(jnp.where(left, both[0], both[1]))
            key, value = joined
            key = key * cosine - turned(key) * sine
            at = q_width + pair * SLAB
            dqkv_ref[rows, at : at + SLAB] = key.astype(BF16)
            at = at + (kv_heads // 2) * SLAB
            dqkv_ref[rows, at : at + SLAB] = value.astype(BF16)
        if tile == tiles - 1:
            for fetch in fetches:
                fetch.wait()
            pl.semaphore_wait(semaphore, replicas - 1 + count - 1)
        partial[rows, :] = project_back(dqkv_ref[rows, :], w_ref[...]).astype(BF16)

    tiles = branch_ref.shape[0] // SPAN
    done = 0
    for tile in reversed(range(tiles)):
        attend_tile(tile, done if tile < tiles - 1 else None)
        if tile < tiles - 1:
            done += min(slabs, STREAM_OFFSET - 1)
        exchange(done)
        done += 1

    block = sums.shape[2]
    out_rows = out_sums.shape[2]

    @pl.loop(done, stream.turns)
    def _(turn):
        exchange(turn)

        @pl.when(turn == done)
        def _():
            for step in range(q_width // SLAB):
                first = step * SLAB
                product = row_contract(mixed_ref[:, first : first + SLAB], branch_ref[...])
                product = product.astype(BF16)
                for row in range(0, SLAB, out_rows):
                    owner = (first + row) // out_rows
                    out_sums[owner // 2, owner % 2] = product[row : row + out_rows]
            out_fold.pair().start()

        @pl.when(turn == done + 1)
        def _():
            @pl.loop(0, replicas // 2)
            def _(half):
                at = pl.ds(pl.multiple_of(half * 2 * block, 2 * block), 2 * block)
                product = row_contract(normed_ref[:, at], dqkv_ref[...]).astype(BF16)
                for side in range(2):
                    sums[half, side] = product[side * block : (side + 1) * block]

            fold.pair().start()

        @pl.when(turn == done + 3)
        def _():
            out_fold.spread()

        @pl.when(turn == done + 4)
        def _():
            fold.spread()

    gain_row[0:1, :] = gain_own[...]
    gain_row[1:2, :] = gain_two_ref[...]

    def share(peer, landing):
        return pltpu.make_async_remote_copy(
            src_ref=gain_row, dst_ref=gain_land.at[landing],
            send_sem=dp_send.at[peer], recv_sem=dp_receive.at[landing], device_id={"dp": peer},
        )

    def pass_line(peer, landing):
        return pltpu.make_async_remote_copy(
            src_ref=gains_ref, dst_ref=gain_line.at[landing],
            send_sem=line_send.at[peer], recv_sem=line_receive.at[landing],
            device_id={"tensor": peer},
        )

    peers = [(replica + step) % replicas for step in range(1, replicas)]
    places = [(line.place + step) % count for step in range(1, count)]
    for peer in peers:
        share(peer, replica).start()
    out_grad_ref[...] = out_fold.total()
    total = fold.total()
    at = 0
    for ref in (query_grad_ref, key_grad_ref, value_grad_ref):
        ref[...] = total[:, at : at + ref.shape[1]]
        at += ref.shape[1]
    total = gain_row[...]
    for peer in peers:
        share(peer, peer).wait_recv()
        total = total + gain_land[peer]
    gains_ref[...] = total
    for peer in places:
        pass_line(peer, line.place).start()
    stream.finish()
    out_fold.finish()
    fold.finish()
    for peer in peers:
        share(peer, replica).wait_send()
    for peer in places:
        pass_line(peer, peer).wait_recv()
        total = total + gain_line[peer]
    for peer in places:
        pass_line(peer, line.place).wait_send()
    own = gain_one_out.shape[1]
    kept = jnp.zeros((2, own), F32)
    for owner in range(replicas):
        part = total[:, owner * own : (owner + 1) * own]
        kept = kept + jnp.where(replica == owner, part, 0.0)
    gain_one_out[...] = kept[0:1]
    gain_two_out[...] = kept[1:2]


def last_turn(
    branch, w_out, mixed, queries, keys, values, lse, cosine, sine, start,
    w_qkv, normed, middle_grad, x, gain, gain_two_grad, widths, count, replicas, collective_id,
    pieces=8,
):
    chunk_rows, width = x.shape
    rows, q_width = queries.shape
    kv_heads = keys.shape[0]
    block = width // replicas
    qkv_width = sum(widths)
    out_rows = q_width // replicas
    flops = 2 * rows * width * (2 * q_width + 2 * qkv_width) + 20 * rows * rows * q_width
    return pl.pallas_call(
        functools.partial(last_turn_kernel, count, pieces, replicas),
        out_shape=(
            jax.ShapeDtypeStruct((chunk_rows, width), BF16),
            jax.ShapeDtypeStruct((out_rows, width), F32),
        )
        + tuple(jax.ShapeDtypeStruct((block, part), F32) for part in widths)
        + (jax.ShapeDtypeStruct((1, block), F32),) * 2,
        in_specs=vmem_specs(10) + [pl.BlockSpec(memory_space=pl.ANY)] * 4 + vmem_specs(2),
        out_specs=tuple(vmem_specs(7)),
        scratch_shapes=[
            pltpu.VMEM((rows, qkv_width), BF16),
            pltpu.VMEM((SPAN, q_width), BF16),
            pltpu.VMEM((rows, SPAN), F32),
            pltpu.VMEM((SPAN, q_width), F32),
            pltpu.VMEM((kv_heads, rows, SLAB), F32),
            pltpu.VMEM((kv_heads, rows, SLAB), F32),
            pltpu.VMEM((width, qkv_width), BF16),
            pltpu.SemaphoreType.DMA((replicas,)),
            pltpu.VMEM((rows, width), BF16),
            pltpu.VMEM((chunk_rows, width), F32),
            pltpu.VMEM((chunk_rows, width), BF16),
            pltpu.SemaphoreType.DMA((3,)),
            pltpu.VMEM((rows, width), BF16),
            pltpu.VMEM((landing_rows(count, chunk_rows), width), BF16),
        ]
        + fold_scratch(replicas, out_rows, width)
        + fold_scratch(replicas, block, qkv_width)
        + [
            pltpu.VMEM((1, width), F32),
            pltpu.VMEM((2, width), F32),
            pltpu.VMEM((replicas, 2, width), F32),
            pltpu.VMEM((2, width), F32),
            pltpu.VMEM((count, 2, width), F32),
        ]
        + [copy_sems(count, pieces)] * 2
        + [pltpu.SemaphoreType.DMA((replicas,))] * 2
        + [pltpu.SemaphoreType.DMA((count,))] * 2,
        compiler_params=params(collective_id=collective_id, has_side_effects=True),
        cost_estimate=pl.CostEstimate(
            flops=flops, bytes_accessed=1 << 25, transcendentals=1 << 23
        ),
        name="last_turn",
    )(
        branch, w_out, mixed, queries, keys, values, lse, cosine, sine, start,
        w_qkv, normed, middle_grad, x, gain, gain_two_grad,
    )


def shards(
    inputs, cotangent, attn_gain, w_query, w_key, w_value, w_out, mlp_gain, w_gate, w_up, w_down,
    seq_lengths, group_perm, group_starts,
):
    count = lax.axis_size("tensor")
    q_width, kv_width = w_query.shape[1], w_key.shape[1]
    qkv_width = q_width + 2 * kv_width
    own = attn_gain.shape[0]
    gains = jnp.concatenate([attn_gain, mlp_gain])[None]
    gains = jnp.pad(gains, ((0, GAIN_ROWS - 1), (0, qkv_width - 2 * own)))
    packed = jnp.concatenate([w_query, w_key, w_value], axis=1)
    packed = jnp.concatenate([packed, gains], axis=0)
    qkv_full = lax.all_gather(packed[None], "dp", axis=0, tiled=True)
    gate_full = lax.all_gather(w_gate, "dp", axis=0, tiled=True)
    up_full = lax.all_gather(w_up, "dp", axis=0, tiled=True)
    down_full = lax.all_gather(w_down, "dp", axis=0, tiled=True)
    gain_rows = qkv_full[:, own, : 2 * own].reshape(-1, 2, own).astype(F32)
    gain_rows = jnp.transpose(gain_rows, (1, 0, 2)).reshape(2, -1)
    gain_one, gain_two = gain_rows[0:1], gain_rows[1:2]

    replicas = lax.axis_size("dp")
    x_full, cosine, sine, start_column, start_row, out_full = line_gather(
        inputs, rotary_freqs()[None], w_out, seq_lengths, group_perm, group_starts,
        count, replicas, 0,
    )
    normed_full, queries, keys, values, mixed, lse, near = attend(
        x_full, qkv_full, gain_one, cosine, sine, start_column, cotangent,
        q_width, kv_width, count, 5,
    )
    middle, normed_two_full = forward_turn(mixed, out_full, inputs, gain_two, count, 1)
    grad_full, active, gate_grad, up_grad, norm_two_grad, outputs = hidden_layer(
        normed_two_full, cotangent, near, middle, gate_full, up_full, down_full, count, 4
    )
    middle_grad, branch_full, gain_two_grad, sums, down_grad, gate_weight_grad, _ = backward_turn(
        norm_two_grad, cotangent, middle, gain_two, normed_two_full, gate_grad, up_grad, active,
        grad_full, count, replicas, 2,
    )
    sides = [list(range(side, replicas, 2)) for side in range(2)]
    up_weight_grad = lax.psum_scatter(
        sums, "dp", scatter_dimension=0, axis_index_groups=sides, tiled=True
    ).astype(F32)
    input_grad, out_grad, query_grad, key_grad, value_grad, gain_one_grad, gain_two_grad = last_turn(
        branch_full, out_full, mixed, queries, keys, values, lse, cosine, sine, start_row,
        qkv_full, normed_full, middle_grad, inputs, gain_one, gain_two_grad,
        (q_width, kv_width, kv_width), count, replicas, 3,
    )
    return (
        outputs,
        input_grad,
        gain_one_grad[0],
        query_grad,
        key_grad,
        value_grad,
        out_grad,
        gain_two_grad[0],
        gate_weight_grad,
        up_weight_grad,
        down_grad,
    )


def solution(mesh):
    in_specs = (
        P(("dp", "tensor"), None),
        P(("dp", "tensor"), None),
        P("dp"),
        P("dp", "tensor"),
        P("dp", "tensor"),
        P("dp", "tensor"),
        P(("tensor", "dp"), None),
        P("dp"),
        P("dp", "tensor"),
        P("dp", "tensor"),
        P(("tensor", "dp"), None),
        P(),
        P(),
        P(),
    )
    out_specs = (
        P(("dp", "tensor"), None),
        P(("dp", "tensor"), None),
        P("dp"),
        P("dp", "tensor"),
        P("dp", "tensor"),
        P("dp", "tensor"),
        P(("tensor", "dp"), None),
        P("dp"),
        P("dp", "tensor"),
        P("dp", "tensor"),
        P(("tensor", "dp"), None),
    )
    return jax.shard_map(shards, mesh=mesh, in_specs=in_specs, out_specs=out_specs, check_vma=False)
```
